32 devices in a mesh: groups: 2 (over x), gx: 4 (over y, core), gy: 4 (over z).
Axes of the slice: x: 2, y: 2, z: 4, core: 2. Of those that a mesh axis runs over, the one named last changes fastest.
Arguments:
- rhs: float32 [64, 256, 512], P('groups', 'gx', 'gy'), parts along dimension 0, may hold values from -6 to 6
- kappa: float32 [64, 256, 512], P('groups', 'gx', 'gy'), parts along dimension 0, may hold values from 0.125 to 8
Outputs:
- solution: float32 [64, 256, 512], P('groups', 'gx', 'gy'), parts along dimension 0
The draws below stay inside these ranges and needn't reach their ends.
There are 2 independent parts, one for each index of `groups`. The reference program is written for one: setup_inputs(seed, part) draws one part's arguments, and reference() takes and returns one part's arrays. A program takes and returns all parts, laid end to end along the dimension named above; each array names one. Nothing has to cross between parts.
All inputs are finite; a program needn't handle non-finite values.
Results may differ from the reference program's by a relative error of at most 0.00002.
Values sent between devices are 32-bit elements; how exact they have to be, the bound alone decides.
No kernel may reach another device: no remote copies, remote signals or barrier semaphores. Data moves between devices by JAX's collectives and lax.ppermute only.
A program may use at most 128 MiB of HBM per device.

```python
import jax
import jax.numpy as jnp

NZ = 32
NX = 256
NY = 512


def factor_field(key, shape):
    unit = jax.random.uniform(key, shape, jnp.float32)
    return jnp.exp(jnp.log(0.5) + unit * (jnp.log(2.0) - jnp.log(0.5)))


def draw_kappa(key, part):
    key_cell = jax.random.fold_in(key, 11)
    key_mid = jax.random.fold_in(key, 23)
    key_low = jax.random.fold_in(key, 37)
    cell = factor_field(key_cell, (NZ, NX, NY))
    middle = factor_field(key_mid, (NZ, NX // 4, NY // 4))
    middle = jnp.repeat(jnp.repeat(middle, 4, axis=1), 4, axis=2)
    lowest = factor_field(key_low, (NZ, NX // 16, NY // 16))
    lowest = jnp.repeat(jnp.repeat(lowest, 16, axis=1), 16, axis=2)
    return (cell * middle * lowest).astype(jnp.float32)


def shard_levels(key, dims, cuts, smallest, high):
    def one(dim, shards_of):
        heights = jax.random.uniform(jax.random.fold_in(jax.random.fold_in(key, 6), dim), (shards_of,), jnp.float32, smallest / len(cuts), high / len(cuts))
        return jnp.repeat(jnp.exp(heights), dims[dim] // shards_of).reshape((-1,) + (1,) * (len(dims) - dim - 1))

    loudness = one(*cuts[0])
    for cut in cuts[1:]:
        loudness = loudness * one(*cut)
    return loudness


def bell_draw(own_key, dims, deviation, limit, split=(), kind=jnp.bfloat16):
    level = shard_levels(own_key, dims, split, -0.22, 0.18) if split else 1.0
    array = jax.random.normal(own_key, dims, jnp.float32) * deviation * level
    return jnp.minimum(jnp.maximum(array, -limit), limit).astype(kind)


def setup_inputs(seed: int = 0, part: int = 0) -> dict:
    streams_of = jax.random.split(jax.random.key(seed), 3)
    part_keys = jax.random.split(jax.random.fold_in(streams_of[2], part), 3)
    return {
        "rhs": bell_draw(part_keys[0], (NZ, NX, NY), 1.0, 6.0, ((1, 4), (2, 4)), jnp.float32),
        "kappa": draw_kappa(jax.random.fold_in(jax.random.fold_in(streams_of[2], part), 71), part),
    }


JACOBI_WEIGHT = 0.8
STEP_WEIGHT = 0.6


def harmonic(first, second):
    return 2.0 * first * second / (first + second)


def face_terms(diffusivity, scale_flat, scale_up):
    along_x = scale_flat * harmonic(diffusivity[:, :-1, :], diffusivity[:, 1:, :])
    along_y = scale_flat * harmonic(diffusivity[:, :, :-1], diffusivity[:, :, 1:])
    along_z = scale_up * harmonic(diffusivity[:-1], diffusivity[1:])
    return along_x, along_y, along_z


def pair_sum(coeff, axis):
    widths = [(0, 0), (0, 0), (0, 0)]
    widths[axis] = (1, 1)
    padded = jnp.pad(coeff, widths)
    count = padded.shape[axis]
    lower = jnp.take(padded, jnp.arange(0, count - 1), axis=axis)
    upper = jnp.take(padded, jnp.arange(1, count), axis=axis)
    return lower, upper


def inner_diag(face_set):
    low_x, high_x = pair_sum(face_set[0], 1)
    low_y, high_y = pair_sum(face_set[1], 2)
    low_z, high_z = pair_sum(face_set[2], 0)
    return (low_x + high_x) + (low_y + high_y) + (low_z + high_z)


def apply_operator(field, face_set):
    flux_x = face_set[0] * (field[:, 1:, :] - field[:, :-1, :])
    flux_y = face_set[1] * (field[:, :, 1:] - field[:, :, :-1])
    flux_z = face_set[2] * (field[1:] - field[:-1])
    low_x, high_x = pair_sum(flux_x, 1)
    low_y, high_y = pair_sum(flux_y, 2)
    low_z, high_z = pair_sum(flux_z, 0)
    return (low_x - high_x) + (low_y - high_y) + (low_z - high_z)


def level_setup(diffusivity, scale_flat, scale_up):
    face_set = face_terms(diffusivity, scale_flat, scale_up)
    return face_set, 1.0 / inner_diag(face_set)


def smooth(resid, setup):
    face_set, inverse = setup
    field = JACOBI_WEIGHT * resid * inverse
    for sweep_count in range(3):
        image = apply_operator(field, face_set)
        field = field + JACOBI_WEIGHT * (resid - image) * inverse
    return field


def block_mean(field):
    depth, rows, cols = field.shape
    return field.reshape(depth, rows // 4, 4, cols // 4, 4).mean(axis=(2, 4))


def restrict_sum(field):
    depth, rows, cols = field.shape
    return field.reshape(depth, rows // 4, 4, cols // 4, 4).sum(axis=(2, 4))


def prolong(field):
    return jnp.repeat(jnp.repeat(field, 4, axis=1), 4, axis=2)


def reference(rhs, kappa):
    kappa_mid = block_mean(kappa)
    kappa_low = block_mean(kappa_mid)
    fine_setup = level_setup(kappa, 1.0, 1.0)
    middle_setup = level_setup(kappa_mid, 4.0, 16.0)
    coarse_setup = level_setup(kappa_low, 16.0, 256.0)

    def precondition(resid):
        fine_part = smooth(resid, fine_setup)
        resid_mid = restrict_sum(resid)
        middle_part = smooth(resid_mid, middle_setup)
        coarse_part = smooth(restrict_sum(resid_mid), coarse_setup)
        middle_part = middle_part + prolong(coarse_part)
        return fine_part + prolong(middle_part)

    first = STEP_WEIGHT * precondition(rhs)
    defect = rhs - apply_operator(first, fine_setup[0])
    return first + STEP_WEIGHT * precondition(defect)
```

```python
import functools

import jax
import jax.numpy as jnp
from jax import lax
from jax.experimental import pallas as pl
from jax.experimental.pallas import tpu as pltpu
from jax.sharding import PartitionSpec as P

JACOBI_WEIGHT = 0.8
STEP_WEIGHT = 0.6
LANES = 128
DEPTH = 32
QUARTERS = 4


class Level:
    def __init__(self, rows, width, flat, up):
        self.n = rows
        self.own = width
        self.span = width + 16
        self.flat = flat
        self.up = up
        self.rows = rows + 8
        self.ghost = rows + 3
        self.chunk = 48 if self.span % 48 == 0 else self.span


def params(mib=56):
    return pltpu.CompilerParams(vmem_limit_bytes=mib << 20)


def quarter(shape):
    return lax.broadcasted_iota(jnp.int32, shape, 1) // DEPTH


def move(value, source, target):
    shift = DEPTH * ((target - source) % QUARTERS)
    return pltpu.roll(value, shift, 1) if shift else value


def join_slots(pieces):
    out = None
    for slot, (value, source) in enumerate(pieces):
        part = move(value, source, slot)
        out = part if out is None else jnp.where(quarter(part.shape) == slot, part, out)
    return out


def ghost_of(from_left, from_right, slot):
    group = quarter(from_left.shape)
    left = move(from_left, slot, 0)
    right = move(from_right, slot, 3)
    return jnp.where(group == 0, left, jnp.where(group == 3, right, 0.0))


def mid_piece(ref, j, low):
    index = j if low else 15 - j
    return ref[index % 4], index // 4


def sum_rows_mid(rows_ref, tmp, out_ref, width, base):
    for m in range(4):
        total = rows_ref[4 * m, base : base + width] + rows_ref[4 * m + 1, base : base + width]
        total = total + rows_ref[4 * m + 2, base : base + width]
        tmp[0:width, :] = total + rows_ref[4 * m + 3, base : base + width]
        out = tmp[pl.ds(0, width // 4, stride=4), :]
        for t in range(1, 4):
            out = out + tmp[pl.ds(t, width // 4, stride=4), :]
        out_ref[m] = out


def sum_rows_low(mid_ref, tmp):
    tmp[0:32, :] = mid_ref[0] + mid_ref[1] + mid_ref[2] + mid_ref[3]
    out = tmp[pl.ds(0, 8, stride=4), :]
    for t in range(1, 4):
        out = out + tmp[pl.ds(t, 8, stride=4), :]
    return out


def first_kernel(rhs, kappa, kz, rz, km, rm, kl, rl, low, high, tmp):
    for x in range(16):
        for source, target in ((kappa, kz), (rhs, rz)):
            rows = [source[pl.ds(16 * q + x, DEPTH, stride=64), :] for q in range(4)]
            target[x] = jnp.concatenate(rows, axis=0).T
    sum_rows_mid(kz, tmp, km, 128, 0)
    for m in range(4):
        km[m] = km[m] * (1.0 / 16.0)
    sum_rows_mid(rz, tmp, rm, 128, 0)
    kl[...] = sum_rows_low(km, tmp) * (1.0 / 16.0)
    rl[...] = sum_rows_low(rm, tmp)
    for out, is_low in ((low, True), (high, False)):
        edge = 0 if is_low else 3
        fine = [(kz[j if is_low else 15 - j], edge) for j in range(5)]
        fine += [(rz[j if is_low else 15 - j], edge) for j in range(4)]
        out[0] = join_slots(fine[0:4])
        out[1] = join_slots(fine[4:8])
        out[2] = join_slots(fine[8:9])
        group = quarter((32, LANES))
        for j in range(4):
            value, source = mid_piece(rm, j, is_low)
            rows = slice(32 * j, 32 * j + 32)
            out[2, rows] = jnp.where(group == 1, move(value, source, 1), out[2, rows])
            value, source = mid_piece(km, j, is_low)
            out[2, rows] = jnp.where(group == 2, move(value, source, 2), out[2, rows])
        value, source = mid_piece(km, 4, is_low)
        out[2, 0:32] = jnp.where(group == 3, move(value, source, 3), out[2, 0:32])
        group = quarter((8, LANES))
        for j in range(4):
            source = j if is_low else 3 - j
            for ref, base in ((kl, 32), (rl, 64)):
                rows = slice(base + 8 * j, base + 8 * j + 8)
                out[2, rows] = jnp.where(group == 3, move(ref[...], source, 3), out[2, rows])


def second_kernel(
    left, right, far_left, far_right, kz, rz, km, rm, kl, rl,
    gk, gr, gkm, grm, gkl, grl, low, high,
):
    for j in range(5):
        gk[j] = ghost_of(left[j // 4], right[j // 4], j % 4)
    for j in range(4):
        slot = j + 5
        gr[j] = ghost_of(left[slot // 4], right[slot // 4], slot % 4)
        rows = slice(32 * j, 32 * j + 32)
        grm[j] = ghost_of(left[2, rows], right[2, rows], 1)
        gkm[j] = ghost_of(left[2, rows], right[2, rows], 2)
        rows = slice(32 + 8 * j, 40 + 8 * j)
        gkl[j] = ghost_of(left[2, rows], right[2, rows], 3)
        rows = slice(64 + 8 * j, 72 + 8 * j)
        grl[j] = ghost_of(left[2, rows], right[2, rows], 3)
    gkm[4] = ghost_of(left[2, 0:32], right[2, 0:32], 3)
    group = quarter((8, LANES))
    gkl[4] = jnp.where(
        group == 0,
        move(far_left[...], 3, 0),
        jnp.where(group == 3, move(far_right[...], 0, 3), 0.0),
    )
    at = 0
    for own, ghost, n, g, width in (
        (kz, gk, 16, 5, 128), (rz, gr, 16, 4, 128),
        (km, gkm, 4, 5, 32), (rm, grm, 4, 4, 32),
        (kl, gkl, 0, 5, 8), (rl, grl, 0, 4, 8),
    ):
        if n == 0:
            low[at] = own[...]
            high[at] = own[...]
            at += 1
        for i in range(n):
            low[at] = own[i, 0:8]
            high[at] = own[i, width - 8 : width]
            at += 1
        for i in range(g):
            low[at] = ghost[i, 0:8]
            high[at] = ghost[i, width - 8 : width]
            at += 1


def fixup(ref, lev, base):
    rows = slice(base, base + lev.span)
    group = quarter((lev.span, LANES))
    ghost = ref[lev.ghost, rows]
    first = ref[1, rows]
    last = ref[lev.n, rows]
    ref[0, rows] = jnp.where(group == 0, ghost, pltpu.roll(last, DEPTH, 1))
    ref[lev.n + 1, rows] = jnp.where(group == 3, ghost, pltpu.roll(first, LANES - DEPTH, 1))
    ref[lev.n + 2, rows] = jnp.where(group == 0, first, last)


def each(lev, ghosts, body):
    def own(i, carry):
        for c in range(0, lev.span, lev.chunk):
            body(i, c, lev.chunk)
        return carry

    if lev.n > 1:
        lax.fori_loop(1, lev.n + 1, own, 0)
    else:
        own(1, 0)
    if ghosts:
        lax.fori_loop(lev.ghost, lev.ghost + ghosts, own, 0)


def fill(dst, base, lev, own, ghost, count, ylo, yhi, at):
    mine = slice(base + 8, base + 8 + lev.own)
    if lev.n == 1:
        dst[1, mine] = own[...]
    else:
        for i in range(lev.n):
            dst[1 + i, mine] = own[i]
    for j in range(count):
        dst[lev.ghost + j, mine] = ghost[j]
    for i in range(lev.n + count):
        row = 1 + i if i < lev.n else lev.ghost + i - lev.n
        dst[row, base : base + 8] = ylo[at + i]
        dst[row, base + 8 + lev.own : base + 16 + lev.own] = yhi[at + i]
    return at + lev.n + count


def setup(lev, k, pad, w, cx, cu, cd, cz):
    def harmonic(a, b):
        total = a + b
        return 2.0 * a * b / jnp.where(total > 0, total, 1.0)

    zeros = jnp.zeros((8, LANES), jnp.float32)
    for i in range(lev.rows):
        k[i, 0:8] = zeros
        k[i, lev.span + 8 : lev.span + 16] = zeros
    fixup(k, lev, 8)

    def along_x(i, carry):
        for c in range(0, lev.span, lev.chunk):
            rows = pl.ds(8 + c, lev.chunk)
            cx[i, pl.ds(c, lev.chunk)] = lev.flat * harmonic(k[i, rows], k[i + 1, rows])
        return carry

    lax.fori_loop(0, lev.rows - 1, along_x, 0)

    def rest(i, c, size):
        here = k[i, pl.ds(8 + c, size)]
        above = lev.flat * harmonic(here, k[i, pl.ds(9 + c, size)])
        below = lev.flat * harmonic(k[i, pl.ds(7 + c, size)], here)
        z = lax.broadcasted_iota(jnp.int32, (size, LANES), 1) % DEPTH
        up = lev.up * harmonic(here, pltpu.roll(here, LANES - 1, 1))
        up = jnp.where(z == DEPTH - 1, 0.0, up)
        rows = pl.ds(c, size)
        cu[i, rows] = above
        cd[i, rows] = below
        cz[i, rows] = up
        diagonal = cx[i - 1, rows] + cx[i, rows] + (below + above) + (pltpu.roll(up, 1, 1) + up)
        good = diagonal > 0
        w[i, rows] = jnp.where(good, JACOBI_WEIGHT / jnp.where(good, diagonal, 1.0), 0.0)

    each(lev, 4, rest)


def clear_pads(ref, lev):
    zeros = jnp.zeros((8, LANES), jnp.float32)
    for i in range(lev.rows):
        ref[i, 0:8] = zeros
        ref[i, lev.span + 8 : lev.span + 16] = zeros


def smooth(lev, r, va, vb, w, cx, cu, cd, cz, reach):
    def start(i, c, size):
        rows = pl.ds(c, size)
        va[i, pl.ds(8 + c, size)] = w[i, rows] * r[i, rows]

    each(lev, reach, start)
    src, dst = va, vb
    for sweep in range(3):
        fixup(src, lev, 8)

        def step(i, c, size, src=src, dst=dst):
            rows = pl.ds(c, size)
            wide = pl.ds(8 + c, size)
            v = src[i, wide]
            up = cz[i, rows]
            acc = r[i, rows] + cx[i - 1, rows] * src[i - 1, wide] + cx[i, rows] * src[i + 1, wide]
            acc = acc + cu[i, rows] * src[i, pl.ds(9 + c, size)]
            acc = acc + cd[i, rows] * src[i, pl.ds(7 + c, size)]
            acc = acc + up * pltpu.roll(v, LANES - 1, 1) + pltpu.roll(up * v, 1, 1)
            dst[i, wide] = (1.0 - JACOBI_WEIGHT) * v + w[i, rows] * acc

        each(lev, reach - 1 - sweep, step)
        src, dst = dst, src
    return src


def expand(values, tmp, lev):
    part = values[14 : 14 + lev.span // 4]
    for t in range(4):
        tmp[pl.ds(t, lev.span // 4, stride=4), :] = part


def combine(vf, vm, vl, levels, tmp, ghosts):
    fine, mid, low = levels
    for row_low, rows_mid in ((1, range(1, 5)), (low.ghost, range(mid.ghost, mid.ghost + ghosts))):
        if not len(rows_mid):
            continue
        expand(vl[row_low], tmp, mid)
        for row in rows_mid:
            vm[row, 8 : 8 + mid.span] = vm[row, 8 : 8 + mid.span] + tmp[0 : mid.span]
    for m in range(4 + ghosts):
        expand(vm[1 + m if m < 4 else mid.ghost], tmp, fine)
        rows = range(1 + 4 * m, 5 + 4 * m) if m < 4 else range(fine.ghost, fine.ghost + 1)
        for row in rows:
            here = slice(8, 8 + fine.span)
            vf[row, here] = STEP_WEIGHT * (vf[row, here] + tmp[0 : fine.span])


def third_kernel(
    levels, kz, rz, km, rm, kl, rl, gk, gr, gkm, grm, gkl, grl, ylo, yhi,
    wf, xf, uf, df, zf, wm, xm, um, dm, zm, wl, xl, ul, dl, zl,
    first, defect, dmid, dlow, low, high,
    kf_s, rf_s, vf_s, km_s, rm_s, vm_s, kl_s, rl_s, vl_s, tmp,
):
    fine, mid, coarse = levels
    at = 0
    for lev, own_k, ghost_k, ks, own_r, ghost_r, rs in (
        (fine, kz, gk, kf_s, rz, gr, rf_s),
        (mid, km, gkm, km_s, rm, grm, rm_s),
        (coarse, kl, gkl, kl_s, rl, grl, rl_s),
    ):
        at = fill(ks, 8, lev, own_k, ghost_k, 5, ylo, yhi, at)
        at = fill(rs, 0, lev, own_r, ghost_r, 4, ylo, yhi, at)
    done = []
    for lev, k, r, v, coef in (
        (fine, kf_s, rf_s, vf_s, (wf, xf, uf, df, zf)),
        (mid, km_s, rm_s, vm_s, (wm, xm, um, dm, zm)),
        (coarse, kl_s, rl_s, vl_s, (wl, xl, ul, dl, zl)),
    ):
        setup(lev, k, None, *coef)
        clear_pads(v, lev)
        done.append(smooth(lev, r, v, k, *coef, 4))
    vf, vm, vl = done
    combine(vf, vm, vl, levels, tmp, 1)
    fixup(vf, fine, 8)

    def apply(i, carry):
        for c in range(8, 136, 64):
            rows = pl.ds(c, 64)
            wide = pl.ds(8 + c, 64)
            v = vf[i, wide]
            flux = zf[i, rows] * (v - pltpu.roll(v, LANES - 1, 1))
            image = xf[i - 1, rows] * (v - vf[i - 1, wide]) + xf[i, rows] * (v - vf[i + 1, wide])
            image = image + uf[i, rows] * (v - vf[i, pl.ds(9 + c, 64)])
            image = image + df[i, rows] * (v - vf[i, pl.ds(7 + c, 64)])
            image = image + (flux - pltpu.roll(flux, 1, 1))
            defect[i - 1, pl.ds(c - 8, 64)] = rf_s[i, rows] - image
            first[i - 1, pl.ds(c - 8, 64)] = v
        return carry

    lax.fori_loop(1, 17, apply, 0)
    sum_rows_mid(defect, tmp, dmid, 128, 0)
    dlow[...] = sum_rows_low(dmid, tmp)
    for out, is_low in ((low, True), (high, False)):
        edge = 0 if is_low else 3
        out[...] = join_slots([(defect[j if is_low else 15 - j], edge) for j in range(3)])
        for j in range(3):
            value, source = mid_piece(dmid, j, is_low)
            rows = slice(32 * j, 32 * j + 32)
            out[rows] = jnp.where(quarter((32, LANES)) == 3, move(value, source, 3), out[rows])
            source = j if is_low else 3 - j
            rows = slice(96 + 8 * j, 104 + 8 * j)
            out[rows] = jnp.where(quarter((8, LANES)) == 3, move(dlow[...], source, 3), out[rows])


def fourth_kernel(left, right, defect, dmid, dlow, gf, gm, gl, low, high):
    for j in range(3):
        gf[j] = ghost_of(left[...], right[...], j)
        rows = slice(32 * j, 32 * j + 32)
        gm[j] = ghost_of(left[rows], right[rows], 3)
        rows = slice(96 + 8 * j, 104 + 8 * j)
        gl[j] = ghost_of(left[rows], right[rows], 3)
    at = 0
    for own, ghost, n, width in ((defect, gf, 16, 128), (dmid, gm, 4, 32), (dlow, gl, 0, 8)):
        if n == 0:
            low[at] = own[...]
            high[at] = own[...]
            at += 1
        for i in range(n):
            low[at] = own[i, 0:8]
            high[at] = own[i, width - 8 : width]
            at += 1
        for i in range(3):
            low[at] = ghost[i, 0:8]
            high[at] = ghost[i, width - 8 : width]
            at += 1


def fifth_kernel(
    levels, wf, xf, uf, df, zf, wm, xm, um, dm, zm, wl, xl, ul, dl, zl,
    first, defect, dmid, dlow, gf, gm, gl, ylo, yhi, out,
    rf_s, va_f, vb_f, rm_s, va_m, vb_m, rl_s, va_l, vb_l, tmp,
):
    fine, mid, coarse = levels
    at = 0
    done = []
    for lev, own, ghost, r, va, vb, coef in (
        (fine, defect, gf, rf_s, va_f, vb_f, (wf, xf, uf, df, zf)),
        (mid, dmid, gm, rm_s, va_m, vb_m, (wm, xm, um, dm, zm)),
        (coarse, dlow, gl, rl_s, va_l, vb_l, (wl, xl, ul, dl, zl)),
    ):
        at = fill(r, 0, lev, own, ghost, 3, ylo, yhi, at)
        clear_pads(va, lev)
        clear_pads(vb, lev)
        done.append(smooth(lev, r, va, vb, *coef, 3))
    vf, vm, vl = done
    combine(vf, vm, vl, levels, tmp, 0)
    for x in range(16):
        total = (first[x] + vf[1 + x, 16:144]).T
        for q in range(4):
            out[pl.ds(16 * q + x, DEPTH, stride=64), :] = total[DEPTH * q : DEPTH * q + DEPTH]


def shape(*dims):
    return jax.ShapeDtypeStruct(dims, jnp.float32)


def scratch(*dims):
    return pltpu.VMEM(dims, jnp.float32)


def neighbour(value, axis, hop, back):
    count = lax.axis_size(axis)
    pairs = [(i, i + hop) for i in range(count - hop)]
    if back:
        pairs = [(b, a) for a, b in pairs]
    if not pairs:
        return jnp.zeros_like(value)
    return lax.ppermute(value, axis, pairs)


def on_device(rhs, kappa):
    levels = (
        Level(16, 128, 1.0, 1.0),
        Level(4, 32, 4.0, 16.0),
        Level(1, 8, 16.0, 256.0),
    )
    fine, mid, coarse = levels
    own = [shape(16, 128, LANES), shape(4, 32, LANES), shape(8, LANES)]
    kz, rz, km, rm, kl, rl, low, high = pl.pallas_call(
        first_kernel,
        out_shape=[own[0], own[0], own[1], own[1], own[2], own[2]] + [shape(3, 128, LANES)] * 2,
        scratch_shapes=[scratch(144, LANES)],
        compiler_params=params(),
    )(rhs.reshape(2048, LANES), kappa.reshape(2048, LANES))
    left = neighbour(high, "gx", 1, False)
    right = neighbour(low, "gx", 1, True)
    far_left = neighbour(kl, "gx", 2, False)
    far_right = neighbour(kl, "gx", 2, True)
    gk, gr, gkm, grm, gkl, grl, low, high = pl.pallas_call(
        second_kernel,
        out_shape=[
            shape(5, 128, LANES), shape(4, 128, LANES),
            shape(5, 32, LANES), shape(4, 32, LANES),
            shape(5, 8, LANES), shape(4, 8, LANES),
            shape(69, 8, LANES), shape(69, 8, LANES),
        ],
        compiler_params=params(),
    )(left, right, far_left, far_right, kz, rz, km, rm, kl, rl)
    ylo = neighbour(high, "gy", 1, False)
    yhi = neighbour(low, "gy", 1, True)
    state = []
    for lev in levels:
        state += [shape(lev.rows, lev.span, LANES)] * 5
    bufs = []
    for lev in levels:
        bufs += [
            scratch(lev.rows, lev.span + 16, LANES),
            scratch(lev.rows, lev.span, LANES),
            scratch(lev.rows, lev.span + 16, LANES),
        ]
    results = pl.pallas_call(
        functools.partial(third_kernel, levels),
        out_shape=state + [own[0], own[0], own[1], own[2]] + [shape(128, LANES)] * 2,
        scratch_shapes=bufs + [scratch(144, LANES)],
        compiler_params=params(),
    )(kz, rz, km, rm, kl, rl, gk, gr, gkm, grm, gkl, grl, ylo, yhi)
    state = results[:15]
    first, defect, dmid, dlow, low, high = results[15:]
    left = neighbour(high, "gx", 1, False)
    right = neighbour(low, "gx", 1, True)
    gf, gm, gl, low, high = pl.pallas_call(
        fourth_kernel,
        out_shape=[
            shape(3, 128, LANES), shape(3, 32, LANES), shape(3, 8, LANES),
            shape(30, 8, LANES), shape(30, 8, LANES),
        ],
        compiler_params=params(),
    )(left, right, defect, dmid, dlow)
    ylo = neighbour(high, "gy", 1, False)
    yhi = neighbour(low, "gy", 1, True)
    bufs = []
    for lev in levels:
        bufs += [
            scratch(lev.rows, lev.span, LANES),
            scratch(lev.rows, lev.span + 16, LANES),
            scratch(lev.rows, lev.span + 16, LANES),
        ]
    out = pl.pallas_call(
        functools.partial(fifth_kernel, levels),
        out_shape=shape(2048, LANES),
        scratch_shapes=bufs + [scratch(144, LANES)],
        compiler_params=params(),
    )(*state, first, defect, dmid, dlow, gf, gm, gl, ylo, yhi)
    return out.reshape(rhs.shape)


def solution(mesh):
    return jax.shard_map(
        on_device,
        mesh=mesh,
        in_specs=(P("groups", "gx", "gy"), P("groups", "gx", "gy")),
        out_specs=P("groups", "gx", "gy"),
        check_vma=False,
    )
```

```python
import functools

import jax
import jax.numpy as jnp
from jax import lax
from jax.experimental import pallas as pl
from jax.experimental.pallas import tpu as pltpu
from jax.sharding import PartitionSpec as P

JACOBI_WEIGHT = 0.8
STEP_WEIGHT = 0.6
LANES = 128
DEPTH = 32
QUARTERS = 4


class Level:
    def __init__(self, rows, width, flat, up):
        self.n = rows
        self.own = width
        self.span = width + 16
        self.flat = flat
        self.up = up
        self.rows = rows + 8
        self.ghost = rows + 3
        self.chunk = 48 if self.span % 48 == 0 else self.span


def params(mib=24):
    return pltpu.CompilerParams(vmem_limit_bytes=mib << 20)


def quarter(shape):
    return lax.broadcasted_iota(jnp.int32, shape, 1) // DEPTH


def move(value, source, target):
    shift = DEPTH * ((target - source) % QUARTERS)
    return pltpu.roll(value, shift, 1) if shift else value


def join_slots(pieces):
    out = None
    for slot, (value, source) in enumerate(pieces):
        part = move(value, source, slot)
        out = part if out is None else jnp.where(quarter(part.shape) == slot, part, out)
    return out


def ghost_of(from_left, from_right, slot):
    group = quarter(from_left.shape)
    left = move(from_left, slot, 0)
    right = move(from_right, slot, 3)
    return jnp.where(group == 0, left, jnp.where(group == 3, right, 0.0))


def mid_piece(ref, j, low):
    index = j if low else 15 - j
    return ref[index % 4], index // 4


def sum_rows_mid(rows_ref, tmp, out_ref, width, base):
    for m in range(4):
        total = rows_ref[4 * m, base : base + width] + rows_ref[4 * m + 1, base : base + width]
        total = total + rows_ref[4 * m + 2, base : base + width]
        tmp[0:width, :] = total + rows_ref[4 * m + 3, base : base + width]
        out = tmp[pl.ds(0, width // 4, stride=4), :]
        for t in range(1, 4):
            out = out + tmp[pl.ds(t, width // 4, stride=4), :]
        out_ref[m] = out


def sum_rows_low(mid_ref, tmp):
    tmp[0:32, :] = mid_ref[0] + mid_ref[1] + mid_ref[2] + mid_ref[3]
    out = tmp[pl.ds(0, 8, stride=4), :]
    for t in range(1, 4):
        out = out + tmp[pl.ds(t, 8, stride=4), :]
    return out


def first_kernel(rhs, kappa, kz, rz, km, rm, kl, rl, low, high, tmp):
    for x in range(16):
        for source, target in ((kappa, kz), (rhs, rz)):
            rows = [source[pl.ds(16 * q + x, DEPTH, stride=64), :] for q in range(4)]
            target[x] = jnp.concatenate(rows, axis=0).T
    sum_rows_mid(kz, tmp, km, 128, 0)
    for m in range(4):
        km[m] = km[m] * (1.0 / 16.0)
    sum_rows_mid(rz, tmp, rm, 128, 0)
    kl[...] = sum_rows_low(km, tmp) * (1.0 / 16.0)
    rl[...] = sum_rows_low(rm, tmp)
    for out, is_low in ((low, True), (high, False)):
        edge = 0 if is_low else 3
        fine = [(kz[j if is_low else 15 - j], edge) for j in range(5)]
        fine += [(rz[j if is_low else 15 - j], edge) for j in range(4)]
        out[0] = join_slots(fine[0:4])
        out[1] = join_slots(fine[4:8])
        out[2] = join_slots(fine[8:9])
        group = quarter((32, LANES))
        for j in range(4):
            value, source = mid_piece(rm, j, is_low)
            rows = slice(32 * j, 32 * j + 32)
            out[2, rows] = jnp.where(group == 1, move(value, source, 1), out[2, rows])
            value, source = mid_piece(km, j, is_low)
            out[2, rows] = jnp.where(group == 2, move(value, source, 2), out[2, rows])
        value, source = mid_piece(km, 4, is_low)
        out[2, 0:32] = jnp.where(group == 3, move(value, source, 3), out[2, 0:32])
        group = quarter((8, LANES))
        for j in range(4):
            source = j if is_low else 3 - j
            for ref, base in ((kl, 32), (rl, 64)):
                rows = slice(base + 8 * j, base + 8 * j + 8)
                out[2, rows] = jnp.where(group == 3, move(ref[...], source, 3), out[2, rows])


def second_kernel(
    left, right, far_left, far_right, kz, rz, km, rm, kl, rl,
    gk, gr, gkm, grm, gkl, grl, low, high,
):
    for j in range(5):
        gk[j] = ghost_of(left[j // 4], right[j // 4], j % 4)
    for j in range(4):
        slot = j + 5
        gr[j] = ghost_of(left[slot // 4], right[slot // 4], slot % 4)
        rows = slice(32 * j, 32 * j + 32)
        grm[j] = ghost_of(left[2, rows], right[2, rows], 1)
        gkm[j] = ghost_of(left[2, rows], right[2, rows], 2)
        rows = slice(32 + 8 * j, 40 + 8 * j)
        gkl[j] = ghost_of(left[2, rows], right[2, rows], 3)
        rows = slice(64 + 8 * j, 72 + 8 * j)
        grl[j] = ghost_of(left[2, rows], right[2, rows], 3)
    gkm[4] = ghost_of(left[2, 0:32], right[2, 0:32], 3)
    group = quarter((8, LANES))
    gkl[4] = jnp.where(
        group == 0,
        move(far_left[...], 3, 0),
        jnp.where(group == 3, move(far_right[...], 0, 3), 0.0),
    )
    at = 0
    for own, ghost, n, g, width in (
        (kz, gk, 16, 5, 128), (rz, gr, 16, 4, 128),
        (km, gkm, 4, 5, 32), (rm, grm, 4, 4, 32),
        (kl, gkl, 0, 5, 8), (rl, grl, 0, 4, 8),
    ):
        if n == 0:
            low[at] = own[...]
            high[at] = own[...]
            at += 1
        for i in range(n):
            low[at] = own[i, 0:8]
            high[at] = own[i, width - 8 : width]
            at += 1
        for i in range(g):
            low[at] = ghost[i, 0:8]
            high[at] = ghost[i, width - 8 : width]
            at += 1


def fixup(ref, lev, base):
    rows = slice(base, base + lev.span)
    group = quarter((lev.span, LANES))
    ghost = ref[lev.ghost, rows]
    first = ref[1, rows]
    last = ref[lev.n, rows]
    ref[0, rows] = jnp.where(group == 0, ghost, pltpu.roll(last, DEPTH, 1))
    ref[lev.n + 1, rows] = jnp.where(group == 3, ghost, pltpu.roll(first, LANES - DEPTH, 1))
    ref[lev.n + 2, rows] = jnp.where(group == 0, first, last)


def each(lev, ghosts, body):
    def own(i, carry):
        for c in range(0, lev.span, lev.chunk):
            body(i, c, lev.chunk)
        return carry

    for i in list(range(1, lev.n + 1)) + list(range(lev.ghost, lev.ghost + ghosts)):
        own(i, 0)


def fill(dst, base, lev, own, ghost, count, ylo, yhi, at):
    mine = slice(base + 8, base + 8 + lev.own)
    if lev.n == 1:
        dst[1, mine] = own[...]
    else:
        for i in range(lev.n):
            dst[1 + i, mine] = own[i]
    for j in range(count):
        dst[lev.ghost + j, mine] = ghost[j]
    for i in range(lev.n + count):
        row = 1 + i if i < lev.n else lev.ghost + i - lev.n
        dst[row, base : base + 8] = ylo[at + i]
        dst[row, base + 8 + lev.own : base + 16 + lev.own] = yhi[at + i]
    return at + lev.n + count


def setup(lev, k, pad, w, cx, cu, cd, cz):
    def harmonic(a, b):
        total = a + b
        return 2.0 * a * b / jnp.where(total > 0, total, 1.0)

    zeros = jnp.zeros((8, LANES), jnp.float32)
    for i in range(lev.rows):
        k[i, 0:8] = zeros
        k[i, lev.span + 8 : lev.span + 16] = zeros
    fixup(k, lev, 8)

    def along_x(i, carry):
        for c in range(0, lev.span, lev.chunk):
            rows = pl.ds(8 + c, lev.chunk)
            cx[i, pl.ds(c, lev.chunk)] = lev.flat * harmonic(k[i, rows], k[i + 1, rows])
        return carry

    for i in range(lev.rows - 1):
        along_x(i, 0)

    def rest(i, c, size):
        here = k[i, pl.ds(8 + c, size)]
        above = lev.flat * harmonic(here, k[i, pl.ds(9 + c, size)])
        below = lev.flat * harmonic(k[i, pl.ds(7 + c, size)], here)
        z = lax.broadcasted_iota(jnp.int32, (size, LANES), 1) % DEPTH
        up = lev.up * harmonic(here, pltpu.roll(here, LANES - 1, 1))
        up = jnp.where(z == DEPTH - 1, 0.0, up)
        rows = pl.ds(c, size)
        cu[i, rows] = above
        cd[i, rows] = below
        cz[i, rows] = up
        diagonal = cx[i - 1, rows] + cx[i, rows] + (below + above) + (pltpu.roll(up, 1, 1) + up)
        good = diagonal > 0
        w[i, rows] = jnp.where(good, JACOBI_WEIGHT / jnp.where(good, diagonal, 1.0), 0.0)

    each(lev, 4, rest)


def clear_pads(ref, lev):
    zeros = jnp.zeros((8, LANES), jnp.float32)
    for i in range(lev.rows):
        ref[i, 0:8] = zeros
        ref[i, lev.span + 8 : lev.span + 16] = zeros


def smooth(lev, r, va, vb, w, cx, cu, cd, cz, reach):
    def start(i, c, size):
        rows = pl.ds(c, size)
        va[i, pl.ds(8 + c, size)] = w[i, rows] * r[i, rows]

    each(lev, reach, start)
    src, dst = va, vb
    for sweep in range(3):
        fixup(src, lev, 8)

        def step(i, c, size, src=src, dst=dst):
            rows = pl.ds(c, size)
            wide = pl.ds(8 + c, size)
            v = src[i, wide]
            up = cz[i, rows]
            acc = r[i, rows] + cx[i - 1, rows] * src[i - 1, wide] + cx[i, rows] * src[i + 1, wide]
            acc = acc + cu[i, rows] * src[i, pl.ds(9 + c, size)]
            acc = acc + cd[i, rows] * src[i, pl.ds(7 + c, size)]
            acc = acc + up * pltpu.roll(v, LANES - 1, 1) + pltpu.roll(up * v, 1, 1)
            dst[i, wide] = (1.0 - JACOBI_WEIGHT) * v + w[i, rows] * acc

        each(lev, reach - 1 - sweep, step)
        src, dst = dst, src
    return src


def expand(values, tmp, lev):
    part = values[14 : 14 + lev.span // 4]
    for t in range(4):
        tmp[pl.ds(t, lev.span // 4, stride=4), :] = part


def combine(vf, vm, vl, levels, tmp, ghosts):
    fine, mid, low = levels
    for row_low, rows_mid in ((1, range(1, 5)), (low.ghost, range(mid.ghost, mid.ghost + ghosts))):
        if not len(rows_mid):
            continue
        expand(vl[row_low], tmp, mid)
        for row in rows_mid:
            vm[row, 8 : 8 + mid.span] = vm[row, 8 : 8 + mid.span] + tmp[0 : mid.span]
    for m in range(4 + ghosts):
        expand(vm[1 + m if m < 4 else mid.ghost], tmp, fine)
        rows = range(1 + 4 * m, 5 + 4 * m) if m < 4 else range(fine.ghost, fine.ghost + 1)
        for row in rows:
            here = slice(8, 8 + fine.span)
            vf[row, here] = STEP_WEIGHT * (vf[row, here] + tmp[0 : fine.span])


def third_kernel(
    levels, kz, rz, km, rm, kl, rl, gk, gr, gkm, grm, gkl, grl, ylo, yhi,
    wf, xf, uf, df, zf, wm, xm, um, dm, zm, wl, xl, ul, dl, zl,
    first, defect, dmid, dlow, low, high,
    kf_s, rf_s, vf_s, km_s, rm_s, vm_s, kl_s, rl_s, vl_s, tmp,
):
    fine, mid, coarse = levels
    at = 0
    for lev, own_k, ghost_k, ks, own_r, ghost_r, rs in (
        (fine, kz, gk, kf_s, rz, gr, rf_s),
        (mid, km, gkm, km_s, rm, grm, rm_s),
        (coarse, kl, gkl, kl_s, rl, grl, rl_s),
    ):
        at = fill(ks, 8, lev, own_k, ghost_k, 5, ylo, yhi, at)
        at = fill(rs, 0, lev, own_r, ghost_r, 4, ylo, yhi, at)
    done = []
    for lev, k, r, v, coef in (
        (fine, kf_s, rf_s, vf_s, (wf, xf, uf, df, zf)),
        (mid, km_s, rm_s, vm_s, (wm, xm, um, dm, zm)),
        (coarse, kl_s, rl_s, vl_s, (wl, xl, ul, dl, zl)),
    ):
        setup(lev, k, None, *coef)
        clear_pads(v, lev)
        done.append(smooth(lev, r, v, k, *coef, 4))
    vf, vm, vl = done
    combine(vf, vm, vl, levels, tmp, 1)
    fixup(vf, fine, 8)

    def apply(i, carry):
        for c in range(8, 136, 64):
            rows = pl.ds(c, 64)
            wide = pl.ds(8 + c, 64)
            v = vf[i, wide]
            flux = zf[i, rows] * (v - pltpu.roll(v, LANES - 1, 1))
            image = xf[i - 1, rows] * (v - vf[i - 1, wide]) + xf[i, rows] * (v - vf[i + 1, wide])
            image = image + uf[i, rows] * (v - vf[i, pl.ds(9 + c, 64)])
            image = image + df[i, rows] * (v - vf[i, pl.ds(7 + c, 64)])
            image = image + (flux - pltpu.roll(flux, 1, 1))
            defect[i - 1, pl.ds(c - 8, 64)] = rf_s[i, rows] - image
            first[i - 1, pl.ds(c - 8, 64)] = v
        return carry

    for i in range(1, 17):
        apply(i, 0)
    sum_rows_mid(defect, tmp, dmid, 128, 0)
    dlow[...] = sum_rows_low(dmid, tmp)
    for out, is_low in ((low, True), (high, False)):
        edge = 0 if is_low else 3
        out[...] = join_slots([(defect[j if is_low else 15 - j], edge) for j in range(3)])
        for j in range(3):
            value, source = mid_piece(dmid, j, is_low)
            rows = slice(32 * j, 32 * j + 32)
            out[rows] = jnp.where(quarter((32, LANES)) == 3, move(value, source, 3), out[rows])
            source = j if is_low else 3 - j
            rows = slice(96 + 8 * j, 104 + 8 * j)
            out[rows] = jnp.where(quarter((8, LANES)) == 3, move(dlow[...], source, 3), out[rows])


def fourth_kernel(left, right, defect, dmid, dlow, gf, gm, gl, low, high):
    for j in range(3):
        gf[j] = ghost_of(left[...], right[...], j)
        rows = slice(32 * j, 32 * j + 32)
        gm[j] = ghost_of(left[rows], right[rows], 3)
        rows = slice(96 + 8 * j, 104 + 8 * j)
        gl[j] = ghost_of(left[rows], right[rows], 3)
    at = 0
    for own, ghost, n, width in ((defect, gf, 16, 128), (dmid, gm, 4, 32), (dlow, gl, 0, 8)):
        if n == 0:
            low[at] = own[...]
            high[at] = own[...]
            at += 1
        for i in range(n):
            low[at] = own[i, 0:8]
            high[at] = own[i, width - 8 : width]
            at += 1
        for i in range(3):
            low[at] = ghost[i, 0:8]
            high[at] = ghost[i, width - 8 : width]
            at += 1


def fifth_kernel(
    levels, wf, xf, uf, df, zf, wm, xm, um, dm, zm, wl, xl, ul, dl, zl,
    first, defect, dmid, dlow, gf, gm, gl, ylo, yhi, out,
    rf_s, va_f, vb_f, rm_s, va_m, vb_m, rl_s, va_l, vb_l, tmp,
):
    fine, mid, coarse = levels
    at = 0
    done = []
    for lev, own, ghost, r, va, vb, coef in (
        (fine, defect, gf, rf_s, va_f, vb_f, (wf, xf, uf, df, zf)),
        (mid, dmid, gm, rm_s, va_m, vb_m, (wm, xm, um, dm, zm)),
        (coarse, dlow, gl, rl_s, va_l, vb_l, (wl, xl, ul, dl, zl)),
    ):
        at = fill(r, 0, lev, own, ghost, 3, ylo, yhi, at)
        clear_pads(va, lev)
        clear_pads(vb, lev)
        done.append(smooth(lev, r, va, vb, *coef, 3))
    vf, vm, vl = done
    combine(vf, vm, vl, levels, tmp, 0)
    for x in range(16):
        total = (first[x] + vf[1 + x, 16:144]).T
        for q in range(4):
            out[pl.ds(16 * q + x, DEPTH, stride=64), :] = total[DEPTH * q : DEPTH * q + DEPTH]


def shape(*dims):
    return jax.ShapeDtypeStruct(dims, jnp.float32)


def scratch(*dims):
    return pltpu.VMEM(dims, jnp.float32)


def neighbour(value, axis, hop, back):
    count = lax.axis_size(axis)
    pairs = [(i, i + hop) for i in range(count - hop)]
    if back:
        pairs = [(b, a) for a, b in pairs]
    if not pairs:
        return jnp.zeros_like(value)
    return lax.ppermute(value, axis, pairs)


def on_device(rhs, kappa):
    levels = (
        Level(16, 128, 1.0, 1.0),
        Level(4, 32, 4.0, 16.0),
        Level(1, 8, 16.0, 256.0),
    )
    fine, mid, coarse = levels
    own = [shape(16, 128, LANES), shape(4, 32, LANES), shape(8, LANES)]
    kz, rz, km, rm, kl, rl, low, high = pl.pallas_call(
        first_kernel,
        out_shape=[own[0], own[0], own[1], own[1], own[2], own[2]] + [shape(3, 128, LANES)] * 2,
        scratch_shapes=[scratch(144, LANES)],
        compiler_params=params(),
    )(rhs.reshape(2048, LANES), kappa.reshape(2048, LANES))
    left = neighbour(high, "gx", 1, False)
    right = neighbour(low, "gx", 1, True)
    far_left = neighbour(kl, "gx", 2, False)
    far_right = neighbour(kl, "gx", 2, True)
    gk, gr, gkm, grm, gkl, grl, low, high = pl.pallas_call(
        second_kernel,
        out_shape=[
            shape(5, 128, LANES), shape(4, 128, LANES),
            shape(5, 32, LANES), shape(4, 32, LANES),
            shape(5, 8, LANES), shape(4, 8, LANES),
            shape(69, 8, LANES), shape(69, 8, LANES),
        ],
        compiler_params=params(),
    )(left, right, far_left, far_right, kz, rz, km, rm, kl, rl)
    ylo = neighbour(high, "gy", 1, False)
    yhi = neighbour(low, "gy", 1, True)
    state = []
    for lev in levels:
        state += [shape(lev.rows, lev.span, LANES)] * 5
    bufs = []
    for lev in levels:
        bufs += [
            scratch(lev.rows, lev.span + 16, LANES),
            scratch(lev.rows, lev.span, LANES),
            scratch(lev.rows, lev.span + 16, LANES),
        ]
    results = pl.pallas_call(
        functools.partial(third_kernel, levels),
        out_shape=state + [own[0], own[0], own[1], own[2]] + [shape(128, LANES)] * 2,
        scratch_shapes=bufs + [scratch(144, LANES)],
        compiler_params=params(),
    )(kz, rz, km, rm, kl, rl, gk, gr, gkm, grm, gkl, grl, ylo, yhi)
    state = results[:15]
    first, defect, dmid, dlow, low, high = results[15:]
    left = neighbour(high, "gx", 1, False)
    right = neighbour(low, "gx", 1, True)
    gf, gm, gl, low, high = pl.pallas_call(
        fourth_kernel,
        out_shape=[
            shape(3, 128, LANES), shape(3, 32, LANES), shape(3, 8, LANES),
            shape(30, 8, LANES), shape(30, 8, LANES),
        ],
        compiler_params=params(),
    )(left, right, defect, dmid, dlow)
    ylo = neighbour(high, "gy", 1, False)
    yhi = neighbour(low, "gy", 1, True)
    bufs = []
    for lev in levels:
        bufs += [
            scratch(lev.rows, lev.span, LANES),
            scratch(lev.rows, lev.span + 16, LANES),
            scratch(lev.rows, lev.span + 16, LANES),
        ]
    out = pl.pallas_call(
        functools.partial(fifth_kernel, levels),
        out_shape=shape(2048, LANES),
        scratch_shapes=bufs + [scratch(144, LANES)],
        compiler_params=params(),
    )(*state, first, defect, dmid, dlow, gf, gm, gl, ylo, yhi)
    return out.reshape(rhs.shape)


def solution(mesh):
    return jax.shard_map(
        on_device,
        mesh=mesh,
        in_specs=(P("groups", "gx", "gy"), P("groups", "gx", "gy")),
        out_specs=P("groups", "gx", "gy"),
        check_vma=False,
    )
```

```python
import jax
import jax.numpy as jnp
from jax import lax
from jax.experimental import pallas as pl
from jax.experimental.pallas import tpu as pltpu
from jax.sharding import PartitionSpec as P

JACOBI_WEIGHT = 0.8
STEP_WEIGHT = 0.6
LANES = 128
DEPTH = 32
QUARTERS = 4
REACH = 3


class Level:
    def __init__(self, rows, width, flat, up):
        self.n = rows
        self.own = width
        self.span = width + 16
        self.flat = flat
        self.up = up
        self.rows = rows + 7
        self.ghost = rows + 3

    def work(self, ghosts):
        return list(range(1, self.n + 1)) + list(range(self.ghost, self.ghost + ghosts))


LEVELS = (Level(16, 128, 1.0, 1.0), Level(4, 32, 4.0, 16.0), Level(1, 8, 16.0, 256.0))
FINE, MID, LOW = LEVELS
INNER = [(16, 56), (72, 56)]


class View:
    def __init__(self, ref, shift, side=None):
        self.ref, self.shift, self.side = ref, shift, side

    def at(self, i, p, size):
        rows = slice(p + self.shift, p + self.shift + size)
        return (i, rows) if self.side is None else (i, self.side, rows)

    def get(self, i, p, size):
        return self.ref[self.at(i, p, size)]

    def set(self, i, p, size, value):
        self.ref[self.at(i, p, size)] = value


class Parts:
    def __init__(self, lev, own, ghost, swap=None):
        self.lev, self.own, self.ghost, self.swap = lev, own, ghost, swap or {}

    def get(self, i, p, size):
        rows = slice(p - 8, p - 8 + size)
        if i >= self.lev.ghost:
            return self.ghost[i - self.lev.ghost, rows]
        if i in self.swap:
            return self.swap[i][rows]
        return self.own[rows] if self.lev.n == 1 else self.own[i - 1, rows]


def params(mib=20):
    return pltpu.CompilerParams(vmem_limit_bytes=mib << 20)


def cost(flops):
    return pl.CostEstimate(flops=flops, bytes_accessed=8 << 20, transcendentals=0)


def quarter(shape):
    return lax.broadcasted_iota(jnp.int32, shape, 1) // DEPTH


def sublane(shape):
    return lax.broadcasted_iota(jnp.int32, shape, 0)


def move(value, source, target):
    shift = DEPTH * ((target - source) % QUARTERS)
    return pltpu.roll(value, shift, 1) if shift else value


def join_slots(pieces):
    out = None
    for slot, (value, source) in enumerate(pieces):
        part = move(value, source, slot)
        out = part if out is None else jnp.where(quarter(part.shape) == slot, part, out)
    return out


def edges(left, right):
    group = quarter(left.shape)
    return jnp.where(group == 0, left, jnp.where(group == 3, right, 0.0))


def ghost_of(from_left, from_right, slot):
    return edges(move(from_left, slot, 0), move(from_right, slot, 3))


def two_in_one(a, b):
    group = quarter(a.shape)
    up, down = pltpu.roll(b, DEPTH, 1), pltpu.roll(b, LANES - DEPTH, 1)
    return jnp.where(group == 1, up, jnp.where(group == 2, down, a))


def one_of_two(v, second):
    if not second:
        return edges(v, v)
    return edges(pltpu.roll(v, LANES - DEPTH, 1), pltpu.roll(v, DEPTH, 1))


def mid_piece(ref, j, low):
    index = j if low else 15 - j
    return ref[index % 4], index // 4


def fourths(tmp, size):
    out = tmp[pl.ds(0, size, stride=4), :]
    for t in range(1, 4):
        out = out + tmp[pl.ds(t, size, stride=4), :]
    return out


def sum_rows_mid(rows_ref, tmp, out_ref):
    for m in range(4):
        total = rows_ref[4 * m] + rows_ref[4 * m + 1]
        tmp[m, 0:128, :] = total + rows_ref[4 * m + 2] + rows_ref[4 * m + 3]
        out_ref[m] = fourths(tmp.at[m], 32)


def sum_rows_low(mid_ref, tmp):
    tmp[4, 0:32, :] = mid_ref[0] + mid_ref[1] + mid_ref[2] + mid_ref[3]
    return fourths(tmp.at[4], 8)


def fixup(v, lev, p, size, ghost=True):
    group = quarter((size, LANES))
    first, last = v.get(1, p, size), v.get(lev.n, p, size)
    edge = v.get(lev.ghost, p, size) if ghost else jnp.zeros((size, LANES), jnp.float32)
    v.set(0, p, size, jnp.where(group == 0, edge, pltpu.roll(last, DEPTH, 1)))
    v.set(lev.n + 1, p, size, jnp.where(group == 3, edge, pltpu.roll(first, LANES - DEPTH, 1)))
    if ghost:
        v.set(lev.n + 2, p, size, jnp.where(group == 0, first, last))


def harmonic(a, b):
    total = a + b
    return 2.0 * a * b / jnp.where(total > 0, total, 1.0)


def setup(lev, k, coef, parts):
    w, cx, cu, cd, cz = coef
    for i in range(lev.rows - 1):
        if i == lev.n + 1:
            continue
        for p, size in parts:
            cx.set(i, p, size, lev.flat * harmonic(k.get(i, p, size), k.get(i + 1, p, size)))
    for i in lev.work(REACH):
        for p, size in parts:
            here = k.get(i, p, size)
            above = lev.flat * harmonic(here, k.get(i, p + 1, size))
            below = lev.flat * harmonic(k.get(i, p - 1, size), here)
            z = lax.broadcasted_iota(jnp.int32, (size, LANES), 1) % DEPTH
            up = lev.up * harmonic(here, pltpu.roll(here, LANES - 1, 1))
            up = jnp.where(z == DEPTH - 1, 0.0, up)
            cu.set(i, p, size, above)
            cd.set(i, p, size, below)
            cz.set(i, p, size, up)
            diagonal = cx.get(i - 1, p, size) + cx.get(i, p, size) + (below + above)
            diagonal = diagonal + (pltpu.roll(up, 1, 1) + up)
            good = diagonal > 0
            value = jnp.where(good, JACOBI_WEIGHT / jnp.where(good, diagonal, 1.0), 0.0)
            w.set(i, p, size, value)


def begin(lev, r, v, coef, parts):
    for i in lev.work(REACH):
        for p, size in parts:
            v.set(i, p, size, coef[0].get(i, p, size) * r.get(i, p, size))


def sweep(lev, r, v, out, coef, parts, ghosts):
    w, cx, cu, cd, cz = coef
    for i in lev.work(ghosts):
        for p, size in parts:
            here = v.get(i, p, size)
            up = cz.get(i, p, size)
            acc = r.get(i, p, size) + cx.get(i - 1, p, size) * v.get(i - 1, p, size)
            acc = acc + cx.get(i, p, size) * v.get(i + 1, p, size)
            acc = acc + cu.get(i, p, size) * v.get(i, p + 1, size)
            acc = acc + cd.get(i, p, size) * v.get(i, p - 1, size)
            acc = acc + up * pltpu.roll(here, LANES - 1, 1) + pltpu.roll(up * here, 1, 1)
            out.set(i, p, size, (1.0 - JACOBI_WEIGHT) * here + w.get(i, p, size) * acc)


def clear(v, rows, p):
    for i in range(rows):
        v.set(i, p, 8, jnp.zeros((8, LANES), jnp.float32))


def smooth(lev, r, va, vb, coef):
    parts = [(0, lev.span)]
    for v in (va, vb):
        clear(v, lev.rows, -8)
        clear(v, lev.rows, lev.span)
    begin(lev, r, va, coef, parts)
    src, dst = va, vb
    for number in range(3):
        fixup(src, lev, 0, lev.span)
        sweep(lev, r, src, dst, coef, parts, REACH - 1 - number)
        src, dst = dst, src
    return src


def early_smooth(r, views, coef):
    for v in views[:3]:
        clear(v, FINE.rows, 8)
        clear(v, FINE.rows, 128)
    begin(FINE, r, views[0], coef, INNER)
    for number in range(3):
        fixup(views[number], FINE, 16, 112)
        sweep(FINE, r, views[number], views[number + 1], coef, INNER, REACH - 1 - number)


BEYOND = (24, 112)


def late_smooth(r, early, bufs, coef):
    out = []
    for side, start in ((0, 0), (1, 120)):
        parts = [(start, 24)]
        src, dst = bufs[side]
        for v in (src, dst):
            clear(v, FINE.rows, -8 if side == 0 else 144)
        begin(FINE, r[side], src, coef[side], parts)
        for number in range(3):
            tile = BEYOND[side]
            for i in FINE.work(REACH - number):
                src.set(i, tile, 8, early[number].get(i, tile, 8))
            fixup(src, FINE, start, 24)
            sweep(FINE, r[side], src, dst, coef[side], parts, REACH - 1 - number)
            src, dst = dst, src
        out.append(src)
    return out


def expand(view, row, lev, tmp):
    part = view.get(row, 6, lev.span // 4)
    for t in range(4):
        tmp[pl.ds(t, lev.span // 4, stride=4), :] = part


def correction(vm, vl, tmp):
    expand(vl, 1, MID, tmp.at[4])
    for m in range(4):
        value = vm.get(1 + m, 0, MID.span) + tmp[4, 0 : MID.span]
        vm.set(1 + m, 0, MID.span, value)
        expand(vm, 1 + m, FINE, tmp.at[m])


def pack_y(tiles_low, tiles_high, low, high):
    for n in range((len(tiles_low) + 1) // 2):
        for tiles, out, is_low in ((tiles_low, low, True), (tiles_high, high, False)):
            a = tiles[2 * n]
            if 2 * n + 1 < len(tiles):
                b = pltpu.roll(tiles[2 * n + 1], 4, 0)
                first = sublane((8, LANES)) < 4
                a = jnp.where(first, a, b) if is_low else jnp.where(first, b, a)
            out[n] = a


def unpack_y(ref, n):
    value = ref[n // 2]
    return pltpu.roll(value, 4, 0) if n % 2 else value


def first_kernel(rhs, kappa, kz, rz, km, rm, kl, rl, low, high, tmp):
    for x in range(16):
        for source, target in ((kappa, kz), (rhs, rz)):
            rows = [source[pl.ds(16 * q + x, DEPTH, stride=64), :] for q in range(4)]
            target[x] = jnp.concatenate(rows, axis=0).T
    sum_rows_mid(kz, tmp, km)
    for m in range(4):
        km[m] = km[m] * (1.0 / 16.0)
    sum_rows_mid(rz, tmp, rm)
    kl[...] = sum_rows_low(km, tmp) * (1.0 / 16.0)
    rl[...] = sum_rows_low(rm, tmp)
    for out, is_low in ((low, True), (high, False)):
        edge = 0 if is_low else 3
        line = [j if is_low else 15 - j for j in range(4)]
        out[0:128] = join_slots([(kz[j], edge) for j in line])
        fine = join_slots([(rz[j], edge) for j in line[:3]])
        for j in range(4):
            value, source = mid_piece(km, j, is_low)
            rows = slice(128 + 32 * j, 160 + 32 * j)
            part = jnp.where(
                quarter((32, LANES)) == 3, move(value, source, 3), fine[32 * j : 32 * j + 32]
            )
            out[rows] = part
        out[256:288] = join_slots([mid_piece(rm, j, is_low) for j in range(3)])
        out[288:296] = kl[...]
        out[296:304] = rl[...]


def second_kernel(
    left, right, kz, rz, km, rm, kl, rl, gk, gr, gkm, grm, gkl, grl, low, high
):
    for j in range(4):
        gk[j] = ghost_of(left[0:128], right[0:128], j)
        rows = slice(128 + 32 * j, 160 + 32 * j)
        gkm[j] = ghost_of(left[rows], right[rows], 3)
        gkl[j] = edges(move(left[288:296], 3 - j, 0), move(right[288:296], j, 3))
    for j in range(3):
        gr[j] = ghost_of(left[128:256], right[128:256], j)
        grm[j] = ghost_of(left[256:288], right[256:288], j)
        grl[j] = edges(move(left[296:304], 3 - j, 0), move(right[296:304], j, 3))
    at = 0
    extra = 0
    row = sublane((8, LANES))
    for lev, k, r, ghost_k, ghost_r in (
        (FINE, kz, rz, gk, gr), (MID, km, rm, gkm, grm), (LOW, kl, rl, gkl, grl),
    ):
        for is_low, out in ((True, low), (False, high)):
            rows = slice(0, 8) if is_low else slice(lev.own - 8, lev.own)
            pairs = []
            for i in range(lev.n):
                pairs.append((k[rows], r[rows]) if lev.n == 1 else (k[i, rows], r[i, rows]))
            for a in (0, 2):
                rest = ghost_r[a, rows]
                rest = two_in_one(rest, ghost_r[a + 1, rows]) if a == 0 else rest
                pairs.append((two_in_one(ghost_k[a, rows], ghost_k[a + 1, rows]), rest))
            for i, (a, b) in enumerate(pairs):
                if is_low:
                    out[at + i] = jnp.where(row < 5, a, pltpu.roll(b, 5, 0))
                else:
                    out[at + i] = jnp.where(row >= 3, a, pltpu.roll(b, 3, 0))
            for i in range(lev.n):
                e = extra + i
                cell = slice(3, 4) if is_low else slice(lev.own - 4, lev.own - 3)
                out[27 + e // 8, e % 8 : e % 8 + 1] = r[cell] if lev.n == 1 else r[i, cell]
        at += lev.n + 2
        extra += lev.n


def halos(lev, ylo, yhi, at, extra, k, r, p_low, p_high):
    row = sublane((8, LANES))
    for side, ref in ((0, ylo), (1, yhi)):
        start = p_low if side == 0 else p_high
        for i in range(lev.n + 2):
            value = ref[at + i]
            if side == 0:
                a = jnp.where(row >= 3, value, 0.0)
                b = jnp.where(row >= 5, pltpu.roll(value, 5, 0), 0.0)
            else:
                a = jnp.where(row < 5, value, 0.0)
                b = jnp.where(row < 3, pltpu.roll(value, 3, 0), 0.0)
            if i < lev.n:
                k[side].set(1 + i, start, 8, a)
                r[side].set(1 + i, start, 8, b)
                e = extra + i
                cell = start + 4 if side == 0 else start + 3
                r[side].set(1 + i, cell, 1, ref[27 + e // 8, e % 8 : e % 8 + 1])
                continue
            for part in (0, 1):
                j = 2 * (i - lev.n) + part
                k[side].set(lev.ghost + j, start, 8, one_of_two(a, part))
                if j < REACH:
                    r[side].set(lev.ghost + j, start, 8, one_of_two(b, part))


def own_rows(lev, dst, src, ghosts, p, size):
    for i in lev.work(ghosts):
        dst.set(i, p, size, src.get(i, p, size))


def early_kernel(kz, rz, gk, gr, w, cx, cu, cd, cz, v0, v1, v2, v3, k_s):
    k = View(k_s, -8)
    own_rows(FINE, k, Parts(FINE, kz, gk), 4, 8, 128)
    fixup(k, FINE, 8, 128)
    coef = [View(ref, -16) for ref in (w, cx, cu, cd, cz)]
    setup(FINE, k, coef, INNER)
    views = [View(ref, -8) for ref in (v0, v1, v2, v3)]
    early_smooth(Parts(FINE, rz, gr), views, coef)


def strip_views(refs):
    return [[View(ref, -120 * side, side) for ref in refs] for side in (0, 1)]


def strip_bufs(*refs):
    return [[View(ref, 8 - 112 * side, side) for ref in refs] for side in (0, 1)]


def third_kernel(
    kz, rz, km, rm, kl, rl, gk, gr, gkm, grm, gkl, grl, ylo, yhi,
    w, cx, cu, cd, cz, v0, v1, v2, v3,
    wf, xf, uf, df, zf, wm, xm, um, dm, zm, wl, xl, ul, dl, zl,
    first, defect, dmid, dlow, cedge, low, high,
    ks, rs, sa, sb, km_s, rm_s, vm_s, kl_s, rl_s, vl_s, full, tmp,
):
    early = [View(ref, -16) for ref in (w, cx, cu, cd, cz)]
    early_v = [View(ref, -8) for ref in (v0, v1, v2, v3)]
    done = []
    at, extra = 18, 16
    for lev, own_k, ghost_k, k_ref, own_r, ghost_r, r_ref, v_ref, refs in (
        (MID, km, gkm, km_s, rm, grm, rm_s, vm_s, (wm, xm, um, dm, zm)),
        (LOW, kl, gkl, kl_s, rl, grl, rl_s, vl_s, (wl, xl, ul, dl, zl)),
    ):
        k, r = View(k_ref, 8), View(r_ref, 0)
        own_rows(lev, k, Parts(lev, own_k, ghost_k), 4, 8, lev.own)
        own_rows(lev, r, Parts(lev, own_r, ghost_r), REACH, 8, lev.own)
        halos(lev, ylo, yhi, at, extra, (k, k), (r, r), 0, 8 + lev.own)
        at, extra = at + lev.n + 2, extra + lev.n
        clear(k, lev.rows, -8)
        clear(k, lev.rows, lev.span)
        fixup(k, lev, 0, lev.span)
        coef = [View(ref, 0) for ref in refs]
        setup(lev, k, coef, [(0, lev.span)])
        done.append(smooth(lev, r, View(v_ref, 8), k, coef))
    correction(done[0], done[1], tmp)
    strips = strip_views((wf, xf, uf, df, zf))
    (kl_v,), (kh_v,) = strip_bufs(ks)
    (rl_v,), (rh_v,) = strip_views((rs,))
    halos(FINE, ylo, yhi, 0, 0, (kl_v, kh_v), (rl_v, rh_v), 0, 136)
    for k, r, p_k, p_r, start, pad, kept in (
        (kl_v, rl_v, 8, 8, 0, -8, 16), (kh_v, rh_v, 120, 120, 128, 144, 120),
    ):
        side = 0 if start == 0 else 1
        own_rows(FINE, k, Parts(FINE, kz, gk), 4, p_k, 16)
        own_rows(FINE, r, Parts(FINE, rz, gr), REACH, p_r, 16)
        clear(k, FINE.rows, pad)
        fixup(k, FINE, start if side == 0 else 120, 24)
        setup(FINE, k, strips[side], [(start, 16)])
        for number, (dst, src) in enumerate(zip(strips[side], early)):
            rows = FINE.work(REACH) + ([0, FINE.n + 2] if number == 1 else [])
            for i in rows:
                dst.set(i, kept, 8, src.get(i, kept, 8))
    late = late_smooth((rl_v, rh_v), early_v, strip_bufs(sa, sb), strips)
    whole = View(full, 8)
    for i in range(1, 17):
        m = (i - 1) // 4
        for p, size, v in ((0, 24, late[0]), (24, 48, early_v[3]), (72, 48, early_v[3]), (120, 24, late[1])):
            whole.set(i, p, size, STEP_WEIGHT * (v.get(i, p, size) + tmp[m, p : p + size]))
    fixup(whole, FINE, 8, 128, ghost=False)
    for i in range(1, 17):
        for p, size, coef in ((8, 8, strips[0]), (16, 56, early), (72, 56, early), (128, 8, strips[1])):
            _, x, u, d, z = [c.get(i, p, size) for c in coef]
            v = whole.get(i, p, size)
            flux = z * (v - pltpu.roll(v, LANES - 1, 1))
            image = coef[1].get(i - 1, p, size) * (v - whole.get(i - 1, p, size))
            image = image + x * (v - whole.get(i + 1, p, size))
            image = image + u * (v - whole.get(i, p + 1, size))
            image = image + d * (v - whole.get(i, p - 1, size))
            image = image + (flux - pltpu.roll(flux, 1, 1))
            defect[i - 1, p - 8 : p - 8 + size] = rz[i - 1, p - 8 : p - 8 + size] - image
            first[i - 1, p - 8 : p - 8 + size] = v
    for p, size, coef in ((8, 8, strips[0]), (16, 112, early), (128, 8, strips[1])):
        cedge[p - 8 : p - 8 + size] = edges(coef[1].get(0, p, size), coef[1].get(16, p, size))
    sum_rows_mid(defect, tmp, dmid)
    dlow[...] = sum_rows_low(dmid, tmp)
    for out, is_low in ((low, True), (high, False)):
        edge = 0 if is_low else 3
        fine = join_slots([(defect[j if is_low else 15 - j], edge) for j in range(3)])
        for j in range(3):
            value, source = mid_piece(dmid, j, is_low)
            rows = slice(32 * j, 32 * j + 32)
            out[rows] = jnp.where(quarter((32, LANES)) == 3, move(value, source, 3), fine[rows])
            source = j if is_low else 3 - j
            rows = slice(96 + 8 * j, 104 + 8 * j)
            out[rows] = jnp.where(quarter((8, LANES)) == 3, move(dlow[...], source, 3), fine[rows])
        out[120:128] = fine[120:128]
        line = 0 if is_low else 15
        out[128:160] = join_slots([(first[line, 32 * g : 32 * g + 32], edge) for g in range(4)])


def fourth_kernel(
    left, right, first, defect, dmid, dlow, cedge,
    gf, gm, gl, d0, d15, m0, m3, lows, low, high, tmp,
):
    face = cedge[...]
    group = quarter((128, LANES))
    other = [ghost_of(left[128:160], right[128:160], g) for g in range(4)]
    mine = face * jnp.concatenate(other, axis=0)
    theirs = face * edges(first[0], first[15])
    d0[...] = defect[0] + jnp.where(group == 0, mine, 0.0)
    d15[...] = defect[15] + jnp.where(group == 3, mine, 0.0)
    sums = []
    for n, value in enumerate((mine, theirs)):
        tmp[n, 0:128, :] = value
        mid = fourths(tmp.at[n], 32)
        tmp[n + 2, 0:32, :] = mid
        sums.append((mid, fourths(tmp.at[n + 2], 8)))
    group = quarter((32, LANES))
    m0[...] = dmid[0] + jnp.where(group == 0, sums[0][0], 0.0)
    m3[...] = dmid[3] + jnp.where(group == 3, sums[0][0], 0.0)
    lows[...] = dlow[...] + sums[0][1]
    for j in range(3):
        for out, rows, slot, add in (
            (gf, slice(0, 128), j, theirs),
            (gm, slice(32 * j, 32 * j + 32), 3, sums[1][0]),
            (gl, slice(96 + 8 * j, 104 + 8 * j), 3, sums[1][1]),
        ):
            value = ghost_of(left[rows], right[rows], slot)
            out[j] = value + add if j == 0 else value
    tiles = ([], [])
    for lev, r, ghost in (
        (FINE, Parts(FINE, defect, gf, {1: d0, 16: d15}), gf),
        (MID, Parts(MID, dmid, gm, {1: m0, 4: m3}), gm),
        (LOW, Parts(LOW, lows, gl), gl),
    ):
        for side, p in ((0, 8), (1, lev.own)):
            tiles[side].extend(r.get(i, p, 8) for i in range(1, lev.n + 1))
            a, b, c = [r.get(lev.ghost + j, p, 8) for j in range(3)]
            tiles[side].extend([two_in_one(a, b), c])
    pack_y(tiles[0], tiles[1], low, high)


def residual_halos(lev, ylo, yhi, at, r, p_low, p_high):
    for side, ref in ((0, ylo), (1, yhi)):
        start = p_low if side == 0 else p_high
        for i in range(lev.n):
            r[side].set(1 + i, start, 8, unpack_y(ref, at + i))
        both = unpack_y(ref, at + lev.n)
        r[side].set(lev.ghost, start, 8, one_of_two(both, 0))
        r[side].set(lev.ghost + 1, start, 8, one_of_two(both, 1))
        r[side].set(lev.ghost + 2, start, 8, unpack_y(ref, at + lev.n + 1))


def early_again_kernel(defect, gf, d0, d15, w, cx, cu, cd, cz, v0, v1, v2, v3):
    coef = [View(ref, -16) for ref in (w, cx, cu, cd, cz)]
    views = [View(ref, -8) for ref in (v0, v1, v2, v3)]
    early_smooth(Parts(FINE, defect, gf, {1: d0, 16: d15}), views, coef)


def fifth_kernel(
    wf, xf, uf, df, zf, wm, xm, um, dm, zm, wl, xl, ul, dl, zl,
    first, defect, dmid, gf, gm, gl, d0, d15, m0, m3, lows, v0, v1, v2, v3, ylo, yhi, out,
    rs, sa, sb, rm_s, va_m, vb_m, rl_s, va_l, vb_l, tmp,
):
    early_v = [View(ref, -8) for ref in (v0, v1, v2, v3)]
    done = []
    at = 18
    for lev, parts, r_ref, va, vb, refs in (
        (MID, Parts(MID, dmid, gm, {1: m0, 4: m3}), rm_s, va_m, vb_m, (wm, xm, um, dm, zm)),
        (LOW, Parts(LOW, lows, gl), rl_s, va_l, vb_l, (wl, xl, ul, dl, zl)),
    ):
        r = View(r_ref, 0)
        own_rows(lev, r, parts, REACH, 8, lev.own)
        residual_halos(lev, ylo, yhi, at, (r, r), 0, 8 + lev.own)
        at += lev.n + 2
        coef = [View(ref, 0) for ref in refs]
        done.append(smooth(lev, r, View(va, 8), View(vb, 8), coef))
    correction(done[0], done[1], tmp)
    strips = strip_views((wf, xf, uf, df, zf))
    (rl_v,), (rh_v,) = strip_views((rs,))
    parts = Parts(FINE, defect, gf, {1: d0, 16: d15})
    own_rows(FINE, rl_v, parts, REACH, 8, 16)
    own_rows(FINE, rh_v, parts, REACH, 120, 16)
    residual_halos(FINE, ylo, yhi, 0, (rl_v, rh_v), 0, 136)
    late = late_smooth((rl_v, rh_v), early_v, strip_bufs(sa, sb), strips)
    for x in range(16):
        pieces = []
        for p, size, v in ((8, 16, late[0]), (24, 96, early_v[3]), (120, 16, late[1])):
            part = v.get(1 + x, p, size) + tmp[x // 4, p : p + size]
            pieces.append(first[x, p - 8 : p - 8 + size] + STEP_WEIGHT * part)
        total = jnp.concatenate(pieces, axis=0).T
        for q in range(4):
            out[pl.ds(16 * q + x, DEPTH, stride=64), :] = total[DEPTH * q : DEPTH * q + DEPTH]


def shape(*dims):
    return jax.ShapeDtypeStruct(dims, jnp.float32)


def scratch(*dims):
    return pltpu.VMEM(dims, jnp.float32)


def neighbour(value, axis, back):
    pairs = [(i, i + 1) for i in range(lax.axis_size(axis) - 1)]
    if back:
        pairs = [(b, a) for a, b in pairs]
    return lax.ppermute(value, axis, pairs)


def on_device(rhs, kappa):
    def call(body, outs, scratches=(), flops=10**6):
        return pl.pallas_call(
            body,
            out_shape=outs,
            scratch_shapes=list(scratches),
            compiler_params=params(),
            cost_estimate=cost(flops),
        )

    n = FINE.rows
    own = [shape(16, 128, LANES), shape(4, 32, LANES), shape(8, LANES)]
    tmp = scratch(5, 144, LANES)
    outs = [own[0], own[0], own[1], own[1], own[2], own[2]] + [shape(304, LANES)] * 2
    kz, rz, km, rm, kl, rl, low, high = call(first_kernel, outs, [tmp])(
        rhs.reshape(2048, LANES), kappa.reshape(2048, LANES)
    )
    left, right = neighbour(high, "gx", False), neighbour(low, "gx", True)
    outs = [shape(g, width, LANES) for width in (128, 32, 8) for g in (4, 3)]
    *ghosts, low, high = call(second_kernel, outs + [shape(30, 8, LANES)] * 2)(
        left, right, kz, rz, km, rm, kl, rl
    )
    gk, gr = ghosts[:2]
    ylo, yhi = neighbour(high, "gy", False), neighbour(low, "gy", True)
    outs = [shape(n, 112, LANES)] * 5 + [shape(n, 128, LANES)] * 4
    early = call(early_kernel, outs, [scratch(n, 128, LANES)], 10**8)(kz, rz, gk, gr)
    strip = shape(n, 2, 24, LANES)
    outs = [strip] * 5
    for lev in (MID, LOW):
        outs += [shape(lev.rows, lev.span, LANES)] * 5
    outs += [own[0], own[0], own[1], own[2], shape(128, LANES)] + [shape(160, LANES)] * 2
    strip_scratch = [scratch(n, 2, 48, LANES), scratch(n, 2, 24, LANES)]
    bufs = strip_scratch + [scratch(n, 2, 48, LANES)] * 2
    for lev in (MID, LOW):
        wide = scratch(lev.rows, lev.span + 16, LANES)
        bufs += [wide, scratch(lev.rows, lev.span, LANES), wide]
    bufs += [scratch(n, 160, LANES), tmp]
    results = call(third_kernel, outs, bufs)(kz, rz, km, rm, kl, rl, *ghosts, ylo, yhi, *early)
    state = results[:15]
    first, defect, dmid, dlow, cedge, low, high = results[15:]
    left, right = neighbour(high, "gx", False), neighbour(low, "gx", True)
    outs = [shape(3, width, LANES) for width in (128, 32, 8)]
    outs += [shape(128, LANES)] * 2 + [shape(32, LANES)] * 2 + [shape(8, LANES)]
    *halo, low, high = call(fourth_kernel, outs + [shape(14, 8, LANES)] * 2, [tmp])(
        left, right, first, defect, dmid, dlow, cedge
    )
    gf, gm, gl, d0, d15, m0, m3, lows = halo
    ylo, yhi = neighbour(high, "gy", False), neighbour(low, "gy", True)
    inner = call(early_again_kernel, [shape(n, 128, LANES)] * 4, (), 10**8)(
        defect, gf, d0, d15, *early[:5]
    )
    bufs = [strip_scratch[1]] + [scratch(n, 2, 48, LANES)] * 2
    for lev in (MID, LOW):
        wide = scratch(lev.rows, lev.span + 16, LANES)
        bufs += [scratch(lev.rows, lev.span, LANES), wide, wide]
    out = call(fifth_kernel, shape(2048, LANES), bufs + [tmp])(
        *state, first, defect, dmid, *halo, *inner, ylo, yhi
    )
    return out.reshape(rhs.shape)


def solution(mesh):
    return jax.shard_map(
        on_device,
        mesh=mesh,
        in_specs=(P("groups", "gx", "gy"), P("groups", "gx", "gy")),
        out_specs=P("groups", "gx", "gy"),
        check_vma=False,
    )
```

```python
import jax
import jax.numpy as jnp
from jax import lax
from jax.experimental import pallas as pl
from jax.experimental.pallas import tpu as pltpu
from jax.sharding import PartitionSpec as P

JACOBI_WEIGHT = 0.8
STEP_WEIGHT = 0.6
LANES = 128
DEPTH = 32
QUARTERS = 4
REACH = 3


class Level:
    def __init__(self, rows, width, flat, up):
        self.n = rows
        self.own = width
        self.span = width + 16
        self.flat = flat
        self.up = up
        self.rows = rows + 7
        self.ghost = rows + 3

    def work(self, ghosts):
        return list(range(1, self.n + 1)) + list(range(self.ghost, self.ghost + ghosts))

    def faces(self):
        return [i for i in range(self.rows - 1) if i != self.n + 1]


LEVELS = (Level(16, 128, 1.0, 1.0), Level(4, 32, 4.0, 16.0), Level(1, 8, 16.0, 256.0))
FINE, MID, LOW = LEVELS
INNER = [(16, 56), (72, 56)]
SAFE, SAFE_FACES = range(2, 16), range(1, 16)


def grouped(rows, most):
    out = []
    for i in rows:
        if out and len(out[-1]) < most and out[-1][-1] == i - 1:
            out[-1].append(i)
        else:
            out.append([i])
    return out


def near(group, by=0):
    if len(group) == 1:
        return group[0] + by
    return slice(group[0] + by, group[-1] + 1 + by)


def spin(value, shift):
    return pltpu.roll(value, shift, value.ndim - 1)


class View:
    def __init__(self, ref, shift, side=None):
        self.ref, self.shift, self.side = ref, shift, side

    def at(self, i, p, size):
        rows = slice(p + self.shift, p + self.shift + size)
        return (i, rows) if self.side is None else (i, self.side, rows)

    def get(self, i, p, size):
        return self.ref[self.at(i, p, size)]

    def set(self, i, p, size, value):
        self.ref[self.at(i, p, size)] = value


class Split:
    def __init__(self, rows, inside, outside):
        self.rows, self.inside, self.outside = rows, inside, outside

    def get(self, i, p, size):
        return (self.inside if i in self.rows else self.outside).get(i, p, size)


def split_views(inside, outside):
    out = []
    for n, (a, b) in enumerate(zip(inside, outside)):
        out.append(Split(SAFE_FACES if n == 1 else SAFE, View(a, -16), View(b, -16)))
    return out


class Parts:
    def __init__(self, lev, own, ghost, swap=None):
        self.lev, self.own, self.ghost, self.swap = lev, own, ghost, swap or {}

    def get(self, i, p, size):
        rows = slice(p - 8, p - 8 + size)
        if i >= self.lev.ghost:
            return self.ghost[i - self.lev.ghost, rows]
        if i in self.swap:
            return self.swap[i][rows]
        return self.own[rows] if self.lev.n == 1 else self.own[i - 1, rows]


def params(mib=20):
    return pltpu.CompilerParams(vmem_limit_bytes=mib << 20)


def cost(flops):
    return pl.CostEstimate(flops=flops, bytes_accessed=8 << 20, transcendentals=0)


def quarter(shape):
    return lax.broadcasted_iota(jnp.int32, shape, 1) // DEPTH


def sublane(shape):
    return lax.broadcasted_iota(jnp.int32, shape, 0)


class Pick:
    def __init__(self, first, second, use_first):
        self.first, self.second, self.use_first = first, second, use_first

    def __getitem__(self, at):
        return jnp.where(self.use_first, self.first[at], self.second[at])


def is_even(axis):
    return lax.axis_index(axis) % 2 == 0


def received(axis, a, b):
    even = is_even(axis)
    return Pick(b, a, even), Pick(a, b, even)


def ship(axis, low, high, a, b):
    even = is_even(axis)
    below, above = low[...], high[...]
    a[...] = jnp.where(even, above, below)
    b[...] = jnp.where(even, below, above)


def move(value, source, target):
    shift = DEPTH * ((target - source) % QUARTERS)
    return pltpu.roll(value, shift, 1) if shift else value


def join_slots(pieces):
    out = None
    for slot, (value, source) in enumerate(pieces):
        part = move(value, source, slot)
        out = part if out is None else jnp.where(quarter(part.shape) == slot, part, out)
    return out


def edges(left, right):
    group = quarter(left.shape)
    return jnp.where(group == 0, left, jnp.where(group == 3, right, 0.0))


def ghost_of(from_left, from_right, slot):
    return edges(move(from_left, slot, 0), move(from_right, slot, 3))


def two_in_one(a, b):
    group = quarter(a.shape)
    up, down = pltpu.roll(b, DEPTH, 1), pltpu.roll(b, LANES - DEPTH, 1)
    return jnp.where(group == 1, up, jnp.where(group == 2, down, a))


def one_of_two(v, second):
    if not second:
        return edges(v, v)
    return edges(pltpu.roll(v, LANES - DEPTH, 1), pltpu.roll(v, DEPTH, 1))


def mid_piece(ref, j, low):
    index = j if low else 15 - j
    return ref[index % 4], index // 4


def fourths(tmp, size):
    out = tmp[pl.ds(0, size, stride=4), :]
    for t in range(1, 4):
        out = out + tmp[pl.ds(t, size, stride=4), :]
    return out


def sum_rows_mid(rows_ref, tmp, out_ref):
    for m in range(4):
        total = rows_ref[4 * m] + rows_ref[4 * m + 1]
        tmp[m, 0:128, :] = total + rows_ref[4 * m + 2] + rows_ref[4 * m + 3]
        out_ref[m] = fourths(tmp.at[m], 32)


def sum_rows_low(mid_ref, tmp):
    tmp[4, 0:32, :] = mid_ref[0] + mid_ref[1] + mid_ref[2] + mid_ref[3]
    return fourths(tmp.at[4], 8)


def fixup(v, lev, p, size, ghost=True):
    group = quarter((size, LANES))
    first, last = v.get(1, p, size), v.get(lev.n, p, size)
    edge = v.get(lev.ghost, p, size) if ghost else jnp.zeros((size, LANES), jnp.float32)
    v.set(0, p, size, jnp.where(group == 0, edge, pltpu.roll(last, DEPTH, 1)))
    v.set(lev.n + 1, p, size, jnp.where(group == 3, edge, pltpu.roll(first, LANES - DEPTH, 1)))
    if ghost:
        v.set(lev.n + 2, p, size, jnp.where(group == 0, first, last))


def harmonic(a, b):
    total = a + b
    return 2.0 * a * b / jnp.where(total > 0, total, 1.0)


def setup(lev, k, coef, parts, most=1, faces=None, work=None):
    w, cx, cu, cd, cz = coef
    for group in grouped(lev.faces() if faces is None else faces, most):
        i, j = near(group), near(group, 1)
        for p, size in parts:
            cx.set(i, p, size, lev.flat * harmonic(k.get(i, p, size), k.get(j, p, size)))
    for group in grouped(lev.work(REACH) if work is None else work, most):
        i = near(group)
        for p, size in parts:
            here = k.get(i, p, size)
            above = lev.flat * harmonic(here, k.get(i, p + 1, size))
            below = lev.flat * harmonic(k.get(i, p - 1, size), here)
            z = lax.broadcasted_iota(jnp.int32, here.shape, here.ndim - 1) % DEPTH
            up = lev.up * harmonic(here, spin(here, LANES - 1))
            up = jnp.where(z == DEPTH - 1, 0.0, up)
            cu.set(i, p, size, above)
            cd.set(i, p, size, below)
            cz.set(i, p, size, up)
            diagonal = cx.get(near(group, -1), p, size) + cx.get(i, p, size) + (below + above)
            diagonal = diagonal + (spin(up, 1) + up)
            good = diagonal > 0
            value = jnp.where(good, JACOBI_WEIGHT / jnp.where(good, diagonal, 1.0), 0.0)
            w.set(i, p, size, value)


def begin(lev, r, v, coef, parts, most=1):
    for group in grouped(lev.work(REACH), most):
        i = near(group)
        for p, size in parts:
            v.set(i, p, size, coef[0].get(i, p, size) * r.get(i, p, size))


def sweep(lev, r, v, out, coef, parts, ghosts, most=1):
    w, cx, cu, cd, cz = coef
    for group in grouped(lev.work(ghosts), most):
        i, before, after = near(group), near(group, -1), near(group, 1)
        for p, size in parts:
            here = v.get(i, p, size)
            up = cz.get(i, p, size)
            acc = r.get(i, p, size) + cx.get(before, p, size) * v.get(before, p, size)
            acc = acc + cx.get(i, p, size) * v.get(after, p, size)
            acc = acc + cu.get(i, p, size) * v.get(i, p + 1, size)
            acc = acc + cd.get(i, p, size) * v.get(i, p - 1, size)
            acc = acc + up * spin(here, LANES - 1) + spin(up * here, 1)
            out.set(i, p, size, (1.0 - JACOBI_WEIGHT) * here + w.get(i, p, size) * acc)


def clear(v, rows, p):
    for i in range(rows):
        v.set(i, p, 8, jnp.zeros((8, LANES), jnp.float32))


def late_smooth(fine_r, early, bufs, fine_coef, others):
    jobs = []
    for side, start in ((0, 0), (1, 120)):
        for v in bufs[side]:
            clear(v, FINE.rows, -8 if side == 0 else 144)
        jobs.append((FINE, fine_r[side], list(bufs[side]), fine_coef[side], start, 24, 3, side))
    for lev, r, va, vb, coef in others:
        for v in (va, vb):
            clear(v, lev.rows, -8)
            clear(v, lev.rows, lev.span)
        jobs.append((lev, r, [va, vb], coef, 0, lev.span, 1 if lev is MID else 3, None))
    for lev, r, pair, coef, start, size, most, side in jobs:
        begin(lev, r, pair[0], coef, [(start, size)], most)
    for number in range(3):
        for lev, r, pair, coef, start, size, most, side in jobs:
            if side is not None:
                tile = BEYOND[side]
                for i in lev.work(REACH - number):
                    pair[0].set(i, tile, 8, early[number].get(i, tile, 8))
            fixup(pair[0], lev, start, size)
        for lev, r, pair, coef, start, size, most, side in jobs:
            sweep(lev, r, pair[0], pair[1], coef, [(start, size)], REACH - 1 - number, most)
            pair.reverse()
    return [job[2][0] for job in jobs]


def early_smooth(r, views, coef):
    for v in views[:3]:
        clear(v, FINE.rows, 8)
        clear(v, FINE.rows, 128)
    begin(FINE, r, views[0], coef, INNER)
    for number in range(3):
        fixup(views[number], FINE, 16, 112)
        sweep(FINE, r, views[number], views[number + 1], coef, INNER, REACH - 1 - number)


BEYOND = (24, 112)


def expand(view, row, lev, tmp):
    part = view.get(row, 6, lev.span // 4)
    for t in range(4):
        tmp[pl.ds(t, lev.span // 4, stride=4), :] = part


def correction(vm, vl, tmp):
    expand(vl, 1, MID, tmp.at[4])
    for m in range(4):
        value = vm.get(1 + m, 0, MID.span) + tmp[4, 0 : MID.span]
        vm.set(1 + m, 0, MID.span, value)
        expand(vm, 1 + m, FINE, tmp.at[m])


def pack_y(tiles_low, tiles_high, low, high):
    for n in range((len(tiles_low) + 1) // 2):
        for tiles, out, is_low in ((tiles_low, low, True), (tiles_high, high, False)):
            a = tiles[2 * n]
            if 2 * n + 1 < len(tiles):
                b = pltpu.roll(tiles[2 * n + 1], 4, 0)
                first = sublane((8, LANES)) < 4
                a = jnp.where(first, a, b) if is_low else jnp.where(first, b, a)
            out[n] = a


def unpack_y(ref, n):
    value = ref[n // 2]
    return pltpu.roll(value, 4, 0) if n % 2 else value


def first_kernel(
    rhs, kappa, kz, rz, km, rm, kl, rl, send_a, send_b, tmp, k_in, r_in, low, high, sems
):
    copies = []
    for n, (source, target) in enumerate(((kappa, k_in), (rhs, r_in))):
        for c in range(4):
            rows = slice(512 * c, 512 * c + 512)
            copy = pltpu.make_async_copy(source.at[rows], target.at[rows], sems.at[4 * n + c])
            copy.start()
            copies.append(copy)
    for n, (source, target) in enumerate(((k_in, kz), (r_in, rz))):
        for copy in copies[4 * n : 4 * n + 4]:
            copy.wait()
        for x in range(16):
            rows = [source[pl.ds(16 * q + x, DEPTH, stride=64), :] for q in range(4)]
            target[x] = jnp.concatenate(rows, axis=0).T
    sum_rows_mid(kz, tmp, km)
    for m in range(4):
        km[m] = km[m] * (1.0 / 16.0)
    sum_rows_mid(rz, tmp, rm)
    kl[...] = sum_rows_low(km, tmp) * (1.0 / 16.0)
    rl[...] = sum_rows_low(rm, tmp)
    for out, is_low in ((low, True), (high, False)):
        edge = 0 if is_low else 3
        line = [j if is_low else 15 - j for j in range(4)]
        out[0:128] = join_slots([(kz[j], edge) for j in line])
        fine = join_slots([(rz[j], edge) for j in line[:3]])
        for j in range(4):
            value, source = mid_piece(km, j, is_low)
            rows = slice(128 + 32 * j, 160 + 32 * j)
            part = jnp.where(
                quarter((32, LANES)) == 3, move(value, source, 3), fine[32 * j : 32 * j + 32]
            )
            out[rows] = part
        out[256:288] = join_slots([mid_piece(rm, j, is_low) for j in range(3)])
        out[288:296] = kl[...]
        out[296:304] = rl[...]
    ship("gx", low, high, send_a, send_b)


def second_kernel(
    got_a, got_b, kz, rz, km, rm, kl, rl, gk, gr, gkm, grm, gkl, grl, send_a, send_b, low, high
):
    left, right = received("gx", got_a, got_b)
    for j in range(4):
        gk[j] = ghost_of(left[0:128], right[0:128], j)
        rows = slice(128 + 32 * j, 160 + 32 * j)
        gkm[j] = ghost_of(left[rows], right[rows], 3)
        gkl[j] = edges(move(left[288:296], 3 - j, 0), move(right[288:296], j, 3))
    for j in range(3):
        gr[j] = ghost_of(left[128:256], right[128:256], j)
        grm[j] = ghost_of(left[256:288], right[256:288], j)
        grl[j] = edges(move(left[296:304], 3 - j, 0), move(right[296:304], j, 3))
    at = 0
    extra = 0
    row = sublane((8, LANES))
    for lev, k, r, ghost_k, ghost_r in (
        (FINE, kz, rz, gk, gr), (MID, km, rm, gkm, grm), (LOW, kl, rl, gkl, grl),
    ):
        for is_low, out in ((True, low), (False, high)):
            rows = slice(0, 8) if is_low else slice(lev.own - 8, lev.own)
            pairs = []
            for i in range(lev.n):
                pairs.append((k[rows], r[rows]) if lev.n == 1 else (k[i, rows], r[i, rows]))
            for a in (0, 2):
                rest = ghost_r[a, rows]
                rest = two_in_one(rest, ghost_r[a + 1, rows]) if a == 0 else rest
                pairs.append((two_in_one(ghost_k[a, rows], ghost_k[a + 1, rows]), rest))
            for i, (a, b) in enumerate(pairs):
                if is_low:
                    out[at + i] = jnp.where(row < 5, a, pltpu.roll(b, 5, 0))
                else:
                    out[at + i] = jnp.where(row >= 3, a, pltpu.roll(b, 3, 0))
            for i in range(lev.n):
                e = extra + i
                cell = slice(3, 4) if is_low else slice(lev.own - 4, lev.own - 3)
                out[27 + e // 8, e % 8 : e % 8 + 1] = r[cell] if lev.n == 1 else r[i, cell]
        at += lev.n + 2
        extra += lev.n
    ship("gy", low, high, send_a, send_b)


def halos(lev, ylo, yhi, at, extra, k, r, p_low, p_high):
    row = sublane((8, LANES))
    for side, ref in ((0, ylo), (1, yhi)):
        start = p_low if side == 0 else p_high
        for i in range(lev.n + 2):
            value = ref[at + i]
            if side == 0:
                a = jnp.where(row >= 3, value, 0.0)
                b = jnp.where(row >= 5, pltpu.roll(value, 5, 0), 0.0)
            else:
                a = jnp.where(row < 5, value, 0.0)
                b = jnp.where(row < 3, pltpu.roll(value, 3, 0), 0.0)
            if i < lev.n:
                k[side].set(1 + i, start, 8, a)
                r[side].set(1 + i, start, 8, b)
                e = extra + i
                cell = start + 4 if side == 0 else start + 3
                r[side].set(1 + i, cell, 1, ref[27 + e // 8, e % 8 : e % 8 + 1])
                continue
            for part in (0, 1):
                j = 2 * (i - lev.n) + part
                k[side].set(lev.ghost + j, start, 8, one_of_two(a, part))
                if j < REACH:
                    r[side].set(lev.ghost + j, start, 8, one_of_two(b, part))


def own_rows(lev, dst, src, ghosts, p, size):
    for i in lev.work(ghosts):
        dst.set(i, p, size, src.get(i, p, size))


def safe_kernel(kz, w, cx, cu, cd, cz):
    coef = [View(ref, -16) for ref in (w, cx, cu, cd, cz)]
    setup(FINE, Parts(FINE, kz, None), coef, INNER, 1, SAFE_FACES, SAFE)


def early_kernel(
    kz, rz, gk, gr, wa, xa, ua, da, za, w, cx, cu, cd, cz, v0, v1, v2, v3, k_s
):
    k = View(k_s, -8)
    own = Parts(FINE, kz, gk)
    edge = [i for i in FINE.work(4) if i not in SAFE]
    for i in edge:
        k.set(i, 8, 128, own.get(i, 8, 128))
    fixup(k, FINE, 8, 128)
    new = [View(ref, -16) for ref in (w, cx, cu, cd, cz)]
    both = split_views((wa, xa, ua, da, za), (w, cx, cu, cd, cz))
    faces = [i for i in FINE.faces() if i not in SAFE_FACES]
    for n, part in enumerate(both):
        part.set = new[n].set
    setup(FINE, k, both, INNER, 1, faces, [i for i in edge if i < FINE.ghost + REACH])
    views = [View(ref, -8) for ref in (v0, v1, v2, v3)]
    early_smooth(Parts(FINE, rz, gr), views, both)


def strip_views(refs):
    return [[View(ref, -120 * side, side) for ref in refs] for side in (0, 1)]


def strip_bufs(*refs):
    return [[View(ref, 8 - 112 * side, side) for ref in refs] for side in (0, 1)]


def third_kernel(
    kz, rz, km, rm, kl, rl, gk, gr, gkm, grm, gkl, grl, got_a, got_b,
    wa, xa, ua, da, za, w, cx, cu, cd, cz, v0, v1, v2, v3,
    wf, xf, uf, df, zf, wm, xm, um, dm, zm, wl, xl, ul, dl, zl,
    first, defect, dmid, dlow, cedge, send_a, send_b,
    ks, rs, sa, sb, km_s, rm_s, vm_s, kl_s, rl_s, vl_s, full, tmp, low, high,
):
    ylo, yhi = received("gy", got_a, got_b)
    early = split_views((wa, xa, ua, da, za), (w, cx, cu, cd, cz))
    early_v = [View(ref, -8) for ref in (v0, v1, v2, v3)]
    others = []
    at, extra = 18, 16
    for lev, own_k, ghost_k, k_ref, own_r, ghost_r, r_ref, v_ref, refs in (
        (MID, km, gkm, km_s, rm, grm, rm_s, vm_s, (wm, xm, um, dm, zm)),
        (LOW, kl, gkl, kl_s, rl, grl, rl_s, vl_s, (wl, xl, ul, dl, zl)),
    ):
        k, r = View(k_ref, 8), View(r_ref, 0)
        own_rows(lev, k, Parts(lev, own_k, ghost_k), 4, 8, lev.own)
        own_rows(lev, r, Parts(lev, own_r, ghost_r), REACH, 8, lev.own)
        halos(lev, ylo, yhi, at, extra, (k, k), (r, r), 0, 8 + lev.own)
        at, extra = at + lev.n + 2, extra + lev.n
        clear(k, lev.rows, -8)
        clear(k, lev.rows, lev.span)
        fixup(k, lev, 0, lev.span)
        coef = [View(ref, 0) for ref in refs]
        setup(lev, k, coef, [(0, lev.span)], 1 if lev is MID else 3)
        others.append((lev, r, View(v_ref, 8), k, coef))
    strips = strip_views((wf, xf, uf, df, zf))
    (kl_v,), (kh_v,) = strip_bufs(ks)
    (rl_v,), (rh_v,) = strip_views((rs,))
    halos(FINE, ylo, yhi, 0, 0, (kl_v, kh_v), (rl_v, rh_v), 0, 136)
    for k, r, p_k, p_r, start, pad, kept in (
        (kl_v, rl_v, 8, 8, 0, -8, 16), (kh_v, rh_v, 120, 120, 128, 144, 120),
    ):
        side = 0 if start == 0 else 1
        own_rows(FINE, k, Parts(FINE, kz, gk), 4, p_k, 16)
        own_rows(FINE, r, Parts(FINE, rz, gr), REACH, p_r, 16)
        clear(k, FINE.rows, pad)
        fixup(k, FINE, start if side == 0 else 120, 24)
        setup(FINE, k, strips[side], [(start, 16)], 4)
        for number, (dst, src) in enumerate(zip(strips[side], early)):
            rows = FINE.work(REACH) + ([0, FINE.n + 2] if number == 1 else [])
            for i in rows:
                dst.set(i, kept, 8, src.get(i, kept, 8))
    *late, vm, vl = late_smooth((rl_v, rh_v), early_v, strip_bufs(sa, sb), strips, others)
    correction(vm, vl, tmp)
    whole = View(full, 8)
    for i in range(1, 17):
        m = (i - 1) // 4
        for p, size, v in ((0, 24, late[0]), (24, 48, early_v[3]), (72, 48, early_v[3]), (120, 24, late[1])):
            whole.set(i, p, size, STEP_WEIGHT * (v.get(i, p, size) + tmp[m, p : p + size]))
    fixup(whole, FINE, 8, 128, ghost=False)
    for most, p, size, coef in (
        (8, 8, 8, strips[0]), (1, 16, 56, early), (1, 72, 56, early), (8, 128, 8, strips[1]),
    ):
        for group in grouped(range(1, 17), most):
            i, before, after = near(group), near(group, -1), near(group, 1)
            _, x, u, d, z = [c.get(i, p, size) for c in coef]
            v = whole.get(i, p, size)
            flux = z * (v - spin(v, LANES - 1))
            image = coef[1].get(before, p, size) * (v - whole.get(before, p, size))
            image = image + x * (v - whole.get(after, p, size))
            image = image + u * (v - whole.get(i, p + 1, size))
            image = image + d * (v - whole.get(i, p - 1, size))
            image = image + (flux - spin(flux, 1))
            defect[before, p - 8 : p - 8 + size] = rz[before, p - 8 : p - 8 + size] - image
            first[before, p - 8 : p - 8 + size] = v
    for p, size, coef in ((8, 8, strips[0]), (16, 112, early), (128, 8, strips[1])):
        cedge[p - 8 : p - 8 + size] = edges(coef[1].get(0, p, size), coef[1].get(16, p, size))
    sum_rows_mid(defect, tmp, dmid)
    dlow[...] = sum_rows_low(dmid, tmp)
    for out, is_low in ((low, True), (high, False)):
        edge = 0 if is_low else 3
        fine = join_slots([(defect[j if is_low else 15 - j], edge) for j in range(3)])
        for j in range(3):
            value, source = mid_piece(dmid, j, is_low)
            rows = slice(32 * j, 32 * j + 32)
            out[rows] = jnp.where(quarter((32, LANES)) == 3, move(value, source, 3), fine[rows])
            source = j if is_low else 3 - j
            rows = slice(96 + 8 * j, 104 + 8 * j)
            out[rows] = jnp.where(quarter((8, LANES)) == 3, move(dlow[...], source, 3), fine[rows])
        out[120:128] = fine[120:128]
        line = 0 if is_low else 15
        out[128:160] = join_slots([(first[line, 32 * g : 32 * g + 32], edge) for g in range(4)])
    ship("gx", low, high, send_a, send_b)


def fourth_kernel(
    got_a, got_b, first, defect, dmid, dlow, cedge,
    gf, gm, gl, d0, d15, m0, m3, lows, send_a, send_b, tmp, low, high,
):
    left, right = received("gx", got_a, got_b)
    face = cedge[...]
    group = quarter((128, LANES))
    other = [ghost_of(left[128:160], right[128:160], g) for g in range(4)]
    mine = face * jnp.concatenate(other, axis=0)
    theirs = face * edges(first[0], first[15])
    d0[...] = defect[0] + jnp.where(group == 0, mine, 0.0)
    d15[...] = defect[15] + jnp.where(group == 3, mine, 0.0)
    sums = []
    for n, value in enumerate((mine, theirs)):
        tmp[n, 0:128, :] = value
        mid = fourths(tmp.at[n], 32)
        tmp[n + 2, 0:32, :] = mid
        sums.append((mid, fourths(tmp.at[n + 2], 8)))
    group = quarter((32, LANES))
    m0[...] = dmid[0] + jnp.where(group == 0, sums[0][0], 0.0)
    m3[...] = dmid[3] + jnp.where(group == 3, sums[0][0], 0.0)
    lows[...] = dlow[...] + sums[0][1]
    for j in range(3):
        for out, rows, slot, add in (
            (gf, slice(0, 128), j, theirs),
            (gm, slice(32 * j, 32 * j + 32), 3, sums[1][0]),
            (gl, slice(96 + 8 * j, 104 + 8 * j), 3, sums[1][1]),
        ):
            value = ghost_of(left[rows], right[rows], slot)
            out[j] = value + add if j == 0 else value
    tiles = ([], [])
    for lev, r, ghost in (
        (FINE, Parts(FINE, defect, gf, {1: d0, 16: d15}), gf),
        (MID, Parts(MID, dmid, gm, {1: m0, 4: m3}), gm),
        (LOW, Parts(LOW, lows, gl), gl),
    ):
        for side, p in ((0, 8), (1, lev.own)):
            tiles[side].extend(r.get(i, p, 8) for i in range(1, lev.n + 1))
            a, b, c = [r.get(lev.ghost + j, p, 8) for j in range(3)]
            tiles[side].extend([two_in_one(a, b), c])
    pack_y(tiles[0], tiles[1], low, high)
    ship("gy", low, high, send_a, send_b)


def residual_halos(lev, ylo, yhi, at, r, p_low, p_high):
    for side, ref in ((0, ylo), (1, yhi)):
        start = p_low if side == 0 else p_high
        for i in range(lev.n):
            r[side].set(1 + i, start, 8, unpack_y(ref, at + i))
        both = unpack_y(ref, at + lev.n)
        r[side].set(lev.ghost, start, 8, one_of_two(both, 0))
        r[side].set(lev.ghost + 1, start, 8, one_of_two(both, 1))
        r[side].set(lev.ghost + 2, start, 8, unpack_y(ref, at + lev.n + 1))


def early_again_kernel(
    defect, gf, d0, d15, wa, xa, ua, da, za, w, cx, cu, cd, cz, v0, v1, v2, v3
):
    coef = split_views((wa, xa, ua, da, za), (w, cx, cu, cd, cz))
    views = [View(ref, -8) for ref in (v0, v1, v2, v3)]
    early_smooth(Parts(FINE, defect, gf, {1: d0, 16: d15}), views, coef)


def fifth_kernel(
    wf, xf, uf, df, zf, wm, xm, um, dm, zm, wl, xl, ul, dl, zl,
    first, defect, dmid, gf, gm, gl, d0, d15, m0, m3, lows, v0, v1, v2, v3, got_a, got_b, out,
    rs, sa, sb, rm_s, va_m, vb_m, rl_s, va_l, vb_l, tmp, out_s, sems,
):
    ylo, yhi = received("gy", got_a, got_b)
    early_v = [View(ref, -8) for ref in (v0, v1, v2, v3)]
    others = []
    at = 18
    for lev, parts, r_ref, va, vb, refs in (
        (MID, Parts(MID, dmid, gm, {1: m0, 4: m3}), rm_s, va_m, vb_m, (wm, xm, um, dm, zm)),
        (LOW, Parts(LOW, lows, gl), rl_s, va_l, vb_l, (wl, xl, ul, dl, zl)),
    ):
        r = View(r_ref, 0)
        own_rows(lev, r, parts, REACH, 8, lev.own)
        residual_halos(lev, ylo, yhi, at, (r, r), 0, 8 + lev.own)
        at += lev.n + 2
        coef = [View(ref, 0) for ref in refs]
        others.append((lev, r, View(va, 8), View(vb, 8), coef))
    strips = strip_views((wf, xf, uf, df, zf))
    (rl_v,), (rh_v,) = strip_views((rs,))
    parts = Parts(FINE, defect, gf, {1: d0, 16: d15})
    own_rows(FINE, rl_v, parts, REACH, 8, 16)
    own_rows(FINE, rh_v, parts, REACH, 120, 16)
    residual_halos(FINE, ylo, yhi, 0, (rl_v, rh_v), 0, 136)
    *late, vm, vl = late_smooth((rl_v, rh_v), early_v, strip_bufs(sa, sb), strips, others)
    correction(vm, vl, tmp)
    flat = out_s.reshape(2048, LANES)
    copies = []
    for x in range(16):
        pieces = []
        for p, size, v in ((8, 16, late[0]), (24, 96, early_v[3]), (120, 16, late[1])):
            part = v.get(1 + x, p, size) + tmp[x // 4, p : p + size]
            pieces.append(first[x, p - 8 : p - 8 + size] + STEP_WEIGHT * part)
        total = jnp.concatenate(pieces, axis=0).T
        for q in range(4):
            flat[pl.ds(16 * q + x, DEPTH, stride=64), :] = total[DEPTH * q : DEPTH * q + DEPTH]
        if x % 8 == 7:
            for q in range(4):
                rows = pl.ds(16 * q + x - 7, 8)
                copies.append(
                    pltpu.make_async_copy(out_s.at[:, rows], out.at[:, rows], sems.at[len(copies)])
                )
                copies[-1].start()
    for copy in copies:
        copy.wait()


def shape(*dims):
    return jax.ShapeDtypeStruct(dims, jnp.float32)


def scratch(*dims):
    return pltpu.VMEM(dims, jnp.float32)


def swap(a, b, axis):
    out = []
    for start, value in ((0, a), (1, b)):
        pairs = []
        for i in range(start, lax.axis_size(axis) - 1, 2):
            pairs += [(i, i + 1), (i + 1, i)]
        out.append(lax.ppermute(value, axis, pairs) if pairs else jnp.zeros_like(value))
    return out


def on_device(rhs, kappa):
    def call(body, outs, scratches=(), flops=10**6, ins=None, out=None, room=20):
        specs = {} if ins is None else {"in_specs": ins}
        if out is not None:
            specs["out_specs"] = out
        return pl.pallas_call(
            body,
            out_shape=outs,
            **specs,
            scratch_shapes=list(scratches),
            compiler_params=params(room),
            cost_estimate=cost(flops),
        )

    n = FINE.rows
    own = [shape(16, 128, LANES), shape(4, 32, LANES), shape(8, LANES)]
    tmp = scratch(5, 144, LANES)
    outs = [own[0], own[0], own[1], own[1], own[2], own[2]] + [shape(304, LANES)] * 2
    held = scratch(2048, LANES)
    far = pl.BlockSpec(memory_space=pltpu.HBM)
    bufs = [tmp, held, held] + [scratch(304, LANES)] * 2 + [pltpu.SemaphoreType.DMA((8,))]
    kz, rz, km, rm, kl, rl, *sends = call(first_kernel, outs, bufs, ins=[far, far], room=52)(
        rhs.reshape(2048, LANES), kappa.reshape(2048, LANES)
    )
    safe = call(safe_kernel, [shape(16, 112, LANES)] * 5, (), 10**8)(kz)
    kl, *safe = lax.optimization_barrier((kl, *safe))
    gots = swap(*sends, "gx")
    outs = [shape(g, width, LANES) for width in (128, 32, 8) for g in (4, 3)]
    bufs = [scratch(30, 8, LANES)] * 2
    *ghosts, send_a, send_b = call(second_kernel, outs + [shape(30, 8, LANES)] * 2, bufs)(
        *gots, kz, rz, km, rm, kl, rl
    )
    gk, gr = ghosts[:2]
    gots = swap(send_a, send_b, "gy")
    outs = [shape(n, 112, LANES)] * 5 + [shape(n, 128, LANES)] * 4
    early = call(early_kernel, outs, [scratch(n, 128, LANES)], 10**8)(
        kz, rz, gk, gr, *safe
    )
    strip = shape(n, 2, 24, LANES)
    outs = [strip] * 5
    for lev in (MID, LOW):
        outs += [shape(lev.rows, lev.span, LANES)] * 5
    outs += [own[0], own[0], own[1], own[2], shape(128, LANES)] + [shape(160, LANES)] * 2
    strip_scratch = [scratch(n, 2, 48, LANES), scratch(n, 2, 24, LANES)]
    bufs = strip_scratch + [scratch(n, 2, 48, LANES)] * 2
    for lev in (MID, LOW):
        wide = scratch(lev.rows, lev.span + 16, LANES)
        bufs += [wide, scratch(lev.rows, lev.span, LANES), wide]
    bufs += [scratch(n, 160, LANES), tmp] + [scratch(160, LANES)] * 2
    results = call(third_kernel, outs, bufs)(
        kz, rz, km, rm, kl, rl, *ghosts, *gots, *safe, *early
    )
    state = results[:15]
    first, defect, dmid, dlow, cedge, send_a, send_b = results[15:]
    gots = swap(send_a, send_b, "gx")
    outs = [shape(3, width, LANES) for width in (128, 32, 8)]
    outs += [shape(128, LANES)] * 2 + [shape(32, LANES)] * 2 + [shape(8, LANES)]
    bufs = [tmp] + [scratch(14, 8, LANES)] * 2
    *halo, send_a, send_b = call(fourth_kernel, outs + [shape(14, 8, LANES)] * 2, bufs)(
        *gots, first, defect, dmid, dlow, cedge
    )
    gf, gm, gl, d0, d15, m0, m3, lows = halo
    gots = swap(send_a, send_b, "gy")
    inner = call(early_again_kernel, [shape(n, 128, LANES)] * 4, (), 10**8)(
        defect, gf, d0, d15, *safe, *early[:5]
    )
    bufs = [strip_scratch[1]] + [scratch(n, 2, 48, LANES)] * 2
    for lev in (MID, LOW):
        wide = scratch(lev.rows, lev.span + 16, LANES)
        bufs += [scratch(lev.rows, lev.span, LANES), wide, wide]
    bufs += [tmp, scratch(*rhs.shape), pltpu.SemaphoreType.DMA((8,))]
    return call(fifth_kernel, shape(*rhs.shape), bufs, out=far)(
        *state, first, defect, dmid, *halo, *inner, *gots
    )


def solution(mesh):
    return jax.shard_map(
        on_device,
        mesh=mesh,
        in_specs=(P("groups", "gx", "gy"), P("groups", "gx", "gy")),
        out_specs=P("groups", "gx", "gy"),
        check_vma=False,
    )
```

```python
import jax
import jax.numpy as jnp
from jax import lax
from jax.experimental import pallas as pl
from jax.experimental.pallas import tpu as pltpu
from jax.sharding import PartitionSpec as P

JACOBI_WEIGHT = 0.8
STEP_WEIGHT = 0.6
LANES = 128
DEPTH = 32
QUARTERS = 4
REACH = 3


class Level:
    def __init__(self, rows, width, flat, up):
        self.n = rows
        self.own = width
        self.span = width + 16
        self.flat = flat
        self.up = up
        self.rows = rows + 7
        self.ghost = rows + 3

    def work(self, ghosts):
        return list(range(1, self.n + 1)) + list(range(self.ghost, self.ghost + ghosts))

    def faces(self):
        return [i for i in range(self.rows - 1) if i != self.n + 1]


LEVELS = (Level(16, 128, 1.0, 1.0), Level(4, 32, 4.0, 16.0), Level(1, 8, 16.0, 256.0))
FINE, MID, LOW = LEVELS
INNER = [(16, 56), (72, 56)]
SAFE, SAFE_FACES = range(2, 16), range(1, 16)


def grouped(rows, most):
    out = []
    for i in rows:
        if out and len(out[-1]) < most and out[-1][-1] == i - 1:
            out[-1].append(i)
        else:
            out.append([i])
    return out


def near(group, by=0):
    if len(group) == 1:
        return group[0] + by
    return slice(group[0] + by, group[-1] + 1 + by)


def spin(value, shift):
    return pltpu.roll(value, shift, value.ndim - 1)


class View:
    def __init__(self, ref, shift, side=None):
        self.ref, self.shift, self.side = ref, shift, side

    def at(self, i, p, size):
        rows = slice(p + self.shift, p + self.shift + size)
        return (i, rows) if self.side is None else (i, self.side, rows)

    def get(self, i, p, size):
        return self.ref[self.at(i, p, size)]

    def set(self, i, p, size, value):
        self.ref[self.at(i, p, size)] = value


class Split:
    def __init__(self, rows, inside, outside):
        self.rows, self.inside, self.outside = rows, inside, outside

    def get(self, i, p, size):
        return (self.inside if i in self.rows else self.outside).get(i, p, size)

    def set(self, i, p, size, value):
        self.outside.set(i, p, size, value)


def split_views(inside, outside):
    out = []
    for n, (a, b) in enumerate(zip(inside, outside)):
        out.append(Split(SAFE_FACES if n == 1 else SAFE, View(a, -16), View(b, -16)))
    return out


def stage_rows(number):
    return range(2 + number, 16 - number)


def stage_views(inside, outside):
    return [
        Split(stage_rows(n), View(a, -8), View(b, -8))
        for n, (a, b) in enumerate(zip(inside, outside))
    ]


class Parts:
    def __init__(self, lev, own, ghost, swap=None):
        self.lev, self.own, self.ghost, self.swap = lev, own, ghost, swap or {}

    def get(self, i, p, size):
        rows = slice(p - 8, p - 8 + size)
        if i >= self.lev.ghost:
            return self.ghost[i - self.lev.ghost, rows]
        if i in self.swap:
            return self.swap[i][rows]
        return self.own[rows] if self.lev.n == 1 else self.own[i - 1, rows]


def params(mib=20):
    return pltpu.CompilerParams(vmem_limit_bytes=mib << 20)


def cost(flops):
    return pl.CostEstimate(flops=flops, bytes_accessed=8 << 20, transcendentals=0)


def quarter(shape):
    return lax.broadcasted_iota(jnp.int32, shape, 1) // DEPTH


def sublane(shape):
    return lax.broadcasted_iota(jnp.int32, shape, 0)


class Pick:
    def __init__(self, first, second, use_first):
        self.first, self.second, self.use_first = first, second, use_first

    def __getitem__(self, at):
        return jnp.where(self.use_first, self.first[at], self.second[at])


def is_even(axis):
    return lax.axis_index(axis) % 2 == 0


def received(axis, a, b):
    even = is_even(axis)
    return Pick(b, a, even), Pick(a, b, even)


def ship(axis, low, high, a, b):
    even = is_even(axis)
    below, above = low[...], high[...]
    a[...] = jnp.where(even, above, below)
    b[...] = jnp.where(even, below, above)


def move(value, source, target):
    shift = DEPTH * ((target - source) % QUARTERS)
    return pltpu.roll(value, shift, 1) if shift else value


def join_slots(pieces):
    out = None
    for slot, (value, source) in enumerate(pieces):
        part = move(value, source, slot)
        out = part if out is None else jnp.where(quarter(part.shape) == slot, part, out)
    return out


def edges(left, right):
    group = quarter(left.shape)
    return jnp.where(group == 0, left, jnp.where(group == 3, right, 0.0))


def ghost_of(from_left, from_right, slot):
    return edges(move(from_left, slot, 0), move(from_right, slot, 3))


def two_in_one(a, b):
    group = quarter(a.shape)
    up, down = pltpu.roll(b, DEPTH, 1), pltpu.roll(b, LANES - DEPTH, 1)
    return jnp.where(group == 1, up, jnp.where(group == 2, down, a))


def one_of_two(v, second):
    if not second:
        return edges(v, v)
    return edges(pltpu.roll(v, LANES - DEPTH, 1), pltpu.roll(v, DEPTH, 1))


def mid_piece(ref, j, low):
    index = j if low else 15 - j
    return ref[index % 4], index // 4


def fourths(tmp, size):
    out = tmp[pl.ds(0, size, stride=4), :]
    for t in range(1, 4):
        out = out + tmp[pl.ds(t, size, stride=4), :]
    return out


def sum_rows_mid(rows_ref, tmp, out_ref):
    for m in range(4):
        total = rows_ref[4 * m] + rows_ref[4 * m + 1]
        tmp[m, 0:128, :] = total + rows_ref[4 * m + 2] + rows_ref[4 * m + 3]
        out_ref[m] = fourths(tmp.at[m], 32)


def sum_rows_low(mid_ref, tmp):
    tmp[4, 0:32, :] = mid_ref[0] + mid_ref[1] + mid_ref[2] + mid_ref[3]
    return fourths(tmp.at[4], 8)


def fixup(v, lev, p, size, ghost=True):
    group = quarter((size, LANES))
    first, last = v.get(1, p, size), v.get(lev.n, p, size)
    edge = v.get(lev.ghost, p, size) if ghost else jnp.zeros((size, LANES), jnp.float32)
    v.set(0, p, size, jnp.where(group == 0, edge, pltpu.roll(last, DEPTH, 1)))
    v.set(lev.n + 1, p, size, jnp.where(group == 3, edge, pltpu.roll(first, LANES - DEPTH, 1)))
    if ghost:
        v.set(lev.n + 2, p, size, jnp.where(group == 0, first, last))


def harmonic(a, b):
    total = a + b
    return 2.0 * a * b / jnp.where(total > 0, total, 1.0)


def setup(lev, k, coef, parts, most=1, faces=None, work=None):
    w, cx, cu, cd, cz = coef
    for group in grouped(lev.faces() if faces is None else faces, most):
        i, j = near(group), near(group, 1)
        for p, size in parts:
            cx.set(i, p, size, lev.flat * harmonic(k.get(i, p, size), k.get(j, p, size)))
    for group in grouped(lev.work(REACH) if work is None else work, most):
        i = near(group)
        for p, size in parts:
            here = k.get(i, p, size)
            above = lev.flat * harmonic(here, k.get(i, p + 1, size))
            below = lev.flat * harmonic(k.get(i, p - 1, size), here)
            z = lax.broadcasted_iota(jnp.int32, here.shape, here.ndim - 1) % DEPTH
            up = lev.up * harmonic(here, spin(here, LANES - 1))
            up = jnp.where(z == DEPTH - 1, 0.0, up)
            cu.set(i, p, size, above)
            cd.set(i, p, size, below)
            cz.set(i, p, size, up)
            diagonal = cx.get(near(group, -1), p, size) + cx.get(i, p, size) + (below + above)
            diagonal = diagonal + (spin(up, 1) + up)
            good = diagonal > 0
            value = jnp.where(good, JACOBI_WEIGHT / jnp.where(good, diagonal, 1.0), 0.0)
            w.set(i, p, size, value)


def begin(lev, r, v, coef, parts, most=1, rows=None):
    for group in grouped(lev.work(REACH) if rows is None else rows, most):
        i = near(group)
        for p, size in parts:
            v.set(i, p, size, coef[0].get(i, p, size) * r.get(i, p, size))


def sweep(lev, r, v, out, coef, parts, ghosts, most=1, rows=None):
    w, cx, cu, cd, cz = coef
    for group in grouped(lev.work(ghosts) if rows is None else rows, most):
        i, before, after = near(group), near(group, -1), near(group, 1)
        for p, size in parts:
            here = v.get(i, p, size)
            up = cz.get(i, p, size)
            acc = r.get(i, p, size) + cx.get(before, p, size) * v.get(before, p, size)
            acc = acc + cx.get(i, p, size) * v.get(after, p, size)
            acc = acc + cu.get(i, p, size) * v.get(i, p + 1, size)
            acc = acc + cd.get(i, p, size) * v.get(i, p - 1, size)
            acc = acc + up * spin(here, LANES - 1) + spin(up * here, 1)
            out.set(i, p, size, (1.0 - JACOBI_WEIGHT) * here + w.get(i, p, size) * acc)


def clear(v, rows, p):
    for i in range(rows) if isinstance(rows, int) else rows:
        v.set(i, p, 8, jnp.zeros((8, LANES), jnp.float32))


def late_smooth(fine_r, early, bufs, fine_coef, others):
    jobs = []
    for side, start in ((0, 0), (1, 120)):
        for v in bufs[side]:
            clear(v, FINE.rows, -8 if side == 0 else 144)
        jobs.append((FINE, fine_r[side], list(bufs[side]), fine_coef[side], start, 24, 3, side))
    for lev, r, va, vb, coef in others:
        for v in (va, vb):
            clear(v, lev.rows, -8)
            clear(v, lev.rows, lev.span)
        jobs.append((lev, r, [va, vb], coef, 0, lev.span, 1 if lev is MID else 3, None))
    for lev, r, pair, coef, start, size, most, side in jobs:
        begin(lev, r, pair[0], coef, [(start, size)], most)
    for number in range(3):
        for lev, r, pair, coef, start, size, most, side in jobs:
            if side is not None:
                tile = BEYOND[side]
                for i in lev.work(REACH - number):
                    pair[0].set(i, tile, 8, early[number].get(i, tile, 8))
            fixup(pair[0], lev, start, size)
        for lev, r, pair, coef, start, size, most, side in jobs:
            sweep(lev, r, pair[0], pair[1], coef, [(start, size)], REACH - 1 - number, most)
            pair.reverse()
    return [job[2][0] for job in jobs]


def early_smooth(r, views, coef, safe):
    stages = []
    for number in range(4):
        inside = stage_rows(number)
        every = FINE.work(REACH - number)
        stages.append([i for i in every if (i in inside) == safe])
    for n, v in enumerate(views[:3]):
        for p in (8, 128):
            clear(v, stage_rows(n) if safe else FINE.rows, p)
    begin(FINE, r, views[0], coef, INNER, 1, stages[0])
    for n in range(3):
        if not safe:
            fixup(views[n], FINE, 16, 112)
        sweep(FINE, r, views[n], views[n + 1], coef, INNER, 0, 1, stages[n + 1])


BEYOND = (24, 112)


def expand(view, row, lev, tmp):
    part = view.get(row, 6, lev.span // 4)
    for t in range(4):
        tmp[pl.ds(t, lev.span // 4, stride=4), :] = part


def correction(vm, vl, tmp):
    expand(vl, 1, MID, tmp.at[4])
    for m in range(4):
        value = vm.get(1 + m, 0, MID.span) + tmp[4, 0 : MID.span]
        vm.set(1 + m, 0, MID.span, value)
        expand(vm, 1 + m, FINE, tmp.at[m])


def pack_y(tiles_low, tiles_high, low, high):
    for n in range((len(tiles_low) + 1) // 2):
        for tiles, out, is_low in ((tiles_low, low, True), (tiles_high, high, False)):
            a = tiles[2 * n]
            if 2 * n + 1 < len(tiles):
                b = pltpu.roll(tiles[2 * n + 1], 4, 0)
                first = sublane((8, LANES)) < 4
                a = jnp.where(first, a, b) if is_low else jnp.where(first, b, a)
            out[n] = a


def unpack_y(ref, n):
    value = ref[n // 2]
    return pltpu.roll(value, 4, 0) if n % 2 else value


def first_kernel(
    rhs, kappa, kz, rz, km, rm, kl, rl, send_a, send_b, tmp, k_in, r_in, low, high, sems
):
    copies = []
    for n, (source, target) in enumerate(((kappa, k_in), (rhs, r_in))):
        for c in range(4):
            rows = slice(512 * c, 512 * c + 512)
            copy = pltpu.make_async_copy(source.at[rows], target.at[rows], sems.at[4 * n + c])
            copies.append(copy)
    for copy in copies[:4]:
        copy.start()
    for n, (source, target, mid, low_level) in enumerate(((k_in, kz, km, kl), (r_in, rz, rm, rl))):
        for c, copy in enumerate(copies[4 * n : 4 * n + 4]):
            copy.wait()
            if n == 0:
                copies[4 + c].start()
        for x in range(16):
            rows = [source[pl.ds(16 * q + x, DEPTH, stride=64), :] for q in range(4)]
            target[x] = jnp.concatenate(rows, axis=0).T
        sum_rows_mid(target, tmp, mid)
        if n == 0:
            for m in range(4):
                mid[m] = mid[m] * (1.0 / 16.0)
            low_level[...] = sum_rows_low(mid, tmp) * (1.0 / 16.0)
        else:
            low_level[...] = sum_rows_low(mid, tmp)
        for out, is_low in ((low, True), (high, False)):
            edge = 0 if is_low else 3
            line = [j if is_low else 15 - j for j in range(4)]
            if n == 0:
                out[0:128] = join_slots([(kz[j], edge) for j in line])
                out[288:296] = kl[...]
                continue
            fine = join_slots([(rz[j], edge) for j in line[:3]])
            for j in range(4):
                value, source_q = mid_piece(km, j, is_low)
                out[128 + 32 * j : 160 + 32 * j] = jnp.where(
                    quarter((32, LANES)) == 3, move(value, source_q, 3), fine[32 * j : 32 * j + 32]
                )
            out[256:288] = join_slots([mid_piece(rm, j, is_low) for j in range(3)])
            out[296:304] = rl[...]
    ship("gx", low, high, send_a, send_b)


def second_kernel(
    got_a, got_b, kz, rz, km, rm, kl, rl, gk, gr, gkm, grm, gkl, grl, send_a, send_b, low, high
):
    left, right = received("gx", got_a, got_b)
    for j in range(4):
        gk[j] = ghost_of(left[0:128], right[0:128], j)
        rows = slice(128 + 32 * j, 160 + 32 * j)
        gkm[j] = ghost_of(left[rows], right[rows], 3)
        gkl[j] = edges(move(left[288:296], 3 - j, 0), move(right[288:296], j, 3))
    for j in range(3):
        gr[j] = ghost_of(left[128:256], right[128:256], j)
        grm[j] = ghost_of(left[256:288], right[256:288], j)
        grl[j] = edges(move(left[296:304], 3 - j, 0), move(right[296:304], j, 3))
    at = 0
    extra = 0
    row = sublane((8, LANES))
    for lev, k, r, ghost_k, ghost_r in (
        (FINE, kz, rz, gk, gr), (MID, km, rm, gkm, grm), (LOW, kl, rl, gkl, grl),
    ):
        for is_low, out in ((True, low), (False, high)):
            rows = slice(0, 8) if is_low else slice(lev.own - 8, lev.own)
            pairs = []
            for i in range(lev.n):
                pairs.append((k[rows], r[rows]) if lev.n == 1 else (k[i, rows], r[i, rows]))
            for a in (0, 2):
                rest = ghost_r[a, rows]
                rest = two_in_one(rest, ghost_r[a + 1, rows]) if a == 0 else rest
                pairs.append((two_in_one(ghost_k[a, rows], ghost_k[a + 1, rows]), rest))
            for i, (a, b) in enumerate(pairs):
                if is_low:
                    out[at + i] = jnp.where(row < 5, a, pltpu.roll(b, 5, 0))
                else:
                    out[at + i] = jnp.where(row >= 3, a, pltpu.roll(b, 3, 0))
            for i in range(lev.n):
                e = extra + i
                cell = slice(3, 4) if is_low else slice(lev.own - 4, lev.own - 3)
                out[27 + e // 8, e % 8 : e % 8 + 1] = r[cell] if lev.n == 1 else r[i, cell]
        at += lev.n + 2
        extra += lev.n
    ship("gy", low, high, send_a, send_b)


def halos(lev, ylo, yhi, at, extra, k, r, p_low, p_high):
    row = sublane((8, LANES))
    for side, ref in ((0, ylo), (1, yhi)):
        start = p_low if side == 0 else p_high
        for i in range(lev.n + 2):
            value = ref[at + i]
            if side == 0:
                a = jnp.where(row >= 3, value, 0.0)
                b = jnp.where(row >= 5, pltpu.roll(value, 5, 0), 0.0)
            else:
                a = jnp.where(row < 5, value, 0.0)
                b = jnp.where(row < 3, pltpu.roll(value, 3, 0), 0.0)
            if i < lev.n:
                k[side].set(1 + i, start, 8, a)
                r[side].set(1 + i, start, 8, b)
                e = extra + i
                cell = start + 4 if side == 0 else start + 3
                r[side].set(1 + i, cell, 1, ref[27 + e // 8, e % 8 : e % 8 + 1])
                continue
            for part in (0, 1):
                j = 2 * (i - lev.n) + part
                k[side].set(lev.ghost + j, start, 8, one_of_two(a, part))
                if j < REACH:
                    r[side].set(lev.ghost + j, start, 8, one_of_two(b, part))


def own_rows(lev, dst, src, ghosts, p, size):
    for i in lev.work(ghosts):
        dst.set(i, p, size, src.get(i, p, size))


def safe_kernel(kz, rz, w, cx, cu, cd, cz, v0, v1, v2, v3):
    coef = [View(ref, -16) for ref in (w, cx, cu, cd, cz)]
    setup(FINE, Parts(FINE, kz, None), coef, INNER, 1, SAFE_FACES, SAFE)
    early_smooth(Parts(FINE, rz, None), [View(ref, -8) for ref in (v0, v1, v2, v3)], coef, True)


def safe_again_kernel(defect, w, cx, cu, cd, cz, v0, v1, v2, v3):
    coef = [View(ref, -16) for ref in (w, cx, cu, cd, cz)]
    views = [View(ref, -8) for ref in (v0, v1, v2, v3)]
    early_smooth(Parts(FINE, defect, None), views, coef, True)


def early_kernel(
    kz, rz, gk, gr, wa, xa, ua, da, za, b0, b1, b2, b3,
    w, cx, cu, cd, cz, v0, v1, v2, v3, k_s,
):
    k = View(k_s, -8)
    own = Parts(FINE, kz, gk)
    edge = [i for i in FINE.work(4) if i not in SAFE]
    for i in edge:
        k.set(i, 8, 128, own.get(i, 8, 128))
    fixup(k, FINE, 8, 128)
    coef = split_views((wa, xa, ua, da, za), (w, cx, cu, cd, cz))
    faces = [i for i in FINE.faces() if i not in SAFE_FACES]
    setup(FINE, k, coef, INNER, 1, faces, [i for i in edge if i < FINE.ghost + REACH])
    views = stage_views((b0, b1, b2, b3), (v0, v1, v2, v3))
    early_smooth(Parts(FINE, rz, gr), views, coef, False)


def strip_views(refs):
    return [[View(ref, -120 * side, side) for ref in refs] for side in (0, 1)]


def strip_bufs(*refs):
    return [[View(ref, 8 - 112 * side, side) for ref in refs] for side in (0, 1)]


def third_kernel(
    kz, rz, km, rm, kl, rl, gk, gr, gkm, grm, gkl, grl, got_a, got_b,
    wa, xa, ua, da, za, b0, b1, b2, b3, w, cx, cu, cd, cz, v0, v1, v2, v3,
    wf, xf, uf, df, zf, wm, xm, um, dm, zm, wl, xl, ul, dl, zl,
    first, defect, dmid, dlow, cedge, send_a, send_b,
    ks, rs, sa, sb, km_s, rm_s, vm_s, kl_s, rl_s, vl_s, full, tmp, low, high,
):
    ylo, yhi = received("gy", got_a, got_b)
    early = split_views((wa, xa, ua, da, za), (w, cx, cu, cd, cz))
    early_v = stage_views((b0, b1, b2, b3), (v0, v1, v2, v3))
    others = []
    at, extra = 18, 16
    for lev, own_k, ghost_k, k_ref, own_r, ghost_r, r_ref, v_ref, refs in (
        (MID, km, gkm, km_s, rm, grm, rm_s, vm_s, (wm, xm, um, dm, zm)),
        (LOW, kl, gkl, kl_s, rl, grl, rl_s, vl_s, (wl, xl, ul, dl, zl)),
    ):
        k, r = View(k_ref, 8), View(r_ref, 0)
        own_rows(lev, k, Parts(lev, own_k, ghost_k), 4, 8, lev.own)
        own_rows(lev, r, Parts(lev, own_r, ghost_r), REACH, 8, lev.own)
        halos(lev, ylo, yhi, at, extra, (k, k), (r, r), 0, 8 + lev.own)
        at, extra = at + lev.n + 2, extra + lev.n
        clear(k, lev.rows, -8)
        clear(k, lev.rows, lev.span)
        fixup(k, lev, 0, lev.span)
        coef = [View(ref, 0) for ref in refs]
        setup(lev, k, coef, [(0, lev.span)], 1 if lev is MID else 3)
        others.append((lev, r, View(v_ref, 8), k, coef))
    strips = strip_views((wf, xf, uf, df, zf))
    (kl_v,), (kh_v,) = strip_bufs(ks)
    (rl_v,), (rh_v,) = strip_views((rs,))
    halos(FINE, ylo, yhi, 0, 0, (kl_v, kh_v), (rl_v, rh_v), 0, 136)
    for k, r, p_k, p_r, start, pad, kept in (
        (kl_v, rl_v, 8, 8, 0, -8, 16), (kh_v, rh_v, 120, 120, 128, 144, 120),
    ):
        side = 0 if start == 0 else 1
        own_rows(FINE, k, Parts(FINE, kz, gk), 4, p_k, 16)
        own_rows(FINE, r, Parts(FINE, rz, gr), REACH, p_r, 16)
        clear(k, FINE.rows, pad)
        fixup(k, FINE, start if side == 0 else 120, 24)
        setup(FINE, k, strips[side], [(start, 16)], 4)
        for number, (dst, src) in enumerate(zip(strips[side], early)):
            rows = FINE.work(REACH) + ([0, FINE.n + 2] if number == 1 else [])
            for i in rows:
                dst.set(i, kept, 8, src.get(i, kept, 8))
    *late, vm, vl = late_smooth((rl_v, rh_v), early_v, strip_bufs(sa, sb), strips, others)
    correction(vm, vl, tmp)
    whole = View(full, 8)
    for i in range(1, 17):
        m = (i - 1) // 4
        for p, size, v in ((0, 24, late[0]), (24, 48, early_v[3]), (72, 48, early_v[3]), (120, 24, late[1])):
            whole.set(i, p, size, STEP_WEIGHT * (v.get(i, p, size) + tmp[m, p : p + size]))
    fixup(whole, FINE, 8, 128, ghost=False)
    for most, p, size, coef in (
        (8, 8, 8, strips[0]), (1, 16, 56, early), (1, 72, 56, early), (8, 128, 8, strips[1]),
    ):
        for group in grouped(range(1, 17), most):
            i, before, after = near(group), near(group, -1), near(group, 1)
            _, x, u, d, z = [c.get(i, p, size) for c in coef]
            v = whole.get(i, p, size)
            flux = z * (v - spin(v, LANES - 1))
            image = coef[1].get(before, p, size) * (v - whole.get(before, p, size))
            image = image + x * (v - whole.get(after, p, size))
            image = image + u * (v - whole.get(i, p + 1, size))
            image = image + d * (v - whole.get(i, p - 1, size))
            image = image + (flux - spin(flux, 1))
            defect[before, p - 8 : p - 8 + size] = rz[before, p - 8 : p - 8 + size] - image
            first[before, p - 8 : p - 8 + size] = v
    for p, size, coef in ((8, 8, strips[0]), (16, 112, early), (128, 8, strips[1])):
        cedge[p - 8 : p - 8 + size] = edges(coef[1].get(0, p, size), coef[1].get(16, p, size))
    sum_rows_mid(defect, tmp, dmid)
    dlow[...] = sum_rows_low(dmid, tmp)
    for out, is_low in ((low, True), (high, False)):
        edge = 0 if is_low else 3
        fine = join_slots([(defect[j if is_low else 15 - j], edge) for j in range(3)])
        for j in range(3):
            value, source = mid_piece(dmid, j, is_low)
            rows = slice(32 * j, 32 * j + 32)
            out[rows] = jnp.where(quarter((32, LANES)) == 3, move(value, source, 3), fine[rows])
            source = j if is_low else 3 - j
            rows = slice(96 + 8 * j, 104 + 8 * j)
            out[rows] = jnp.where(quarter((8, LANES)) == 3, move(dlow[...], source, 3), fine[rows])
        out[120:128] = fine[120:128]
        line = 0 if is_low else 15
        out[128:160] = join_slots([(first[line, 32 * g : 32 * g + 32], edge) for g in range(4)])
    ship("gx", low, high, send_a, send_b)


def fourth_kernel(
    got_a, got_b, first, defect, dmid, dlow, cedge,
    gf, gm, gl, d0, d15, m0, m3, lows, send_a, send_b, tmp, low, high,
):
    left, right = received("gx", got_a, got_b)
    face = cedge[...]
    group = quarter((128, LANES))
    other = [ghost_of(left[128:160], right[128:160], g) for g in range(4)]
    mine = face * jnp.concatenate(other, axis=0)
    theirs = face * edges(first[0], first[15])
    d0[...] = defect[0] + jnp.where(group == 0, mine, 0.0)
    d15[...] = defect[15] + jnp.where(group == 3, mine, 0.0)
    sums = []
    for n, value in enumerate((mine, theirs)):
        tmp[n, 0:128, :] = value
        mid = fourths(tmp.at[n], 32)
        tmp[n + 2, 0:32, :] = mid
        sums.append((mid, fourths(tmp.at[n + 2], 8)))
    group = quarter((32, LANES))
    m0[...] = dmid[0] + jnp.where(group == 0, sums[0][0], 0.0)
    m3[...] = dmid[3] + jnp.where(group == 3, sums[0][0], 0.0)
    lows[...] = dlow[...] + sums[0][1]
    for j in range(3):
        for out, rows, slot, add in (
            (gf, slice(0, 128), j, theirs),
            (gm, slice(32 * j, 32 * j + 32), 3, sums[1][0]),
            (gl, slice(96 + 8 * j, 104 + 8 * j), 3, sums[1][1]),
        ):
            value = ghost_of(left[rows], right[rows], slot)
            out[j] = value + add if j == 0 else value
    tiles = ([], [])
    for lev, r, ghost in (
        (FINE, Parts(FINE, defect, gf, {1: d0, 16: d15}), gf),
        (MID, Parts(MID, dmid, gm, {1: m0, 4: m3}), gm),
        (LOW, Parts(LOW, lows, gl), gl),
    ):
        for side, p in ((0, 8), (1, lev.own)):
            tiles[side].extend(r.get(i, p, 8) for i in range(1, lev.n + 1))
            a, b, c = [r.get(lev.ghost + j, p, 8) for j in range(3)]
            tiles[side].extend([two_in_one(a, b), c])
    pack_y(tiles[0], tiles[1], low, high)
    ship("gy", low, high, send_a, send_b)


def residual_halos(lev, ylo, yhi, at, r, p_low, p_high):
    for side, ref in ((0, ylo), (1, yhi)):
        start = p_low if side == 0 else p_high
        for i in range(lev.n):
            r[side].set(1 + i, start, 8, unpack_y(ref, at + i))
        both = unpack_y(ref, at + lev.n)
        r[side].set(lev.ghost, start, 8, one_of_two(both, 0))
        r[side].set(lev.ghost + 1, start, 8, one_of_two(both, 1))
        r[side].set(lev.ghost + 2, start, 8, unpack_y(ref, at + lev.n + 1))


def early_again_kernel(
    defect, gf, d0, d15, wa, xa, ua, da, za, w, cx, cu, cd, cz, b0, b1, b2, b3, v0, v1, v2, v3
):
    coef = split_views((wa, xa, ua, da, za), (w, cx, cu, cd, cz))
    views = stage_views((b0, b1, b2, b3), (v0, v1, v2, v3))
    early_smooth(Parts(FINE, defect, gf, {1: d0, 16: d15}), views, coef, False)


def fifth_kernel(
    wf, xf, uf, df, zf, wm, xm, um, dm, zm, wl, xl, ul, dl, zl,
    first, defect, dmid, gf, gm, gl, d0, d15, m0, m3, lows,
    b0, b1, b2, b3, v0, v1, v2, v3, got_a, got_b, out,
    rs, sa, sb, rm_s, va_m, vb_m, rl_s, va_l, vb_l, tmp, out_s, sems,
):
    ylo, yhi = received("gy", got_a, got_b)
    early_v = stage_views((b0, b1, b2, b3), (v0, v1, v2, v3))
    others = []
    at = 18
    for lev, parts, r_ref, va, vb, refs in (
        (MID, Parts(MID, dmid, gm, {1: m0, 4: m3}), rm_s, va_m, vb_m, (wm, xm, um, dm, zm)),
        (LOW, Parts(LOW, lows, gl), rl_s, va_l, vb_l, (wl, xl, ul, dl, zl)),
    ):
        r = View(r_ref, 0)
        own_rows(lev, r, parts, REACH, 8, lev.own)
        residual_halos(lev, ylo, yhi, at, (r, r), 0, 8 + lev.own)
        at += lev.n + 2
        coef = [View(ref, 0) for ref in refs]
        others.append((lev, r, View(va, 8), View(vb, 8), coef))
    strips = strip_views((wf, xf, uf, df, zf))
    (rl_v,), (rh_v,) = strip_views((rs,))
    parts = Parts(FINE, defect, gf, {1: d0, 16: d15})
    own_rows(FINE, rl_v, parts, REACH, 8, 16)
    own_rows(FINE, rh_v, parts, REACH, 120, 16)
    residual_halos(FINE, ylo, yhi, 0, (rl_v, rh_v), 0, 136)
    *late, vm, vl = late_smooth((rl_v, rh_v), early_v, strip_bufs(sa, sb), strips, others)
    correction(vm, vl, tmp)
    flat = out_s.reshape(2048, LANES)
    copies = []
    for x in range(16):
        pieces = []
        for p, size, v in ((8, 16, late[0]), (24, 96, early_v[3]), (120, 16, late[1])):
            part = v.get(1 + x, p, size) + tmp[x // 4, p : p + size]
            pieces.append(first[x, p - 8 : p - 8 + size] + STEP_WEIGHT * part)
        total = jnp.concatenate(pieces, axis=0).T
        for q in range(4):
            flat[pl.ds(16 * q + x, DEPTH, stride=64), :] = total[DEPTH * q : DEPTH * q + DEPTH]
        if x % 8 == 7:
            for q in range(4):
                rows = pl.ds(16 * q + x - 7, 8)
                copies.append(
                    pltpu.make_async_copy(out_s.at[:, rows], out.at[:, rows], sems.at[len(copies)])
                )
                copies[-1].start()
    for copy in copies:
        copy.wait()


def shape(*dims):
    return jax.ShapeDtypeStruct(dims, jnp.float32)


def scratch(*dims):
    return pltpu.VMEM(dims, jnp.float32)


def swap(a, b, axis):
    out = []
    for start, value in ((0, a), (1, b)):
        pairs = []
        for i in range(start, lax.axis_size(axis) - 1, 2):
            pairs += [(i, i + 1), (i + 1, i)]
        out.append(lax.ppermute(value, axis, pairs) if pairs else jnp.zeros_like(value))
    return out


def on_device(rhs, kappa):
    def call(body, outs, scratches=(), flops=10**6, ins=None, out=None, room=20):
        specs = {} if ins is None else {"in_specs": ins}
        if out is not None:
            specs["out_specs"] = out
        return pl.pallas_call(
            body,
            out_shape=outs,
            **specs,
            scratch_shapes=list(scratches),
            compiler_params=params(room),
            cost_estimate=cost(flops),
        )

    n = FINE.rows
    own = [shape(16, 128, LANES), shape(4, 32, LANES), shape(8, LANES)]
    tmp = scratch(5, 144, LANES)
    outs = [own[0], own[0], own[1], own[1], own[2], own[2]] + [shape(304, LANES)] * 2
    held = scratch(2048, LANES)
    far = pl.BlockSpec(memory_space=pltpu.HBM)
    bufs = [tmp, held, held] + [scratch(304, LANES)] * 2 + [pltpu.SemaphoreType.DMA((8,))]
    kz, rz, km, rm, kl, rl, *sends = call(first_kernel, outs, bufs, ins=[far, far], room=51)(
        rhs.reshape(2048, LANES), kappa.reshape(2048, LANES)
    )
    inside = [shape(16, 128, LANES)] * 4
    outs = [shape(16, 112, LANES)] * 5 + inside
    safe = call(safe_kernel, outs, (), 10**8)(kz, rz)
    kl, *safe = lax.optimization_barrier((kl, *safe))
    gots = swap(*sends, "gx")
    outs = [shape(g, width, LANES) for width in (128, 32, 8) for g in (4, 3)]
    bufs = [scratch(30, 8, LANES)] * 2
    *ghosts, send_a, send_b = call(second_kernel, outs + [shape(30, 8, LANES)] * 2, bufs)(
        *gots, kz, rz, km, rm, kl, rl
    )
    gk, gr = ghosts[:2]
    gots = swap(send_a, send_b, "gy")
    outs = [shape(n, 112, LANES)] * 5 + [shape(n, 128, LANES)] * 4
    early = call(early_kernel, outs, [scratch(n, 128, LANES)], 10**8)(
        kz, rz, gk, gr, *safe
    )
    strip = shape(n, 2, 24, LANES)
    outs = [strip] * 5
    for lev in (MID, LOW):
        outs += [shape(lev.rows, lev.span, LANES)] * 5
    outs += [own[0], own[0], own[1], own[2], shape(128, LANES)] + [shape(160, LANES)] * 2
    strip_scratch = [scratch(n, 2, 48, LANES), scratch(n, 2, 24, LANES)]
    bufs = strip_scratch + [scratch(n, 2, 48, LANES)] * 2
    for lev in (MID, LOW):
        wide = scratch(lev.rows, lev.span + 16, LANES)
        bufs += [wide, scratch(lev.rows, lev.span, LANES), wide]
    bufs += [scratch(n, 160, LANES), tmp] + [scratch(160, LANES)] * 2
    results = call(third_kernel, outs, bufs)(
        kz, rz, km, rm, kl, rl, *ghosts, *gots, *safe, *early
    )
    state = results[:15]
    first, defect, dmid, dlow, cedge, send_a, send_b = results[15:]
    gots = swap(send_a, send_b, "gx")
    again = call(safe_again_kernel, inside, (), 10**8)(defect, *safe[:5])
    dlow, *again = lax.optimization_barrier((dlow, *again))
    outs = [shape(3, width, LANES) for width in (128, 32, 8)]
    outs += [shape(128, LANES)] * 2 + [shape(32, LANES)] * 2 + [shape(8, LANES)]
    bufs = [tmp] + [scratch(14, 8, LANES)] * 2
    *halo, send_a, send_b = call(fourth_kernel, outs + [shape(14, 8, LANES)] * 2, bufs)(
        *gots, first, defect, dmid, dlow, cedge
    )
    gf, gm, gl, d0, d15, m0, m3, lows = halo
    gots = swap(send_a, send_b, "gy")
    inner = call(early_again_kernel, [shape(n, 128, LANES)] * 4, (), 10**8)(
        defect, gf, d0, d15, *safe[:5], *early[:5], *again
    )
    bufs = [strip_scratch[1]] + [scratch(n, 2, 48, LANES)] * 2
    for lev in (MID, LOW):
        wide = scratch(lev.rows, lev.span + 16, LANES)
        bufs += [scratch(lev.rows, lev.span, LANES), wide, wide]
    bufs += [tmp, scratch(*rhs.shape), pltpu.SemaphoreType.DMA((8,))]
    return call(fifth_kernel, shape(*rhs.shape), bufs, out=far)(
        *state, first, defect, dmid, *halo, *again, *inner, *gots
    )


def solution(mesh):
    return jax.shard_map(
        on_device,
        mesh=mesh,
        in_specs=(P("groups", "gx", "gy"), P("groups", "gx", "gy")),
        out_specs=P("groups", "gx", "gy"),
        check_vma=False,
    )
```

```python
import jax
import jax.numpy as jnp
from jax import lax
from jax.experimental import pallas as pl
from jax.experimental.pallas import tpu as pltpu
from jax.sharding import PartitionSpec as P

JACOBI_WEIGHT = 0.8
STEP_WEIGHT = 0.6
LANES = 128
DEPTH = 32
QUARTERS = 4
REACH = 3


class Level:
    def __init__(self, rows, width, flat, up):
        self.n = rows
        self.own = width
        self.span = width + 16
        self.flat = flat
        self.up = up
        self.rows = rows + 7
        self.ghost = rows + 3

    def work(self, ghosts):
        return list(range(1, self.n + 1)) + list(range(self.ghost, self.ghost + ghosts))

    def faces(self):
        return [i for i in range(self.rows - 1) if i != self.n + 1]


LEVELS = (Level(16, 128, 1.0, 1.0), Level(4, 32, 4.0, 16.0), Level(1, 8, 16.0, 256.0))
FINE, MID, LOW = LEVELS
INNER = [(16, 56), (72, 56)]
SAFE, SAFE_FACES = range(2, 16), range(1, 16)


def grouped(rows, most):
    out = []
    for i in rows:
        if out and len(out[-1]) < most and out[-1][-1] == i - 1:
            out[-1].append(i)
        else:
            out.append([i])
    return out


def near(group, by=0):
    if len(group) == 1:
        return group[0] + by
    return slice(group[0] + by, group[-1] + 1 + by)


def spin(value, shift):
    return pltpu.roll(value, shift, value.ndim - 1)


class View:
    def __init__(self, ref, shift, side=None):
        self.ref, self.shift, self.side = ref, shift, side

    def at(self, i, p, size):
        rows = slice(p + self.shift, p + self.shift + size)
        return (i, rows) if self.side is None else (i, self.side, rows)

    def get(self, i, p, size):
        return self.ref[self.at(i, p, size)]

    def set(self, i, p, size, value):
        self.ref[self.at(i, p, size)] = value


class Split:
    def __init__(self, rows, inside, outside):
        self.rows, self.inside, self.outside = rows, inside, outside

    def get(self, i, p, size):
        return (self.inside if i in self.rows else self.outside).get(i, p, size)

    def set(self, i, p, size, value):
        self.outside.set(i, p, size, value)


def split_views(inside, outside):
    out = []
    for n, (a, b) in enumerate(zip(inside, outside)):
        out.append(Split(SAFE_FACES if n == 1 else SAFE, View(a, -16), View(b, -16)))
    return out


def stage_rows(number):
    return range(2 + number, 16 - number)


def stage_views(inside, outside):
    return [
        Split(stage_rows(n), View(a, -8), View(b, -8))
        for n, (a, b) in enumerate(zip(inside, outside))
    ]


class Parts:
    def __init__(self, lev, own, ghost, swap=None):
        self.lev, self.own, self.ghost, self.swap = lev, own, ghost, swap or {}

    def get(self, i, p, size):
        rows = slice(p - 8, p - 8 + size)
        if i >= self.lev.ghost:
            return self.ghost[i - self.lev.ghost, rows]
        if i in self.swap:
            return self.swap[i][rows]
        return self.own[rows] if self.lev.n == 1 else self.own[i - 1, rows]


def params(mib=20):
    return pltpu.CompilerParams(vmem_limit_bytes=mib << 20)


def cost(flops):
    return pl.CostEstimate(flops=flops, bytes_accessed=8 << 20, transcendentals=0)


def quarter(shape):
    return lax.broadcasted_iota(jnp.int32, shape, 1) // DEPTH


def sublane(shape):
    return lax.broadcasted_iota(jnp.int32, shape, 0)


class Pick:
    def __init__(self, first, second, use_first):
        self.first, self.second, self.use_first = first, second, use_first

    def __getitem__(self, at):
        return jnp.where(self.use_first, self.first[at], self.second[at])


def is_even(axis):
    return lax.axis_index(axis) % 2 == 0


def received(axis, a, b):
    even = is_even(axis)
    return Pick(b, a, even), Pick(a, b, even)


def ship(axis, low, high, a, b):
    even = is_even(axis)
    below, above = low[...], high[...]
    a[...] = jnp.where(even, above, below)
    b[...] = jnp.where(even, below, above)


def move(value, source, target):
    shift = DEPTH * ((target - source) % QUARTERS)
    return pltpu.roll(value, shift, 1) if shift else value


def join_slots(pieces):
    out = None
    for slot, (value, source) in enumerate(pieces):
        part = move(value, source, slot)
        out = part if out is None else jnp.where(quarter(part.shape) == slot, part, out)
    return out


def edges(left, right):
    group = quarter(left.shape)
    return jnp.where(group == 0, left, jnp.where(group == 3, right, 0.0))


def ghost_of(from_left, from_right, slot):
    return edges(move(from_left, slot, 0), move(from_right, slot, 3))


def two_in_one(a, b):
    group = quarter(a.shape)
    up, down = pltpu.roll(b, DEPTH, 1), pltpu.roll(b, LANES - DEPTH, 1)
    return jnp.where(group == 1, up, jnp.where(group == 2, down, a))


def one_of_two(v, second):
    if not second:
        return edges(v, v)
    return edges(pltpu.roll(v, LANES - DEPTH, 1), pltpu.roll(v, DEPTH, 1))


def mid_piece(ref, j, low):
    index = j if low else 15 - j
    return ref[index % 4], index // 4


def fourths(tmp, size):
    out = tmp[pl.ds(0, size, stride=4), :]
    for t in range(1, 4):
        out = out + tmp[pl.ds(t, size, stride=4), :]
    return out


def sum_rows_mid(rows_ref, tmp, out_ref):
    for m in range(4):
        total = rows_ref[4 * m] + rows_ref[4 * m + 1]
        tmp[m, 0:128, :] = total + rows_ref[4 * m + 2] + rows_ref[4 * m + 3]
        out_ref[m] = fourths(tmp.at[m], 32)


def sum_rows_low(mid_ref, tmp):
    tmp[4, 0:32, :] = mid_ref[0] + mid_ref[1] + mid_ref[2] + mid_ref[3]
    return fourths(tmp.at[4], 8)


def fixup(v, lev, p, size, ghost=True):
    group = quarter((size, LANES))
    first, last = v.get(1, p, size), v.get(lev.n, p, size)
    edge = v.get(lev.ghost, p, size) if ghost else jnp.zeros((size, LANES), jnp.float32)
    v.set(0, p, size, jnp.where(group == 0, edge, pltpu.roll(last, DEPTH, 1)))
    v.set(lev.n + 1, p, size, jnp.where(group == 3, edge, pltpu.roll(first, LANES - DEPTH, 1)))
    if ghost:
        v.set(lev.n + 2, p, size, jnp.where(group == 0, first, last))


def harmonic(a, b):
    total = a + b
    return 2.0 * a * b / jnp.where(total > 0, total, 1.0)


def setup(lev, k, coef, parts, most=1, faces=None, work=None):
    w, cx, cu, cd, cz = coef
    for group in grouped(lev.faces() if faces is None else faces, most):
        i, j = near(group), near(group, 1)
        for p, size in parts:
            cx.set(i, p, size, lev.flat * harmonic(k.get(i, p, size), k.get(j, p, size)))
    for group in grouped(lev.work(REACH) if work is None else work, most):
        i = near(group)
        for p, size in parts:
            here = k.get(i, p, size)
            above = lev.flat * harmonic(here, k.get(i, p + 1, size))
            below = lev.flat * harmonic(k.get(i, p - 1, size), here)
            z = lax.broadcasted_iota(jnp.int32, here.shape, here.ndim - 1) % DEPTH
            up = lev.up * harmonic(here, spin(here, LANES - 1))
            up = jnp.where(z == DEPTH - 1, 0.0, up)
            cu.set(i, p, size, above)
            cd.set(i, p, size, below)
            cz.set(i, p, size, up)
    for group in grouped(lev.work(REACH) if work is None else work, most):
        i = near(group)
        for p, size in parts:
            up = cz.get(i, p, size)
            diagonal = cx.get(near(group, -1), p, size) + cx.get(i, p, size)
            diagonal = diagonal + (cd.get(i, p, size) + cu.get(i, p, size)) + (spin(up, 1) + up)
            good = diagonal > 0
            value = jnp.where(good, JACOBI_WEIGHT / jnp.where(good, diagonal, 1.0), 0.0)
            w.set(i, p, size, value)


def begin(lev, r, v, coef, parts, most=1, rows=None):
    for group in grouped(lev.work(REACH) if rows is None else rows, most):
        i = near(group)
        for p, size in parts:
            v.set(i, p, size, coef[0].get(i, p, size) * r.get(i, p, size))


def sweep(lev, r, v, out, coef, parts, ghosts, most=1, rows=None):
    w, cx, cu, cd, cz = coef
    for group in grouped(lev.work(ghosts) if rows is None else rows, most):
        i, before, after = near(group), near(group, -1), near(group, 1)
        for p, size in parts:
            here = v.get(i, p, size)
            up = cz.get(i, p, size)
            acc = r.get(i, p, size) + cx.get(before, p, size) * v.get(before, p, size)
            acc = acc + cx.get(i, p, size) * v.get(after, p, size)
            acc = acc + cu.get(i, p, size) * v.get(i, p + 1, size)
            acc = acc + cd.get(i, p, size) * v.get(i, p - 1, size)
            acc = acc + up * spin(here, LANES - 1) + spin(up * here, 1)
            out.set(i, p, size, (1.0 - JACOBI_WEIGHT) * here + w.get(i, p, size) * acc)


def clear(v, rows, p):
    for i in range(rows) if isinstance(rows, int) else rows:
        v.set(i, p, 8, jnp.zeros((8, LANES), jnp.float32))


def late_smooth(fine_r, early, bufs, fine_coef, others):
    jobs = []
    for side, start in ((0, 0), (1, 120)):
        for v in bufs[side]:
            clear(v, FINE.rows, -8 if side == 0 else 144)
        jobs.append((FINE, fine_r[side], list(bufs[side]), fine_coef[side], start, 24, 3, side))
    for lev, r, va, vb, coef in others:
        for v in (va, vb):
            clear(v, lev.rows, -8)
            clear(v, lev.rows, lev.span)
        jobs.append((lev, r, [va, vb], coef, 0, lev.span, 1 if lev is MID else 3, None))
    for lev, r, pair, coef, start, size, most, side in jobs:
        begin(lev, r, pair[0], coef, [(start, size)], most)
    for number in range(3):
        for lev, r, pair, coef, start, size, most, side in jobs:
            if side is not None:
                tile = BEYOND[side]
                for i in lev.work(REACH - number):
                    pair[0].set(i, tile, 8, early[number].get(i, tile, 8))
            fixup(pair[0], lev, start, size)
        for lev, r, pair, coef, start, size, most, side in jobs:
            sweep(lev, r, pair[0], pair[1], coef, [(start, size)], REACH - 1 - number, most)
            pair.reverse()
    return [job[2][0] for job in jobs]


def early_smooth(r, views, coef, safe):
    stages = []
    for number in range(4):
        inside = stage_rows(number)
        every = FINE.work(REACH - number)
        stages.append([i for i in every if (i in inside) == safe])
    for n, v in enumerate(views[:3]):
        for p in (8, 128):
            clear(v, stage_rows(n) if safe else FINE.rows, p)
    begin(FINE, r, views[0], coef, INNER, 1, stages[0])
    for n in range(3):
        if not safe:
            fixup(views[n], FINE, 16, 112)
        sweep(FINE, r, views[n], views[n + 1], coef, INNER, 0, 1, stages[n + 1])


BEYOND = (24, 112)


def expand(view, row, lev, tmp):
    part = view.get(row, 6, lev.span // 4)
    for t in range(4):
        tmp[pl.ds(t, lev.span // 4, stride=4), :] = part


def correction(vm, vl, tmp):
    expand(vl, 1, MID, tmp.at[4])
    for m in range(4):
        value = vm.get(1 + m, 0, MID.span) + tmp[4, 0 : MID.span]
        vm.set(1 + m, 0, MID.span, value)
        expand(vm, 1 + m, FINE, tmp.at[m])


def pack_y(tiles_low, tiles_high, low, high):
    for n in range((len(tiles_low) + 1) // 2):
        for tiles, out, is_low in ((tiles_low, low, True), (tiles_high, high, False)):
            a = tiles[2 * n]
            if 2 * n + 1 < len(tiles):
                b = pltpu.roll(tiles[2 * n + 1], 4, 0)
                first = sublane((8, LANES)) < 4
                a = jnp.where(first, a, b) if is_low else jnp.where(first, b, a)
            out[n] = a


def unpack_y(ref, n):
    value = ref[n // 2]
    return pltpu.roll(value, 4, 0) if n % 2 else value


def first_kernel(
    rhs, kappa, kz, rz, km, rm, kl, rl, send_a, send_b, tmp, k_in, r_in, low, high, sems
):
    copies = []
    for n, (source, target) in enumerate(((kappa, k_in), (rhs, r_in))):
        for c in range(4):
            rows = slice(512 * c, 512 * c + 512)
            copy = pltpu.make_async_copy(source.at[rows], target.at[rows], sems.at[4 * n + c])
            copies.append(copy)
    for copy in copies[:4]:
        copy.start()
    for n, (source, target, mid, low_level) in enumerate(((k_in, kz, km, kl), (r_in, rz, rm, rl))):
        for c, copy in enumerate(copies[4 * n : 4 * n + 4]):
            copy.wait()
            if n == 0:
                copies[4 + c].start()
        for x in range(16):
            rows = [source[pl.ds(16 * q + x, DEPTH, stride=64), :] for q in range(4)]
            target[x] = jnp.concatenate(rows, axis=0).T
        sum_rows_mid(target, tmp, mid)
        if n == 0:
            for m in range(4):
                mid[m] = mid[m] * (1.0 / 16.0)
            low_level[...] = sum_rows_low(mid, tmp) * (1.0 / 16.0)
        else:
            low_level[...] = sum_rows_low(mid, tmp)
        for out, is_low in ((low, True), (high, False)):
            edge = 0 if is_low else 3
            line = [j if is_low else 15 - j for j in range(4)]
            if n == 0:
                out[0:128] = join_slots([(kz[j], edge) for j in line])
                out[288:296] = kl[...]
                continue
            fine = join_slots([(rz[j], edge) for j in line[:3]])
            for j in range(4):
                value, source_q = mid_piece(km, j, is_low)
                out[128 + 32 * j : 160 + 32 * j] = jnp.where(
                    quarter((32, LANES)) == 3, move(value, source_q, 3), fine[32 * j : 32 * j + 32]
                )
            out[256:288] = join_slots([mid_piece(rm, j, is_low) for j in range(3)])
            out[296:304] = rl[...]
    ship("gx", low, high, send_a, send_b)


def second_kernel(
    got_a, got_b, kz, rz, km, rm, kl, rl, gk, gr, gkm, grm, gkl, grl, send_a, send_b, low, high
):
    left, right = received("gx", got_a, got_b)
    for j in range(4):
        gk[j] = ghost_of(left[0:128], right[0:128], j)
        rows = slice(128 + 32 * j, 160 + 32 * j)
        gkm[j] = ghost_of(left[rows], right[rows], 3)
        gkl[j] = edges(move(left[288:296], 3 - j, 0), move(right[288:296], j, 3))
    for j in range(3):
        gr[j] = ghost_of(left[128:256], right[128:256], j)
        grm[j] = ghost_of(left[256:288], right[256:288], j)
        grl[j] = edges(move(left[296:304], 3 - j, 0), move(right[296:304], j, 3))
    at = 0
    extra = 0
    row = sublane((8, LANES))
    for lev, k, r, ghost_k, ghost_r in (
        (FINE, kz, rz, gk, gr), (MID, km, rm, gkm, grm), (LOW, kl, rl, gkl, grl),
    ):
        for is_low, out in ((True, low), (False, high)):
            rows = slice(0, 8) if is_low else slice(lev.own - 8, lev.own)
            pairs = []
            for i in range(lev.n):
                pairs.append((k[rows], r[rows]) if lev.n == 1 else (k[i, rows], r[i, rows]))
            for a in (0, 2):
                rest = ghost_r[a, rows]
                rest = two_in_one(rest, ghost_r[a + 1, rows]) if a == 0 else rest
                pairs.append((two_in_one(ghost_k[a, rows], ghost_k[a + 1, rows]), rest))
            for i, (a, b) in enumerate(pairs):
                if is_low:
                    out[at + i] = jnp.where(row < 5, a, pltpu.roll(b, 5, 0))
                else:
                    out[at + i] = jnp.where(row >= 3, a, pltpu.roll(b, 3, 0))
            for i in range(lev.n):
                e = extra + i
                cell = slice(3, 4) if is_low else slice(lev.own - 4, lev.own - 3)
                out[27 + e // 8, e % 8 : e % 8 + 1] = r[cell] if lev.n == 1 else r[i, cell]
        at += lev.n + 2
        extra += lev.n
    ship("gy", low, high, send_a, send_b)


def halos(lev, ylo, yhi, at, extra, k, r, p_low, p_high):
    row = sublane((8, LANES))
    for side, ref in ((0, ylo), (1, yhi)):
        start = p_low if side == 0 else p_high
        for i in range(lev.n + 2):
            value = ref[at + i]
            if side == 0:
                a = jnp.where(row >= 3, value, 0.0)
                b = jnp.where(row >= 5, pltpu.roll(value, 5, 0), 0.0)
            else:
                a = jnp.where(row < 5, value, 0.0)
                b = jnp.where(row < 3, pltpu.roll(value, 3, 0), 0.0)
            if i < lev.n:
                k[side].set(1 + i, start, 8, a)
                r[side].set(1 + i, start, 8, b)
                e = extra + i
                cell = start + 4 if side == 0 else start + 3
                r[side].set(1 + i, cell, 1, ref[27 + e // 8, e % 8 : e % 8 + 1])
                continue
            for part in (0, 1):
                j = 2 * (i - lev.n) + part
                k[side].set(lev.ghost + j, start, 8, one_of_two(a, part))
                if j < REACH:
                    r[side].set(lev.ghost + j, start, 8, one_of_two(b, part))


def own_rows(lev, dst, src, ghosts, p, size):
    for i in lev.work(ghosts):
        dst.set(i, p, size, src.get(i, p, size))


def safe_kernel(kz, rz, w, cx, cu, cd, cz, v0, v1, v2, v3):
    coef = [View(ref, -16) for ref in (w, cx, cu, cd, cz)]
    setup(FINE, Parts(FINE, kz, None), coef, INNER, 1, SAFE_FACES, SAFE)
    early_smooth(Parts(FINE, rz, None), [View(ref, -8) for ref in (v0, v1, v2, v3)], coef, True)


def safe_again_kernel(defect, w, cx, cu, cd, cz, v0, v1, v2, v3):
    coef = [View(ref, -16) for ref in (w, cx, cu, cd, cz)]
    views = [View(ref, -8) for ref in (v0, v1, v2, v3)]
    early_smooth(Parts(FINE, defect, None), views, coef, True)


def early_kernel(
    kz, rz, gk, gr, wa, xa, ua, da, za, b0, b1, b2, b3,
    w, cx, cu, cd, cz, v0, v1, v2, v3, k_s,
):
    k = View(k_s, -8)
    own = Parts(FINE, kz, gk)
    edge = [i for i in FINE.work(4) if i not in SAFE]
    for i in edge:
        k.set(i, 8, 128, own.get(i, 8, 128))
    fixup(k, FINE, 8, 128)
    coef = split_views((wa, xa, ua, da, za), (w, cx, cu, cd, cz))
    faces = [i for i in FINE.faces() if i not in SAFE_FACES]
    setup(FINE, k, coef, INNER, 1, faces, [i for i in edge if i < FINE.ghost + REACH])
    views = stage_views((b0, b1, b2, b3), (v0, v1, v2, v3))
    early_smooth(Parts(FINE, rz, gr), views, coef, False)


def strip_views(refs):
    return [[View(ref, -120 * side, side) for ref in refs] for side in (0, 1)]


def strip_bufs(*refs):
    return [[View(ref, 8 - 112 * side, side) for ref in refs] for side in (0, 1)]


def third_kernel(
    kz, rz, km, rm, kl, rl, gk, gr, gkm, grm, gkl, grl, got_a, got_b,
    wa, xa, ua, da, za, b0, b1, b2, b3, w, cx, cu, cd, cz, v0, v1, v2, v3,
    wf, xf, uf, df, zf, wm, xm, um, dm, zm, wl, xl, ul, dl, zl,
    first, defect, dmid, dlow, cedge, send_a, send_b,
    ks, rs, sa, sb, km_s, rm_s, vm_s, kl_s, rl_s, vl_s, full, tmp, low, high,
):
    ylo, yhi = received("gy", got_a, got_b)
    early = split_views((wa, xa, ua, da, za), (w, cx, cu, cd, cz))
    early_v = stage_views((b0, b1, b2, b3), (v0, v1, v2, v3))
    others = []
    at, extra = 18, 16
    for lev, own_k, ghost_k, k_ref, own_r, ghost_r, r_ref, v_ref, refs in (
        (MID, km, gkm, km_s, rm, grm, rm_s, vm_s, (wm, xm, um, dm, zm)),
        (LOW, kl, gkl, kl_s, rl, grl, rl_s, vl_s, (wl, xl, ul, dl, zl)),
    ):
        k, r = View(k_ref, 8), View(r_ref, 0)
        own_rows(lev, k, Parts(lev, own_k, ghost_k), 4, 8, lev.own)
        own_rows(lev, r, Parts(lev, own_r, ghost_r), REACH, 8, lev.own)
        halos(lev, ylo, yhi, at, extra, (k, k), (r, r), 0, 8 + lev.own)
        at, extra = at + lev.n + 2, extra + lev.n
        clear(k, lev.rows, -8)
        clear(k, lev.rows, lev.span)
        fixup(k, lev, 0, lev.span)
        coef = [View(ref, 0) for ref in refs]
        setup(lev, k, coef, [(0, lev.span)], 1 if lev is MID else 3)
        others.append((lev, r, View(v_ref, 8), k, coef))
    strips = strip_views((wf, xf, uf, df, zf))
    (kl_v,), (kh_v,) = strip_bufs(ks)
    (rl_v,), (rh_v,) = strip_views((rs,))
    halos(FINE, ylo, yhi, 0, 0, (kl_v, kh_v), (rl_v, rh_v), 0, 136)
    for k, r, p_k, p_r, start, pad, kept in (
        (kl_v, rl_v, 8, 8, 0, -8, 16), (kh_v, rh_v, 120, 120, 128, 144, 120),
    ):
        side = 0 if start == 0 else 1
        own_rows(FINE, k, Parts(FINE, kz, gk), 4, p_k, 16)
        own_rows(FINE, r, Parts(FINE, rz, gr), REACH, p_r, 16)
        clear(k, FINE.rows, pad)
        fixup(k, FINE, start if side == 0 else 120, 24)
        setup(FINE, k, strips[side], [(start, 16)], 4)
        for number, (dst, src) in enumerate(zip(strips[side], early)):
            rows = FINE.work(REACH) + ([0, FINE.n + 2] if number == 1 else [])
            for i in rows:
                dst.set(i, kept, 8, src.get(i, kept, 8))
    *late, vm, vl = late_smooth((rl_v, rh_v), early_v, strip_bufs(sa, sb), strips, others)
    correction(vm, vl, tmp)
    whole = View(full, 8)
    for i in range(1, 17):
        m = (i - 1) // 4
        for p, size, v in ((0, 24, late[0]), (24, 48, early_v[3]), (72, 48, early_v[3]), (120, 24, late[1])):
            whole.set(i, p, size, STEP_WEIGHT * (v.get(i, p, size) + tmp[m, p : p + size]))
    fixup(whole, FINE, 8, 128, ghost=False)
    for most, p, size, coef in (
        (8, 8, 8, strips[0]), (1, 16, 56, early), (1, 72, 56, early), (8, 128, 8, strips[1]),
    ):
        for group in grouped(range(1, 17), most):
            i, before, after = near(group), near(group, -1), near(group, 1)
            _, x, u, d, z = [c.get(i, p, size) for c in coef]
            v = whole.get(i, p, size)
            image_z = z * (v - spin(v, LANES - 1)) + spin(z, 1) * (v - spin(v, 1))
            image = coef[1].get(before, p, size) * (v - whole.get(before, p, size))
            image = image + x * (v - whole.get(after, p, size))
            image = image + u * (v - whole.get(i, p + 1, size))
            image = image + d * (v - whole.get(i, p - 1, size))
            image = image + image_z
            defect[before, p - 8 : p - 8 + size] = rz[before, p - 8 : p - 8 + size] - image
            first[before, p - 8 : p - 8 + size] = v
    for p, size, coef in ((8, 8, strips[0]), (16, 112, early), (128, 8, strips[1])):
        cedge[p - 8 : p - 8 + size] = edges(coef[1].get(0, p, size), coef[1].get(16, p, size))
    sum_rows_mid(defect, tmp, dmid)
    dlow[...] = sum_rows_low(dmid, tmp)
    for out, is_low in ((low, True), (high, False)):
        edge = 0 if is_low else 3
        fine = join_slots([(defect[j if is_low else 15 - j], edge) for j in range(3)])
        for j in range(3):
            value, source = mid_piece(dmid, j, is_low)
            rows = slice(32 * j, 32 * j + 32)
            out[rows] = jnp.where(quarter((32, LANES)) == 3, move(value, source, 3), fine[rows])
            source = j if is_low else 3 - j
            rows = slice(96 + 8 * j, 104 + 8 * j)
            out[rows] = jnp.where(quarter((8, LANES)) == 3, move(dlow[...], source, 3), fine[rows])
        out[120:128] = fine[120:128]
        line = 0 if is_low else 15
        out[128:160] = join_slots([(first[line, 32 * g : 32 * g + 32], edge) for g in range(4)])
    ship("gx", low, high, send_a, send_b)


def fourth_kernel(
    got_a, got_b, first, defect, dmid, dlow, cedge,
    gf, gm, gl, d0, d15, m0, m3, lows, send_a, send_b, tmp, low, high,
):
    left, right = received("gx", got_a, got_b)
    face = cedge[...]
    group = quarter((128, LANES))
    other = [ghost_of(left[128:160], right[128:160], g) for g in range(4)]
    mine = face * jnp.concatenate(other, axis=0)
    theirs = face * edges(first[0], first[15])
    d0[...] = defect[0] + jnp.where(group == 0, mine, 0.0)
    d15[...] = defect[15] + jnp.where(group == 3, mine, 0.0)
    sums = []
    for n, value in enumerate((mine, theirs)):
        tmp[n, 0:128, :] = value
        mid = fourths(tmp.at[n], 32)
        tmp[n + 2, 0:32, :] = mid
        sums.append((mid, fourths(tmp.at[n + 2], 8)))
    group = quarter((32, LANES))
    m0[...] = dmid[0] + jnp.where(group == 0, sums[0][0], 0.0)
    m3[...] = dmid[3] + jnp.where(group == 3, sums[0][0], 0.0)
    lows[...] = dlow[...] + sums[0][1]
    for j in range(3):
        for out, rows, slot, add in (
            (gf, slice(0, 128), j, theirs),
            (gm, slice(32 * j, 32 * j + 32), 3, sums[1][0]),
            (gl, slice(96 + 8 * j, 104 + 8 * j), 3, sums[1][1]),
        ):
            value = ghost_of(left[rows], right[rows], slot)
            out[j] = value + add if j == 0 else value
    tiles = ([], [])
    for lev, r, ghost in (
        (FINE, Parts(FINE, defect, gf, {1: d0, 16: d15}), gf),
        (MID, Parts(MID, dmid, gm, {1: m0, 4: m3}), gm),
        (LOW, Parts(LOW, lows, gl), gl),
    ):
        for side, p in ((0, 8), (1, lev.own)):
            tiles[side].extend(r.get(i, p, 8) for i in range(1, lev.n + 1))
            a, b, c = [r.get(lev.ghost + j, p, 8) for j in range(3)]
            tiles[side].extend([two_in_one(a, b), c])
    pack_y(tiles[0], tiles[1], low, high)
    ship("gy", low, high, send_a, send_b)


def residual_halos(lev, ylo, yhi, at, r, p_low, p_high):
    for side, ref in ((0, ylo), (1, yhi)):
        start = p_low if side == 0 else p_high
        for i in range(lev.n):
            r[side].set(1 + i, start, 8, unpack_y(ref, at + i))
        both = unpack_y(ref, at + lev.n)
        r[side].set(lev.ghost, start, 8, one_of_two(both, 0))
        r[side].set(lev.ghost + 1, start, 8, one_of_two(both, 1))
        r[side].set(lev.ghost + 2, start, 8, unpack_y(ref, at + lev.n + 1))


def early_again_kernel(
    defect, gf, d0, d15, wa, xa, ua, da, za, w, cx, cu, cd, cz, b0, b1, b2, b3, v0, v1, v2, v3
):
    coef = split_views((wa, xa, ua, da, za), (w, cx, cu, cd, cz))
    views = stage_views((b0, b1, b2, b3), (v0, v1, v2, v3))
    early_smooth(Parts(FINE, defect, gf, {1: d0, 16: d15}), views, coef, False)


def fifth_kernel(
    wf, xf, uf, df, zf, wm, xm, um, dm, zm, wl, xl, ul, dl, zl,
    first, defect, dmid, gf, gm, gl, d0, d15, m0, m3, lows,
    b0, b1, b2, b3, v0, v1, v2, v3, got_a, got_b, out,
    rs, sa, sb, rm_s, va_m, vb_m, rl_s, va_l, vb_l, tmp, out_s, sems,
):
    ylo, yhi = received("gy", got_a, got_b)
    early_v = stage_views((b0, b1, b2, b3), (v0, v1, v2, v3))
    others = []
    at = 18
    for lev, parts, r_ref, va, vb, refs in (
        (MID, Parts(MID, dmid, gm, {1: m0, 4: m3}), rm_s, va_m, vb_m, (wm, xm, um, dm, zm)),
        (LOW, Parts(LOW, lows, gl), rl_s, va_l, vb_l, (wl, xl, ul, dl, zl)),
    ):
        r = View(r_ref, 0)
        own_rows(lev, r, parts, REACH, 8, lev.own)
        residual_halos(lev, ylo, yhi, at, (r, r), 0, 8 + lev.own)
        at += lev.n + 2
        coef = [View(ref, 0) for ref in refs]
        others.append((lev, r, View(va, 8), View(vb, 8), coef))
    strips = strip_views((wf, xf, uf, df, zf))
    (rl_v,), (rh_v,) = strip_views((rs,))
    parts = Parts(FINE, defect, gf, {1: d0, 16: d15})
    own_rows(FINE, rl_v, parts, REACH, 8, 16)
    own_rows(FINE, rh_v, parts, REACH, 120, 16)
    residual_halos(FINE, ylo, yhi, 0, (rl_v, rh_v), 0, 136)
    *late, vm, vl = late_smooth((rl_v, rh_v), early_v, strip_bufs(sa, sb), strips, others)
    correction(vm, vl, tmp)
    flat = out_s.reshape(2048, LANES)
    copies = []
    for x in range(16):
        pieces = []
        for p, size, v in ((8, 16, late[0]), (24, 96, early_v[3]), (120, 16, late[1])):
            part = v.get(1 + x, p, size) + tmp[x // 4, p : p + size]
            pieces.append(first[x, p - 8 : p - 8 + size] + STEP_WEIGHT * part)
        total = jnp.concatenate(pieces, axis=0).T
        for q in range(4):
            flat[pl.ds(16 * q + x, DEPTH, stride=64), :] = total[DEPTH * q : DEPTH * q + DEPTH]
        if x % 8 == 7:
            for q in range(4):
                rows = pl.ds(16 * q + x - 7, 8)
                copies.append(
                    pltpu.make_async_copy(out_s.at[:, rows], out.at[:, rows], sems.at[len(copies)])
                )
                copies[-1].start()
    for copy in copies:
        copy.wait()


def shape(*dims):
    return jax.ShapeDtypeStruct(dims, jnp.float32)


def scratch(*dims):
    return pltpu.VMEM(dims, jnp.float32)


def swap(a, b, axis):
    out = []
    for start, value in ((0, a), (1, b)):
        pairs = []
        for i in range(start, lax.axis_size(axis) - 1, 2):
            pairs += [(i, i + 1), (i + 1, i)]
        out.append(lax.ppermute(value, axis, pairs) if pairs else jnp.zeros_like(value))
    return out


def on_device(rhs, kappa):
    def call(body, outs, scratches=(), flops=10**6, ins=None, out=None, room=20):
        specs = {} if ins is None else {"in_specs": ins}
        if out is not None:
            specs["out_specs"] = out
        return pl.pallas_call(
            body,
            out_shape=outs,
            **specs,
            scratch_shapes=list(scratches),
            compiler_params=params(room),
            cost_estimate=cost(flops),
        )

    n = FINE.rows
    own = [shape(16, 128, LANES), shape(4, 32, LANES), shape(8, LANES)]
    tmp = scratch(5, 144, LANES)
    outs = [own[0], own[0], own[1], own[1], own[2], own[2]] + [shape(304, LANES)] * 2
    held = scratch(2048, LANES)
    far = pl.BlockSpec(memory_space=pltpu.HBM)
    bufs = [tmp, held, held] + [scratch(304, LANES)] * 2 + [pltpu.SemaphoreType.DMA((8,))]
    kz, rz, km, rm, kl, rl, *sends = call(first_kernel, outs, bufs, ins=[far, far], room=51)(
        rhs.reshape(2048, LANES), kappa.reshape(2048, LANES)
    )
    inside = [shape(16, 128, LANES)] * 4
    outs = [shape(16, 112, LANES)] * 5 + inside
    safe = call(safe_kernel, outs, (), 10**8)(kz, rz)
    kl, *safe = lax.optimization_barrier((kl, *safe))
    gots = swap(*sends, "gx")
    outs = [shape(g, width, LANES) for width in (128, 32, 8) for g in (4, 3)]
    bufs = [scratch(30, 8, LANES)] * 2
    *ghosts, send_a, send_b = call(second_kernel, outs + [shape(30, 8, LANES)] * 2, bufs)(
        *gots, kz, rz, km, rm, kl, rl
    )
    gk, gr = ghosts[:2]
    gots = swap(send_a, send_b, "gy")
    outs = [shape(n, 112, LANES)] * 5 + [shape(n, 128, LANES)] * 4
    early = call(early_kernel, outs, [scratch(n, 128, LANES)], 10**8)(
        kz, rz, gk, gr, *safe
    )
    strip = shape(n, 2, 24, LANES)
    outs = [strip] * 5
    for lev in (MID, LOW):
        outs += [shape(lev.rows, lev.span, LANES)] * 5
    outs += [own[0], own[0], own[1], own[2], shape(128, LANES)] + [shape(160, LANES)] * 2
    strip_scratch = [scratch(n, 2, 48, LANES), scratch(n, 2, 24, LANES)]
    bufs = strip_scratch + [scratch(n, 2, 48, LANES)] * 2
    for lev in (MID, LOW):
        wide = scratch(lev.rows, lev.span + 16, LANES)
        bufs += [wide, scratch(lev.rows, lev.span, LANES), wide]
    bufs += [scratch(n, 160, LANES), tmp] + [scratch(160, LANES)] * 2
    results = call(third_kernel, outs, bufs)(
        kz, rz, km, rm, kl, rl, *ghosts, *gots, *safe, *early
    )
    state = results[:15]
    first, defect, dmid, dlow, cedge, send_a, send_b = results[15:]
    gots = swap(send_a, send_b, "gx")
    again = call(safe_again_kernel, inside, (), 10**8)(defect, *safe[:5])
    dlow, *again = lax.optimization_barrier((dlow, *again))
    outs = [shape(3, width, LANES) for width in (128, 32, 8)]
    outs += [shape(128, LANES)] * 2 + [shape(32, LANES)] * 2 + [shape(8, LANES)]
    bufs = [tmp] + [scratch(14, 8, LANES)] * 2
    *halo, send_a, send_b = call(fourth_kernel, outs + [shape(14, 8, LANES)] * 2, bufs)(
        *gots, first, defect, dmid, dlow, cedge
    )
    gf, gm, gl, d0, d15, m0, m3, lows = halo
    gots = swap(send_a, send_b, "gy")
    inner = call(early_again_kernel, [shape(n, 128, LANES)] * 4, (), 10**8)(
        defect, gf, d0, d15, *safe[:5], *early[:5], *again
    )
    bufs = [strip_scratch[1]] + [scratch(n, 2, 48, LANES)] * 2
    for lev in (MID, LOW):
        wide = scratch(lev.rows, lev.span + 16, LANES)
        bufs += [scratch(lev.rows, lev.span, LANES), wide, wide]
    bufs += [tmp, scratch(*rhs.shape), pltpu.SemaphoreType.DMA((8,))]
    return call(fifth_kernel, shape(*rhs.shape), bufs, out=far)(
        *state, first, defect, dmid, *halo, *again, *inner, *gots
    )


def solution(mesh):
    return jax.shard_map(
        on_device,
        mesh=mesh,
        in_specs=(P("groups", "gx", "gy"), P("groups", "gx", "gy")),
        out_specs=P("groups", "gx", "gy"),
        check_vma=False,
    )
```

```python
import jax
import jax.numpy as jnp
from jax import lax
from jax.experimental import pallas as pl
from jax.experimental.pallas import tpu as pltpu
from jax.sharding import PartitionSpec as P

JACOBI_WEIGHT = 0.8
STEP_WEIGHT = 0.6
LANES = 128
DEPTH = 32
QUARTERS = 4
REACH = 3


class Level:
    def __init__(self, rows, width, flat, up):
        self.n = rows
        self.own = width
        self.span = width + 16
        self.flat = flat
        self.up = up
        self.rows = rows + 7
        self.ghost = rows + 3

    def work(self, ghosts):
        return list(range(1, self.n + 1)) + list(range(self.ghost, self.ghost + ghosts))

    def faces(self):
        return [i for i in range(self.rows - 1) if i != self.n + 1]


LEVELS = (Level(16, 128, 1.0, 1.0), Level(4, 32, 4.0, 16.0), Level(1, 8, 16.0, 256.0))
FINE, MID, LOW = LEVELS
INNER = [(16, 56), (72, 56)]
SAFE, SAFE_FACES = range(2, 16), range(1, 16)


def grouped(rows, most):
    out = []
    for i in rows:
        if out and len(out[-1]) < most and out[-1][-1] == i - 1:
            out[-1].append(i)
        else:
            out.append([i])
    return out


def near(group, by=0):
    if len(group) == 1:
        return group[0] + by
    return slice(group[0] + by, group[-1] + 1 + by)


def spin(value, shift):
    return pltpu.roll(value, shift, value.ndim - 1)


class View:
    def __init__(self, ref, shift, side=None):
        self.ref, self.shift, self.side = ref, shift, side

    def at(self, i, p, size):
        rows = slice(p + self.shift, p + self.shift + size)
        return (i, rows) if self.side is None else (i, self.side, rows)

    def get(self, i, p, size):
        return self.ref[self.at(i, p, size)]

    def set(self, i, p, size, value):
        self.ref[self.at(i, p, size)] = value


class Split:
    def __init__(self, rows, inside, outside):
        self.rows, self.inside, self.outside = rows, inside, outside

    def get(self, i, p, size):
        return (self.inside if i in self.rows else self.outside).get(i, p, size)

    def set(self, i, p, size, value):
        self.outside.set(i, p, size, value)


def split_views(inside, outside):
    out = []
    for n, (a, b) in enumerate(zip(inside, outside)):
        out.append(Split(SAFE_FACES if n == 1 else SAFE, View(a, -16), View(b, -16)))
    return out


def stage_rows(number):
    return range(2 + number, 16 - number)


def stage_views(inside, outside):
    return [
        Split(stage_rows(n), View(a, -8), View(b, -8))
        for n, (a, b) in enumerate(zip(inside, outside))
    ]


class Parts:
    def __init__(self, lev, own, ghost, swap=None):
        self.lev, self.own, self.ghost, self.swap = lev, own, ghost, swap or {}

    def get(self, i, p, size):
        rows = slice(p - 8, p - 8 + size)
        if i >= self.lev.ghost:
            return self.ghost[i - self.lev.ghost, rows]
        if i in self.swap:
            return self.swap[i][rows]
        return self.own[rows] if self.lev.n == 1 else self.own[i - 1, rows]


def params(mib=20):
    return pltpu.CompilerParams(vmem_limit_bytes=mib << 20)


def cost(flops):
    return pl.CostEstimate(flops=flops, bytes_accessed=8 << 20, transcendentals=0)


def quarter(shape):
    return lax.broadcasted_iota(jnp.int32, shape, 1) // DEPTH


def sublane(shape):
    return lax.broadcasted_iota(jnp.int32, shape, 0)


class Pick:
    def __init__(self, first, second, use_first):
        self.first, self.second, self.use_first = first, second, use_first

    def __getitem__(self, at):
        return jnp.where(self.use_first, self.first[at], self.second[at])


def is_even(axis):
    return lax.axis_index(axis) % 2 == 0


def received(axis, a, b):
    even = is_even(axis)
    return Pick(b, a, even), Pick(a, b, even)


def ship(axis, low, high, a, b):
    even = is_even(axis)
    below, above = low[...], high[...]
    a[...] = jnp.where(even, above, below)
    b[...] = jnp.where(even, below, above)


def move(value, source, target):
    shift = DEPTH * ((target - source) % QUARTERS)
    return pltpu.roll(value, shift, 1) if shift else value


def join_slots(pieces):
    out = None
    for slot, (value, source) in enumerate(pieces):
        part = move(value, source, slot)
        out = part if out is None else jnp.where(quarter(part.shape) == slot, part, out)
    return out


def edges(left, right):
    group = quarter(left.shape)
    return jnp.where(group == 0, left, jnp.where(group == 3, right, 0.0))


def ghost_of(from_left, from_right, slot):
    return edges(move(from_left, slot, 0), move(from_right, slot, 3))


def two_in_one(a, b):
    group = quarter(a.shape)
    up, down = pltpu.roll(b, DEPTH, 1), pltpu.roll(b, LANES - DEPTH, 1)
    return jnp.where(group == 1, up, jnp.where(group == 2, down, a))


def one_of_two(v, second):
    if not second:
        return edges(v, v)
    return edges(pltpu.roll(v, LANES - DEPTH, 1), pltpu.roll(v, DEPTH, 1))


def mid_piece(ref, j, low):
    index = j if low else 15 - j
    return ref[index % 4], index // 4


def fourths(tmp, size):
    out = tmp[pl.ds(0, size, stride=4), :]
    for t in range(1, 4):
        out = out + tmp[pl.ds(t, size, stride=4), :]
    return out


def sum_rows_mid(rows_ref, tmp, out_ref):
    for m in range(4):
        total = rows_ref[4 * m] + rows_ref[4 * m + 1]
        tmp[m, 0:128, :] = total + rows_ref[4 * m + 2] + rows_ref[4 * m + 3]
        out_ref[m] = fourths(tmp.at[m], 32)


def sum_rows_low(mid_ref, tmp):
    tmp[4, 0:32, :] = mid_ref[0] + mid_ref[1] + mid_ref[2] + mid_ref[3]
    return fourths(tmp.at[4], 8)


def fixup(v, lev, p, size, ghost=True):
    group = quarter((size, LANES))
    first, last = v.get(1, p, size), v.get(lev.n, p, size)
    edge = v.get(lev.ghost, p, size) if ghost else jnp.zeros((size, LANES), jnp.float32)
    v.set(0, p, size, jnp.where(group == 0, edge, pltpu.roll(last, DEPTH, 1)))
    v.set(lev.n + 1, p, size, jnp.where(group == 3, edge, pltpu.roll(first, LANES - DEPTH, 1)))
    if ghost:
        v.set(lev.n + 2, p, size, jnp.where(group == 0, first, last))


def harmonic(a, b):
    total = a + b
    return 2.0 * a * b / jnp.where(total > 0, total, 1.0)


def setup(lev, k, coef, parts, most=1, faces=None, work=None):
    w, cx, cu, cd, cz = coef
    for group in grouped(lev.faces() if faces is None else faces, most):
        i, j = near(group), near(group, 1)
        for p, size in parts:
            cx.set(i, p, size, lev.flat * harmonic(k.get(i, p, size), k.get(j, p, size)))
    for group in grouped(lev.work(REACH) if work is None else work, most):
        i = near(group)
        for p, size in parts:
            here = k.get(i, p, size)
            above = lev.flat * harmonic(here, k.get(i, p + 1, size))
            below = lev.flat * harmonic(k.get(i, p - 1, size), here)
            z = lax.broadcasted_iota(jnp.int32, here.shape, here.ndim - 1) % DEPTH
            up = lev.up * harmonic(here, spin(here, LANES - 1))
            up = jnp.where(z == DEPTH - 1, 0.0, up)
            cu.set(i, p, size, above)
            cd.set(i, p, size, below)
            cz.set(i, p, size, up)
    for group in grouped(lev.work(REACH) if work is None else work, most):
        i = near(group)
        for p, size in parts:
            up = cz.get(i, p, size)
            diagonal = cx.get(near(group, -1), p, size) + cx.get(i, p, size)
            diagonal = diagonal + (cd.get(i, p, size) + cu.get(i, p, size)) + (spin(up, 1) + up)
            good = diagonal > 0
            value = jnp.where(good, JACOBI_WEIGHT / jnp.where(good, diagonal, 1.0), 0.0)
            w.set(i, p, size, value)


def begin(lev, r, v, coef, parts, most=1, rows=None):
    for group in grouped(lev.work(REACH) if rows is None else rows, most):
        i = near(group)
        for p, size in parts:
            v.set(i, p, size, coef[0].get(i, p, size) * r.get(i, p, size))


def sweep(lev, r, v, out, coef, parts, ghosts, most=1, rows=None):
    w, cx, cu, cd, cz = coef
    for group in grouped(lev.work(ghosts) if rows is None else rows, most):
        i, before, after = near(group), near(group, -1), near(group, 1)
        for p, size in parts:
            here = v.get(i, p, size)
            up = cz.get(i, p, size)
            acc = r.get(i, p, size) + cx.get(before, p, size) * v.get(before, p, size)
            acc = acc + cx.get(i, p, size) * v.get(after, p, size)
            acc = acc + cu.get(i, p, size) * v.get(i, p + 1, size)
            acc = acc + cd.get(i, p, size) * v.get(i, p - 1, size)
            acc = acc + up * spin(here, LANES - 1) + spin(up * here, 1)
            out.set(i, p, size, (1.0 - JACOBI_WEIGHT) * here + w.get(i, p, size) * acc)


def clear(v, rows, p):
    for i in range(rows) if isinstance(rows, int) else rows:
        v.set(i, p, 8, jnp.zeros((8, LANES), jnp.float32))


def late_smooth(fine_r, early, bufs, fine_coef, others, own_only):
    jobs = []
    for side, start in ((0, 0), (1, 120)):
        for v in bufs[side]:
            clear(v, FINE.rows, -8 if side == 0 else 144)
        jobs.append((FINE, fine_r[side], list(bufs[side]), fine_coef[side], start, 24, 3, side))
    for lev, r, va, vb, coef in others:
        for v in (va, vb):
            clear(v, lev.rows, -8)
            clear(v, lev.rows, lev.span)
        jobs.append((lev, r, [va, vb], coef, 0, lev.span, 1 if lev is MID else 3, None))
    for lev, r, pair, coef, start, size, most, side in jobs:
        begin(lev, r, pair[0], coef, [(start, size)], most)
    for number in range(3):
        for lev, r, pair, coef, start, size, most, side in jobs:
            if side is not None:
                tile = BEYOND[side]
                for i in lev.work(REACH - number):
                    pair[0].set(i, tile, 8, early[number].get(i, tile, 8))
            fixup(pair[0], lev, start, size)
        for lev, r, pair, coef, start, size, most, side in jobs:
            if own_only and number == 2:
                size = lev.own if side is None else 16
                start = 120 if side == 1 else 8
            sweep(lev, r, pair[0], pair[1], coef, [(start, size)], REACH - 1 - number, most)
            pair.reverse()
    return [job[2][0] for job in jobs]


def early_smooth(r, views, coef, safe):
    stages = []
    for number in range(4):
        inside = stage_rows(number)
        every = FINE.work(REACH - number)
        stages.append([i for i in every if (i in inside) == safe])
    for n, v in enumerate(views[:3]):
        for p in (8, 128):
            clear(v, stage_rows(n) if safe else FINE.rows, p)
    begin(FINE, r, views[0], coef, INNER, 1, stages[0])
    for n in range(3):
        if not safe:
            fixup(views[n], FINE, 16, 112)
        sweep(FINE, r, views[n], views[n + 1], coef, INNER, 0, 1, stages[n + 1])


BEYOND = (24, 112)


def expand(view, row, lev, tmp):
    part = view.get(row, 6, lev.span // 4)
    for t in range(4):
        tmp[pl.ds(t, lev.span // 4, stride=4), :] = part


def correction(vm, vl, tmp):
    expand(vl, 1, MID, tmp.at[4])
    for m in range(4):
        value = vm.get(1 + m, 0, MID.span) + tmp[4, 0 : MID.span]
        vm.set(1 + m, 0, MID.span, value)
        expand(vm, 1 + m, FINE, tmp.at[m])


def pack_y(tiles_low, tiles_high, low, high):
    for n in range((len(tiles_low) + 1) // 2):
        for tiles, out, is_low in ((tiles_low, low, True), (tiles_high, high, False)):
            a = tiles[2 * n]
            if 2 * n + 1 < len(tiles):
                b = pltpu.roll(tiles[2 * n + 1], 4, 0)
                first = sublane((8, LANES)) < 4
                a = jnp.where(first, a, b) if is_low else jnp.where(first, b, a)
            out[n] = a


def unpack_y(ref, n):
    value = ref[n // 2]
    return pltpu.roll(value, 4, 0) if n % 2 else value


def first_kernel(
    rhs, kappa, kz, rz, km, rm, kl, rl, send_a, send_b, tmp, k_in, r_in, low, high, sems
):
    copies = []
    for n, (source, target) in enumerate(((kappa, k_in), (rhs, r_in))):
        for c in range(4):
            rows = slice(512 * c, 512 * c + 512)
            copy = pltpu.make_async_copy(source.at[rows], target.at[rows], sems.at[4 * n + c])
            copies.append(copy)
    for copy in copies[:4]:
        copy.start()
    for n, (source, target, mid, low_level) in enumerate(((k_in, kz, km, kl), (r_in, rz, rm, rl))):
        for c, copy in enumerate(copies[4 * n : 4 * n + 4]):
            copy.wait()
            if n == 0:
                copies[4 + c].start()
        for x in range(16):
            rows = [source[pl.ds(16 * q + x, DEPTH, stride=64), :] for q in range(4)]
            target[x] = jnp.concatenate(rows, axis=0).T
        sum_rows_mid(target, tmp, mid)
        if n == 0:
            for m in range(4):
                mid[m] = mid[m] * (1.0 / 16.0)
            low_level[...] = sum_rows_low(mid, tmp) * (1.0 / 16.0)
        else:
            low_level[...] = sum_rows_low(mid, tmp)
        for out, is_low in ((low, True), (high, False)):
            edge = 0 if is_low else 3
            line = [j if is_low else 15 - j for j in range(4)]
            if n == 0:
                out[0:128] = join_slots([(kz[j], edge) for j in line])
                out[288:296] = kl[...]
                continue
            fine = join_slots([(rz[j], edge) for j in line[:3]])
            for j in range(4):
                value, source_q = mid_piece(km, j, is_low)
                out[128 + 32 * j : 160 + 32 * j] = jnp.where(
                    quarter((32, LANES)) == 3, move(value, source_q, 3), fine[32 * j : 32 * j + 32]
                )
            out[256:288] = join_slots([mid_piece(rm, j, is_low) for j in range(3)])
            out[296:304] = rl[...]
    ship("gx", low, high, send_a, send_b)


def second_kernel(
    got_a, got_b, kz, rz, km, rm, kl, rl, gk, gr, gkm, grm, gkl, grl, send_a, send_b, low, high
):
    left, right = received("gx", got_a, got_b)
    for j in range(4):
        gk[j] = ghost_of(left[0:128], right[0:128], j)
        rows = slice(128 + 32 * j, 160 + 32 * j)
        gkm[j] = ghost_of(left[rows], right[rows], 3)
        gkl[j] = edges(move(left[288:296], 3 - j, 0), move(right[288:296], j, 3))
    for j in range(3):
        gr[j] = ghost_of(left[128:256], right[128:256], j)
        grm[j] = ghost_of(left[256:288], right[256:288], j)
        grl[j] = edges(move(left[296:304], 3 - j, 0), move(right[296:304], j, 3))
    at = 0
    extra = 0
    row = sublane((8, LANES))
    for lev, k, r, ghost_k, ghost_r in (
        (FINE, kz, rz, gk, gr), (MID, km, rm, gkm, grm), (LOW, kl, rl, gkl, grl),
    ):
        for is_low, out in ((True, low), (False, high)):
            rows = slice(0, 8) if is_low else slice(lev.own - 8, lev.own)
            pairs = []
            for i in range(lev.n):
                pairs.append((k[rows], r[rows]) if lev.n == 1 else (k[i, rows], r[i, rows]))
            for a in (0, 2):
                rest = ghost_r[a, rows]
                rest = two_in_one(rest, ghost_r[a + 1, rows]) if a == 0 else rest
                pairs.append((two_in_one(ghost_k[a, rows], ghost_k[a + 1, rows]), rest))
            for i, (a, b) in enumerate(pairs):
                if is_low:
                    out[at + i] = jnp.where(row < 5, a, pltpu.roll(b, 5, 0))
                else:
                    out[at + i] = jnp.where(row >= 3, a, pltpu.roll(b, 3, 0))
            for i in range(lev.n):
                e = extra + i
                cell = slice(3, 4) if is_low else slice(lev.own - 4, lev.own - 3)
                out[27 + e // 8, e % 8 : e % 8 + 1] = r[cell] if lev.n == 1 else r[i, cell]
        at += lev.n + 2
        extra += lev.n
    ship("gy", low, high, send_a, send_b)


def halos(lev, ylo, yhi, at, extra, k, r, p_low, p_high):
    row = sublane((8, LANES))
    for side, ref in ((0, ylo), (1, yhi)):
        start = p_low if side == 0 else p_high
        for i in range(lev.n + 2):
            value = ref[at + i]
            if side == 0:
                a = jnp.where(row >= 3, value, 0.0)
                b = jnp.where(row >= 5, pltpu.roll(value, 5, 0), 0.0)
            else:
                a = jnp.where(row < 5, value, 0.0)
                b = jnp.where(row < 3, pltpu.roll(value, 3, 0), 0.0)
            if i < lev.n:
                k[side].set(1 + i, start, 8, a)
                r[side].set(1 + i, start, 8, b)
                e = extra + i
                cell = start + 4 if side == 0 else start + 3
                r[side].set(1 + i, cell, 1, ref[27 + e // 8, e % 8 : e % 8 + 1])
                continue
            for part in (0, 1):
                j = 2 * (i - lev.n) + part
                k[side].set(lev.ghost + j, start, 8, one_of_two(a, part))
                if j < REACH:
                    r[side].set(lev.ghost + j, start, 8, one_of_two(b, part))


def own_rows(lev, dst, src, ghosts, p, size):
    for i in lev.work(ghosts):
        dst.set(i, p, size, src.get(i, p, size))


def safe_kernel(kz, rz, w, cx, cu, cd, cz, v0, v1, v2, v3):
    coef = [View(ref, -16) for ref in (w, cx, cu, cd, cz)]
    setup(FINE, Parts(FINE, kz, None), coef, INNER, 1, SAFE_FACES, SAFE)
    early_smooth(Parts(FINE, rz, None), [View(ref, -8) for ref in (v0, v1, v2, v3)], coef, True)


def safe_again_kernel(defect, w, cx, cu, cd, cz, v0, v1, v2, v3):
    coef = [View(ref, -16) for ref in (w, cx, cu, cd, cz)]
    views = [View(ref, -8) for ref in (v0, v1, v2, v3)]
    early_smooth(Parts(FINE, defect, None), views, coef, True)


def early_kernel(
    kz, rz, gk, gr, wa, xa, ua, da, za, b0, b1, b2, b3,
    w, cx, cu, cd, cz, v0, v1, v2, v3, k_s,
):
    k = View(k_s, -8)
    own = Parts(FINE, kz, gk)
    edge = [i for i in FINE.work(4) if i not in SAFE]
    for i in edge:
        k.set(i, 8, 128, own.get(i, 8, 128))
    fixup(k, FINE, 8, 128)
    coef = split_views((wa, xa, ua, da, za), (w, cx, cu, cd, cz))
    faces = [i for i in FINE.faces() if i not in SAFE_FACES]
    setup(FINE, k, coef, INNER, 1, faces, [i for i in edge if i < FINE.ghost + REACH])
    views = stage_views((b0, b1, b2, b3), (v0, v1, v2, v3))
    early_smooth(Parts(FINE, rz, gr), views, coef, False)


def strip_views(refs):
    return [[View(ref, -120 * side, side) for ref in refs] for side in (0, 1)]


def strip_bufs(*refs):
    return [[View(ref, 8 - 112 * side, side) for ref in refs] for side in (0, 1)]


def third_kernel(
    kz, rz, km, rm, kl, rl, gk, gr, gkm, grm, gkl, grl, got_a, got_b,
    wa, xa, ua, da, za, b0, b1, b2, b3, w, cx, cu, cd, cz, v0, v1, v2, v3,
    wf, xf, uf, df, zf, wm, xm, um, dm, zm, wl, xl, ul, dl, zl,
    first, defect, dmid, dlow, cedge, send_a, send_b,
    ks, rs, sa, sb, km_s, rm_s, vm_s, kl_s, rl_s, vl_s, full, tmp, low, high,
):
    ylo, yhi = received("gy", got_a, got_b)
    early = split_views((wa, xa, ua, da, za), (w, cx, cu, cd, cz))
    early_v = stage_views((b0, b1, b2, b3), (v0, v1, v2, v3))
    others = []
    at, extra = 18, 16
    for lev, own_k, ghost_k, k_ref, own_r, ghost_r, r_ref, v_ref, refs in (
        (MID, km, gkm, km_s, rm, grm, rm_s, vm_s, (wm, xm, um, dm, zm)),
        (LOW, kl, gkl, kl_s, rl, grl, rl_s, vl_s, (wl, xl, ul, dl, zl)),
    ):
        k, r = View(k_ref, 8), View(r_ref, 0)
        own_rows(lev, k, Parts(lev, own_k, ghost_k), 4, 8, lev.own)
        own_rows(lev, r, Parts(lev, own_r, ghost_r), REACH, 8, lev.own)
        halos(lev, ylo, yhi, at, extra, (k, k), (r, r), 0, 8 + lev.own)
        at, extra = at + lev.n + 2, extra + lev.n
        clear(k, lev.rows, -8)
        clear(k, lev.rows, lev.span)
        fixup(k, lev, 0, lev.span)
        coef = [View(ref, 0) for ref in refs]
        setup(lev, k, coef, [(0, lev.span)], 1 if lev is MID else 3)
        others.append((lev, r, View(v_ref, 8), k, coef))
    strips = strip_views((wf, xf, uf, df, zf))
    (kl_v,), (kh_v,) = strip_bufs(ks)
    (rl_v,), (rh_v,) = strip_views((rs,))
    halos(FINE, ylo, yhi, 0, 0, (kl_v, kh_v), (rl_v, rh_v), 0, 136)
    for k, r, p_k, p_r, start, pad, kept in (
        (kl_v, rl_v, 8, 8, 0, -8, 16), (kh_v, rh_v, 120, 120, 128, 144, 120),
    ):
        side = 0 if start == 0 else 1
        own_rows(FINE, k, Parts(FINE, kz, gk), 4, p_k, 16)
        own_rows(FINE, r, Parts(FINE, rz, gr), REACH, p_r, 16)
        clear(k, FINE.rows, pad)
        fixup(k, FINE, start if side == 0 else 120, 24)
        setup(FINE, k, strips[side], [(start, 16)], 4)
        for number, (dst, src) in enumerate(zip(strips[side], early)):
            rows = FINE.work(REACH) + ([0, FINE.n + 2] if number == 1 else [])
            for i in rows:
                dst.set(i, kept, 8, src.get(i, kept, 8))
    bufs = strip_bufs(sa, sb)
    *late, vm, vl = late_smooth((rl_v, rh_v), early_v, bufs, strips, others, False)
    correction(vm, vl, tmp)
    whole = View(full, 8)
    for i in range(1, 17):
        m = (i - 1) // 4
        for p, size, v in ((0, 24, late[0]), (24, 48, early_v[3]), (72, 48, early_v[3]), (120, 24, late[1])):
            whole.set(i, p, size, STEP_WEIGHT * (v.get(i, p, size) + tmp[m, p : p + size]))
    fixup(whole, FINE, 8, 128, ghost=False)
    for most, p, size, coef in (
        (8, 8, 8, strips[0]), (1, 16, 56, early), (1, 72, 56, early), (8, 128, 8, strips[1]),
    ):
        for group in grouped(range(1, 17), most):
            i, before, after = near(group), near(group, -1), near(group, 1)
            _, x, u, d, z = [c.get(i, p, size) for c in coef]
            v = whole.get(i, p, size)
            image_z = z * (v - spin(v, LANES - 1)) + spin(z, 1) * (v - spin(v, 1))
            image = coef[1].get(before, p, size) * (v - whole.get(before, p, size))
            image = image + x * (v - whole.get(after, p, size))
            image = image + u * (v - whole.get(i, p + 1, size))
            image = image + d * (v - whole.get(i, p - 1, size))
            image = image + image_z
            defect[before, p - 8 : p - 8 + size] = rz[before, p - 8 : p - 8 + size] - image
            first[before, p - 8 : p - 8 + size] = v
    for p, size, coef in ((8, 8, strips[0]), (16, 112, early), (128, 8, strips[1])):
        cedge[p - 8 : p - 8 + size] = edges(coef[1].get(0, p, size), coef[1].get(16, p, size))
    sum_rows_mid(defect, tmp, dmid)
    dlow[...] = sum_rows_low(dmid, tmp)
    for out, is_low in ((low, True), (high, False)):
        edge = 0 if is_low else 3
        fine = join_slots([(defect[j if is_low else 15 - j], edge) for j in range(3)])
        for j in range(3):
            value, source = mid_piece(dmid, j, is_low)
            rows = slice(32 * j, 32 * j + 32)
            out[rows] = jnp.where(quarter((32, LANES)) == 3, move(value, source, 3), fine[rows])
            source = j if is_low else 3 - j
            rows = slice(96 + 8 * j, 104 + 8 * j)
            out[rows] = jnp.where(quarter((8, LANES)) == 3, move(dlow[...], source, 3), fine[rows])
        out[120:128] = fine[120:128]
        line = 0 if is_low else 15
        out[128:160] = join_slots([(first[line, 32 * g : 32 * g + 32], edge) for g in range(4)])
    ship("gx", low, high, send_a, send_b)


def fourth_kernel(
    got_a, got_b, first, defect, dmid, dlow, cedge,
    gf, gm, gl, d0, d15, m0, m3, lows, send_a, send_b, tmp, low, high,
):
    left, right = received("gx", got_a, got_b)
    face = cedge[...]
    group = quarter((128, LANES))
    other = [ghost_of(left[128:160], right[128:160], g) for g in range(4)]
    mine = face * jnp.concatenate(other, axis=0)
    theirs = face * edges(first[0], first[15])
    d0[...] = defect[0] + jnp.where(group == 0, mine, 0.0)
    d15[...] = defect[15] + jnp.where(group == 3, mine, 0.0)
    sums = []
    for n, value in enumerate((mine, theirs)):
        tmp[n, 0:128, :] = value
        mid = fourths(tmp.at[n], 32)
        tmp[n + 2, 0:32, :] = mid
        sums.append((mid, fourths(tmp.at[n + 2], 8)))
    group = quarter((32, LANES))
    m0[...] = dmid[0] + jnp.where(group == 0, sums[0][0], 0.0)
    m3[...] = dmid[3] + jnp.where(group == 3, sums[0][0], 0.0)
    lows[...] = dlow[...] + sums[0][1]
    for j in range(3):
        for out, rows, slot, add in (
            (gf, slice(0, 128), j, theirs),
            (gm, slice(32 * j, 32 * j + 32), 3, sums[1][0]),
            (gl, slice(96 + 8 * j, 104 + 8 * j), 3, sums[1][1]),
        ):
            value = ghost_of(left[rows], right[rows], slot)
            out[j] = value + add if j == 0 else value
    tiles = ([], [])
    for lev, r, ghost in (
        (FINE, Parts(FINE, defect, gf, {1: d0, 16: d15}), gf),
        (MID, Parts(MID, dmid, gm, {1: m0, 4: m3}), gm),
        (LOW, Parts(LOW, lows, gl), gl),
    ):
        for side, p in ((0, 8), (1, lev.own)):
            tiles[side].extend(r.get(i, p, 8) for i in range(1, lev.n + 1))
            a, b, c = [r.get(lev.ghost + j, p, 8) for j in range(3)]
            tiles[side].extend([two_in_one(a, b), c])
    pack_y(tiles[0], tiles[1], low, high)
    ship("gy", low, high, send_a, send_b)


def residual_halos(lev, ylo, yhi, at, r, p_low, p_high):
    for side, ref in ((0, ylo), (1, yhi)):
        start = p_low if side == 0 else p_high
        for i in range(lev.n):
            r[side].set(1 + i, start, 8, unpack_y(ref, at + i))
        both = unpack_y(ref, at + lev.n)
        r[side].set(lev.ghost, start, 8, one_of_two(both, 0))
        r[side].set(lev.ghost + 1, start, 8, one_of_two(both, 1))
        r[side].set(lev.ghost + 2, start, 8, unpack_y(ref, at + lev.n + 1))


def early_again_kernel(
    defect, gf, d0, d15, wa, xa, ua, da, za, w, cx, cu, cd, cz, b0, b1, b2, b3, v0, v1, v2, v3
):
    coef = split_views((wa, xa, ua, da, za), (w, cx, cu, cd, cz))
    views = stage_views((b0, b1, b2, b3), (v0, v1, v2, v3))
    early_smooth(Parts(FINE, defect, gf, {1: d0, 16: d15}), views, coef, False)


def fifth_kernel(
    wf, xf, uf, df, zf, wm, xm, um, dm, zm, wl, xl, ul, dl, zl,
    first, defect, dmid, gf, gm, gl, d0, d15, m0, m3, lows,
    b0, b1, b2, b3, v0, v1, v2, v3, got_a, got_b, out,
    rs, sa, sb, rm_s, va_m, vb_m, rl_s, va_l, vb_l, tmp, out_s, sems,
):
    ylo, yhi = received("gy", got_a, got_b)
    early_v = stage_views((b0, b1, b2, b3), (v0, v1, v2, v3))
    others = []
    at = 18
    for lev, parts, r_ref, va, vb, refs in (
        (MID, Parts(MID, dmid, gm, {1: m0, 4: m3}), rm_s, va_m, vb_m, (wm, xm, um, dm, zm)),
        (LOW, Parts(LOW, lows, gl), rl_s, va_l, vb_l, (wl, xl, ul, dl, zl)),
    ):
        r = View(r_ref, 0)
        own_rows(lev, r, parts, REACH, 8, lev.own)
        residual_halos(lev, ylo, yhi, at, (r, r), 0, 8 + lev.own)
        at += lev.n + 2
        coef = [View(ref, 0) for ref in refs]
        others.append((lev, r, View(va, 8), View(vb, 8), coef))
    strips = strip_views((wf, xf, uf, df, zf))
    (rl_v,), (rh_v,) = strip_views((rs,))
    parts = Parts(FINE, defect, gf, {1: d0, 16: d15})
    own_rows(FINE, rl_v, parts, REACH, 8, 16)
    own_rows(FINE, rh_v, parts, REACH, 120, 16)
    residual_halos(FINE, ylo, yhi, 0, (rl_v, rh_v), 0, 136)
    bufs = strip_bufs(sa, sb)
    *late, vm, vl = late_smooth((rl_v, rh_v), early_v, bufs, strips, others, True)
    correction(vm, vl, tmp)
    flat = out_s.reshape(2048, LANES)
    copies = []
    for x in range(16):
        pieces = []
        for p, size, v in ((8, 16, late[0]), (24, 96, early_v[3]), (120, 16, late[1])):
            part = v.get(1 + x, p, size) + tmp[x // 4, p : p + size]
            pieces.append(first[x, p - 8 : p - 8 + size] + STEP_WEIGHT * part)
        total = jnp.concatenate(pieces, axis=0).T
        for q in range(4):
            flat[pl.ds(16 * q + x, DEPTH, stride=64), :] = total[DEPTH * q : DEPTH * q + DEPTH]
        if x % 8 == 7:
            for q in range(4):
                rows = pl.ds(16 * q + x - 7, 8)
                copies.append(
                    pltpu.make_async_copy(out_s.at[:, rows], out.at[:, rows], sems.at[len(copies)])
                )
                copies[-1].start()
    for copy in copies:
        copy.wait()


def shape(*dims):
    return jax.ShapeDtypeStruct(dims, jnp.float32)


def scratch(*dims):
    return pltpu.VMEM(dims, jnp.float32)


def swap(a, b, axis):
    out = []
    for start, value in ((0, a), (1, b)):
        pairs = []
        for i in range(start, lax.axis_size(axis) - 1, 2):
            pairs += [(i, i + 1), (i + 1, i)]
        out.append(lax.ppermute(value, axis, pairs) if pairs else jnp.zeros_like(value))
    return out


def on_device(rhs, kappa):
    def call(body, outs, scratches=(), flops=10**6, ins=None, out=None, room=20):
        specs = {} if ins is None else {"in_specs": ins}
        if out is not None:
            specs["out_specs"] = out
        return pl.pallas_call(
            body,
            out_shape=outs,
            **specs,
            scratch_shapes=list(scratches),
            compiler_params=params(room),
            cost_estimate=cost(flops),
        )

    n = FINE.rows
    own = [shape(16, 128, LANES), shape(4, 32, LANES), shape(8, LANES)]
    tmp = scratch(5, 144, LANES)
    outs = [own[0], own[0], own[1], own[1], own[2], own[2]] + [shape(304, LANES)] * 2
    held = scratch(2048, LANES)
    far = pl.BlockSpec(memory_space=pltpu.HBM)
    bufs = [tmp, held, held] + [scratch(304, LANES)] * 2 + [pltpu.SemaphoreType.DMA((8,))]
    kz, rz, km, rm, kl, rl, *sends = call(first_kernel, outs, bufs, ins=[far, far], room=51)(
        rhs.reshape(2048, LANES), kappa.reshape(2048, LANES)
    )
    inside = [shape(16, 128, LANES)] * 4
    outs = [shape(16, 112, LANES)] * 5 + inside
    safe = call(safe_kernel, outs, (), 10**8)(kz, rz)
    kl, *safe = lax.optimization_barrier((kl, *safe))
    gots = swap(*sends, "gx")
    outs = [shape(g, width, LANES) for width in (128, 32, 8) for g in (4, 3)]
    bufs = [scratch(30, 8, LANES)] * 2
    *ghosts, send_a, send_b = call(second_kernel, outs + [shape(30, 8, LANES)] * 2, bufs)(
        *gots, kz, rz, km, rm, kl, rl
    )
    gk, gr = ghosts[:2]
    gots = swap(send_a, send_b, "gy")
    outs = [shape(n, 112, LANES)] * 5 + [shape(n, 128, LANES)] * 4
    early = call(early_kernel, outs, [scratch(n, 128, LANES)], 10**8)(
        kz, rz, gk, gr, *safe
    )
    strip = shape(n, 2, 24, LANES)
    outs = [strip] * 5
    for lev in (MID, LOW):
        outs += [shape(lev.rows, lev.span, LANES)] * 5
    outs += [own[0], own[0], own[1], own[2], shape(128, LANES)] + [shape(160, LANES)] * 2
    strip_scratch = [scratch(n, 2, 48, LANES), scratch(n, 2, 24, LANES)]
    bufs = strip_scratch + [scratch(n, 2, 48, LANES)] * 2
    for lev in (MID, LOW):
        wide = scratch(lev.rows, lev.span + 16, LANES)
        bufs += [wide, scratch(lev.rows, lev.span, LANES), wide]
    bufs += [scratch(n, 160, LANES), tmp] + [scratch(160, LANES)] * 2
    results = call(third_kernel, outs, bufs)(
        kz, rz, km, rm, kl, rl, *ghosts, *gots, *safe, *early
    )
    state = results[:15]
    first, defect, dmid, dlow, cedge, send_a, send_b = results[15:]
    gots = swap(send_a, send_b, "gx")
    again = call(safe_again_kernel, inside, (), 10**8)(defect, *safe[:5])
    dlow, *again = lax.optimization_barrier((dlow, *again))
    outs = [shape(3, width, LANES) for width in (128, 32, 8)]
    outs += [shape(128, LANES)] * 2 + [shape(32, LANES)] * 2 + [shape(8, LANES)]
    bufs = [tmp] + [scratch(14, 8, LANES)] * 2
    *halo, send_a, send_b = call(fourth_kernel, outs + [shape(14, 8, LANES)] * 2, bufs)(
        *gots, first, defect, dmid, dlow, cedge
    )
    gf, gm, gl, d0, d15, m0, m3, lows = halo
    gots = swap(send_a, send_b, "gy")
    inner = call(early_again_kernel, [shape(n, 128, LANES)] * 4, (), 10**8)(
        defect, gf, d0, d15, *safe[:5], *early[:5], *again
    )
    bufs = [strip_scratch[1]] + [scratch(n, 2, 48, LANES)] * 2
    for lev in (MID, LOW):
        wide = scratch(lev.rows, lev.span + 16, LANES)
        bufs += [scratch(lev.rows, lev.span, LANES), wide, wide]
    bufs += [tmp, scratch(*rhs.shape), pltpu.SemaphoreType.DMA((8,))]
    return call(fifth_kernel, shape(*rhs.shape), bufs, out=far)(
        *state, first, defect, dmid, *halo, *again, *inner, *gots
    )


def solution(mesh):
    return jax.shard_map(
        on_device,
        mesh=mesh,
        in_specs=(P("groups", "gx", "gy"), P("groups", "gx", "gy")),
        out_specs=P("groups", "gx", "gy"),
        check_vma=False,
    )
```

```python
import jax
import jax.numpy as jnp
from jax import lax
from jax.experimental import pallas as pl
from jax.experimental.pallas import tpu as pltpu
from jax.sharding import PartitionSpec as P

JACOBI_WEIGHT = 0.8
STEP_WEIGHT = 0.6
LANES = 128
DEPTH = 32
QUARTERS = 4
REACH = 3


class Level:
    def __init__(self, rows, width, flat, up):
        self.n = rows
        self.own = width
        self.span = width + 16
        self.flat = flat
        self.up = up
        self.rows = rows + 7
        self.ghost = rows + 3

    def work(self, ghosts):
        return list(range(1, self.n + 1)) + list(range(self.ghost, self.ghost + ghosts))

    def faces(self):
        return [i for i in range(self.rows - 1) if i != self.n + 1]


LEVELS = (Level(16, 128, 1.0, 1.0), Level(4, 32, 4.0, 16.0), Level(1, 8, 16.0, 256.0))
FINE, MID, LOW = LEVELS
INNER = [(16, 56), (72, 56)]
SAFE, SAFE_FACES = range(2, 16), range(1, 16)


def grouped(rows, most):
    out = []
    for i in rows:
        if out and len(out[-1]) < most and out[-1][-1] == i - 1:
            out[-1].append(i)
        else:
            out.append([i])
    return out


def near(group, by=0):
    if len(group) == 1:
        return group[0] + by
    return slice(group[0] + by, group[-1] + 1 + by)


def spin(value, shift):
    return pltpu.roll(value, shift, value.ndim - 1)


class View:
    def __init__(self, ref, shift, side=None):
        self.ref, self.shift, self.side = ref, shift, side

    def at(self, i, p, size):
        rows = slice(p + self.shift, p + self.shift + size)
        return (i, rows) if self.side is None else (i, self.side, rows)

    def get(self, i, p, size):
        return self.ref[self.at(i, p, size)]

    def set(self, i, p, size, value):
        self.ref[self.at(i, p, size)] = value


class Split:
    def __init__(self, rows, inside, outside):
        self.rows, self.inside, self.outside = rows, inside, outside

    def get(self, i, p, size):
        return (self.inside if i in self.rows else self.outside).get(i, p, size)

    def set(self, i, p, size, value):
        self.outside.set(i, p, size, value)


def split_views(inside, outside):
    out = []
    for n, (a, b) in enumerate(zip(inside, outside)):
        out.append(Split(SAFE_FACES if n == 1 else SAFE, View(a, -16), View(b, -16)))
    return out


def stage_rows(number):
    return range(2 + number, 16 - number)


def stage_views(inside, outside):
    return [
        Split(stage_rows(n), View(a, -8), View(b, -8))
        for n, (a, b) in enumerate(zip(inside, outside))
    ]


class Parts:
    def __init__(self, lev, own, ghost, swap=None):
        self.lev, self.own, self.ghost, self.swap = lev, own, ghost, swap or {}

    def get(self, i, p, size):
        rows = slice(p - 8, p - 8 + size)
        if i >= self.lev.ghost:
            return self.ghost[i - self.lev.ghost, rows]
        if i in self.swap:
            return self.swap[i][rows]
        return self.own[rows] if self.lev.n == 1 else self.own[i - 1, rows]


def params(mib=20):
    return pltpu.CompilerParams(vmem_limit_bytes=mib << 20)


def cost(flops):
    return pl.CostEstimate(flops=flops, bytes_accessed=8 << 20, transcendentals=0)


def quarter(shape):
    return lax.broadcasted_iota(jnp.int32, shape, 1) // DEPTH


def sublane(shape):
    return lax.broadcasted_iota(jnp.int32, shape, 0)


class Pick:
    def __init__(self, first, second, use_first):
        self.first, self.second, self.use_first = first, second, use_first

    def __getitem__(self, at):
        return jnp.where(self.use_first, self.first[at], self.second[at])


def is_even(axis):
    return lax.axis_index(axis) % 2 == 0


def received(axis, a, b):
    even = is_even(axis)
    return Pick(b, a, even), Pick(a, b, even)


def ship(axis, low, high, a, b):
    even = is_even(axis)
    below, above = low[...], high[...]
    a[...] = jnp.where(even, above, below)
    b[...] = jnp.where(even, below, above)


def move(value, source, target):
    shift = DEPTH * ((target - source) % QUARTERS)
    return pltpu.roll(value, shift, 1) if shift else value


def join_slots(pieces):
    out = None
    for slot, (value, source) in enumerate(pieces):
        part = move(value, source, slot)
        out = part if out is None else jnp.where(quarter(part.shape) == slot, part, out)
    return out


def edges(left, right):
    group = quarter(left.shape)
    return jnp.where(group == 0, left, jnp.where(group == 3, right, 0.0))


def ghost_of(from_left, from_right, slot):
    return edges(move(from_left, slot, 0), move(from_right, slot, 3))


def two_in_one(a, b):
    group = quarter(a.shape)
    up, down = pltpu.roll(b, DEPTH, 1), pltpu.roll(b, LANES - DEPTH, 1)
    return jnp.where(group == 1, up, jnp.where(group == 2, down, a))


def one_of_two(v, second):
    if not second:
        return edges(v, v)
    return edges(pltpu.roll(v, LANES - DEPTH, 1), pltpu.roll(v, DEPTH, 1))


def mid_piece(ref, j, low):
    index = j if low else 15 - j
    return ref[index % 4], index // 4


def fourths(tmp, size):
    out = tmp[pl.ds(0, size, stride=4), :]
    for t in range(1, 4):
        out = out + tmp[pl.ds(t, size, stride=4), :]
    return out


def sum_rows_mid(rows_ref, tmp, out_ref):
    for m in range(4):
        total = rows_ref[4 * m] + rows_ref[4 * m + 1]
        tmp[m, 0:128, :] = total + rows_ref[4 * m + 2] + rows_ref[4 * m + 3]
        out_ref[m] = fourths(tmp.at[m], 32)


def sum_rows_low(mid_ref, tmp):
    tmp[4, 0:32, :] = mid_ref[0] + mid_ref[1] + mid_ref[2] + mid_ref[3]
    return fourths(tmp.at[4], 8)


def fixup(v, lev, p, size, ghost=True):
    group = quarter((size, LANES))
    first, last = v.get(1, p, size), v.get(lev.n, p, size)
    edge = v.get(lev.ghost, p, size) if ghost else jnp.zeros((size, LANES), jnp.float32)
    v.set(0, p, size, jnp.where(group == 0, edge, pltpu.roll(last, DEPTH, 1)))
    v.set(lev.n + 1, p, size, jnp.where(group == 3, edge, pltpu.roll(first, LANES - DEPTH, 1)))
    if ghost:
        v.set(lev.n + 2, p, size, jnp.where(group == 0, first, last))


def harmonic(a, b):
    total = a + b
    return 2.0 * a * b / jnp.where(total > 0, total, 1.0)


def setup(lev, k, coef, parts, most=1, faces=None, work=None):
    w, cx, cu, cd, cz = coef
    for group in grouped(lev.faces() if faces is None else faces, most):
        i, j = near(group), near(group, 1)
        for p, size in parts:
            cx.set(i, p, size, lev.flat * harmonic(k.get(i, p, size), k.get(j, p, size)))
    for group in grouped(lev.work(REACH) if work is None else work, most):
        i = near(group)
        for p, size in parts:
            here = k.get(i, p, size)
            above = lev.flat * harmonic(here, k.get(i, p + 1, size))
            below = lev.flat * harmonic(k.get(i, p - 1, size), here)
            z = lax.broadcasted_iota(jnp.int32, here.shape, here.ndim - 1) % DEPTH
            up = lev.up * harmonic(here, spin(here, LANES - 1))
            up = jnp.where(z == DEPTH - 1, 0.0, up)
            cu.set(i, p, size, above)
            cd.set(i, p, size, below)
            cz.set(i, p, size, up)
    for group in grouped(lev.work(REACH) if work is None else work, most):
        i = near(group)
        for p, size in parts:
            up = cz.get(i, p, size)
            diagonal = cx.get(near(group, -1), p, size) + cx.get(i, p, size)
            diagonal = diagonal + (cd.get(i, p, size) + cu.get(i, p, size)) + (spin(up, 1) + up)
            good = diagonal > 0
            value = jnp.where(good, JACOBI_WEIGHT / jnp.where(good, diagonal, 1.0), 0.0)
            w.set(i, p, size, value)


def begin(lev, r, v, coef, parts, most=1, rows=None):
    for group in grouped(lev.work(REACH) if rows is None else rows, most):
        i = near(group)
        for p, size in parts:
            v.set(i, p, size, coef[0].get(i, p, size) * r.get(i, p, size))


def sweep(lev, r, v, out, coef, parts, ghosts, most=1, rows=None):
    w, cx, cu, cd, cz = coef
    for group in grouped(lev.work(ghosts) if rows is None else rows, most):
        i, before, after = near(group), near(group, -1), near(group, 1)
        for p, size in parts:
            here = v.get(i, p, size)
            up = cz.get(i, p, size)
            acc = r.get(i, p, size) + cx.get(before, p, size) * v.get(before, p, size)
            acc = acc + cx.get(i, p, size) * v.get(after, p, size)
            acc = acc + cu.get(i, p, size) * v.get(i, p + 1, size)
            acc = acc + cd.get(i, p, size) * v.get(i, p - 1, size)
            acc = acc + up * spin(here, LANES - 1) + spin(up * here, 1)
            out.set(i, p, size, (1.0 - JACOBI_WEIGHT) * here + w.get(i, p, size) * acc)


def clear(v, rows, p):
    for i in range(rows) if isinstance(rows, int) else rows:
        v.set(i, p, 8, jnp.zeros((8, LANES), jnp.float32))


def late_smooth(fine_r, early, bufs, fine_coef, others, own_only):
    jobs = []
    for side, start in ((0, 0), (1, 120)):
        for v in bufs[side]:
            clear(v, FINE.rows, -8 if side == 0 else 144)
        jobs.append((FINE, fine_r[side], list(bufs[side]), fine_coef[side], start, 24, 3, side))
    for lev, r, va, vb, coef in others:
        for v in (va, vb):
            clear(v, lev.rows, -8)
            clear(v, lev.rows, lev.span)
        jobs.append((lev, r, [va, vb], coef, 0, lev.span, 1 if lev is MID else 3, None))
    for lev, r, pair, coef, start, size, most, side in jobs:
        begin(lev, r, pair[0], coef, [(start, size)], most)
    for number in range(3):
        for lev, r, pair, coef, start, size, most, side in jobs:
            if side is not None:
                tile = BEYOND[side]
                for i in lev.work(REACH - number):
                    pair[0].set(i, tile, 8, early[number].get(i, tile, 8))
            fixup(pair[0], lev, start, size)
        for lev, r, pair, coef, start, size, most, side in jobs:
            if own_only and number == 2:
                size = lev.own if side is None else 16
                start = 120 if side == 1 else 8
            sweep(lev, r, pair[0], pair[1], coef, [(start, size)], REACH - 1 - number, most)
            pair.reverse()
    return [job[2][0] for job in jobs]


def early_smooth(r, views, coef, safe):
    stages = []
    for number in range(4):
        inside = stage_rows(number)
        every = FINE.work(REACH - number)
        stages.append([i for i in every if (i in inside) == safe])
    for n, v in enumerate(views[:3]):
        for p in (8, 128):
            clear(v, stage_rows(n) if safe else FINE.rows, p)
    begin(FINE, r, views[0], coef, INNER, 1, stages[0])
    for n in range(3):
        if not safe:
            fixup(views[n], FINE, 16, 112)
        sweep(FINE, r, views[n], views[n + 1], coef, INNER, 0, 1, stages[n + 1])


BEYOND = (24, 112)


def expand(view, row, lev, tmp):
    part = view.get(row, 6, lev.span // 4)
    for t in range(4):
        tmp[pl.ds(t, lev.span // 4, stride=4), :] = part


def correction(vm, vl, tmp):
    expand(vl, 1, MID, tmp.at[4])
    for m in range(4):
        value = vm.get(1 + m, 0, MID.span) + tmp[4, 0 : MID.span]
        vm.set(1 + m, 0, MID.span, value)
        expand(vm, 1 + m, FINE, tmp.at[m])


def pack_y(tiles_low, tiles_high, low, high):
    for n in range((len(tiles_low) + 1) // 2):
        for tiles, out, is_low in ((tiles_low, low, True), (tiles_high, high, False)):
            a = tiles[2 * n]
            if 2 * n + 1 < len(tiles):
                b = pltpu.roll(tiles[2 * n + 1], 4, 0)
                first = sublane((8, LANES)) < 4
                a = jnp.where(first, a, b) if is_low else jnp.where(first, b, a)
            out[n] = a


def unpack_y(ref, n):
    value = ref[n // 2]
    return pltpu.roll(value, 4, 0) if n % 2 else value


def first_kernel(
    rhs, kappa, kz, rz, km, rm, kl, rl, send_a, send_b, tmp, k_in, r_in, low, high, sems
):
    copies = []
    for n, (source, target) in enumerate(((kappa, k_in), (rhs, r_in))):
        for c in range(4):
            rows = slice(512 * c, 512 * c + 512)
            copy = pltpu.make_async_copy(source.at[rows], target.at[rows], sems.at[4 * n + c])
            copies.append(copy)
    for copy in copies[:6]:
        copy.start()
    for n, (source, target, mid, low_level) in enumerate(((k_in, kz, km, kl), (r_in, rz, rm, rl))):
        for c, copy in enumerate(copies[4 * n : 4 * n + 4]):
            copy.wait()
            if n == 0 and c < 2:
                copies[6 + c].start()
        for x in range(16):
            rows = [source[pl.ds(16 * q + x, DEPTH, stride=64), :] for q in range(4)]
            target[x] = jnp.concatenate(rows, axis=0).T
        sum_rows_mid(target, tmp, mid)
        if n == 0:
            for m in range(4):
                mid[m] = mid[m] * (1.0 / 16.0)
            low_level[...] = sum_rows_low(mid, tmp) * (1.0 / 16.0)
        else:
            low_level[...] = sum_rows_low(mid, tmp)
        for out, is_low in ((low, True), (high, False)):
            edge = 0 if is_low else 3
            line = [j if is_low else 15 - j for j in range(4)]
            if n == 0:
                out[0:128] = join_slots([(kz[j], edge) for j in line])
                out[288:296] = kl[...]
                continue
            fine = join_slots([(rz[j], edge) for j in line[:3]])
            for j in range(4):
                value, source_q = mid_piece(km, j, is_low)
                out[128 + 32 * j : 160 + 32 * j] = jnp.where(
                    quarter((32, LANES)) == 3, move(value, source_q, 3), fine[32 * j : 32 * j + 32]
                )
            out[256:288] = join_slots([mid_piece(rm, j, is_low) for j in range(3)])
            out[296:304] = rl[...]
    ship("gx", low, high, send_a, send_b)


def second_kernel(
    got_a, got_b, kz, rz, km, rm, kl, rl, gk, gr, gkm, grm, gkl, grl, send_a, send_b, low, high
):
    left, right = received("gx", got_a, got_b)
    for j in range(4):
        gk[j] = ghost_of(left[0:128], right[0:128], j)
        rows = slice(128 + 32 * j, 160 + 32 * j)
        gkm[j] = ghost_of(left[rows], right[rows], 3)
        gkl[j] = edges(move(left[288:296], 3 - j, 0), move(right[288:296], j, 3))
    for j in range(3):
        gr[j] = ghost_of(left[128:256], right[128:256], j)
        grm[j] = ghost_of(left[256:288], right[256:288], j)
        grl[j] = edges(move(left[296:304], 3 - j, 0), move(right[296:304], j, 3))
    at = 0
    extra = 0
    row = sublane((8, LANES))
    for lev, k, r, ghost_k, ghost_r in (
        (FINE, kz, rz, gk, gr), (MID, km, rm, gkm, grm), (LOW, kl, rl, gkl, grl),
    ):
        for is_low, out in ((True, low), (False, high)):
            rows = slice(0, 8) if is_low else slice(lev.own - 8, lev.own)
            pairs = []
            for i in range(lev.n):
                pairs.append((k[rows], r[rows]) if lev.n == 1 else (k[i, rows], r[i, rows]))
            for a in (0, 2):
                rest = ghost_r[a, rows]
                rest = two_in_one(rest, ghost_r[a + 1, rows]) if a == 0 else rest
                pairs.append((two_in_one(ghost_k[a, rows], ghost_k[a + 1, rows]), rest))
            for i, (a, b) in enumerate(pairs):
                if is_low:
                    out[at + i] = jnp.where(row < 5, a, pltpu.roll(b, 5, 0))
                else:
                    out[at + i] = jnp.where(row >= 3, a, pltpu.roll(b, 3, 0))
            for i in range(lev.n):
                e = extra + i
                cell = slice(3, 4) if is_low else slice(lev.own - 4, lev.own - 3)
                out[27 + e // 8, e % 8 : e % 8 + 1] = r[cell] if lev.n == 1 else r[i, cell]
        at += lev.n + 2
        extra += lev.n
    ship("gy", low, high, send_a, send_b)


def halos(lev, ylo, yhi, at, extra, k, r, p_low, p_high):
    row = sublane((8, LANES))
    for side, ref in ((0, ylo), (1, yhi)):
        start = p_low if side == 0 else p_high
        for i in range(lev.n + 2):
            value = ref[at + i]
            if side == 0:
                a = jnp.where(row >= 3, value, 0.0)
                b = jnp.where(row >= 5, pltpu.roll(value, 5, 0), 0.0)
            else:
                a = jnp.where(row < 5, value, 0.0)
                b = jnp.where(row < 3, pltpu.roll(value, 3, 0), 0.0)
            if i < lev.n:
                k[side].set(1 + i, start, 8, a)
                r[side].set(1 + i, start, 8, b)
                e = extra + i
                cell = start + 4 if side == 0 else start + 3
                r[side].set(1 + i, cell, 1, ref[27 + e // 8, e % 8 : e % 8 + 1])
                continue
            for part in (0, 1):
                j = 2 * (i - lev.n) + part
                k[side].set(lev.ghost + j, start, 8, one_of_two(a, part))
                if j < REACH:
                    r[side].set(lev.ghost + j, start, 8, one_of_two(b, part))


def own_rows(lev, dst, src, ghosts, p, size):
    for i in lev.work(ghosts):
        dst.set(i, p, size, src.get(i, p, size))


def safe_kernel(kz, rz, w, cx, cu, cd, cz, v0, v1, v2, v3):
    coef = [View(ref, -16) for ref in (w, cx, cu, cd, cz)]
    setup(FINE, Parts(FINE, kz, None), coef, INNER, 1, SAFE_FACES, SAFE)
    early_smooth(Parts(FINE, rz, None), [View(ref, -8) for ref in (v0, v1, v2, v3)], coef, True)


def safe_again_kernel(defect, w, cx, cu, cd, cz, v0, v1, v2, v3):
    coef = [View(ref, -16) for ref in (w, cx, cu, cd, cz)]
    views = [View(ref, -8) for ref in (v0, v1, v2, v3)]
    early_smooth(Parts(FINE, defect, None), views, coef, True)


def early_kernel(
    kz, rz, gk, gr, wa, xa, ua, da, za, b0, b1, b2, b3,
    w, cx, cu, cd, cz, v0, v1, v2, v3, k_s,
):
    k = View(k_s, -8)
    own = Parts(FINE, kz, gk)
    edge = [i for i in FINE.work(4) if i not in SAFE]
    for i in edge:
        k.set(i, 8, 128, own.get(i, 8, 128))
    fixup(k, FINE, 8, 128)
    coef = split_views((wa, xa, ua, da, za), (w, cx, cu, cd, cz))
    faces = [i for i in FINE.faces() if i not in SAFE_FACES]
    setup(FINE, k, coef, INNER, 1, faces, [i for i in edge if i < FINE.ghost + REACH])
    views = stage_views((b0, b1, b2, b3), (v0, v1, v2, v3))
    early_smooth(Parts(FINE, rz, gr), views, coef, False)


def strip_views(refs):
    return [[View(ref, -120 * side, side) for ref in refs] for side in (0, 1)]


def strip_bufs(*refs):
    return [[View(ref, 8 - 112 * side, side) for ref in refs] for side in (0, 1)]


def third_kernel(
    kz, rz, km, rm, kl, rl, gk, gr, gkm, grm, gkl, grl, got_a, got_b,
    wa, xa, ua, da, za, b0, b1, b2, b3, w, cx, cu, cd, cz, v0, v1, v2, v3,
    wf, xf, uf, df, zf, wm, xm, um, dm, zm, wl, xl, ul, dl, zl,
    first, defect, dmid, dlow, cedge, send_a, send_b,
    ks, rs, sa, sb, km_s, rm_s, vm_s, kl_s, rl_s, vl_s, full, tmp, low, high,
):
    ylo, yhi = received("gy", got_a, got_b)
    early = split_views((wa, xa, ua, da, za), (w, cx, cu, cd, cz))
    early_v = stage_views((b0, b1, b2, b3), (v0, v1, v2, v3))
    others = []
    at, extra = 18, 16
    for lev, own_k, ghost_k, k_ref, own_r, ghost_r, r_ref, v_ref, refs in (
        (MID, km, gkm, km_s, rm, grm, rm_s, vm_s, (wm, xm, um, dm, zm)),
        (LOW, kl, gkl, kl_s, rl, grl, rl_s, vl_s, (wl, xl, ul, dl, zl)),
    ):
        k, r = View(k_ref, 8), View(r_ref, 0)
        own_rows(lev, k, Parts(lev, own_k, ghost_k), 4, 8, lev.own)
        own_rows(lev, r, Parts(lev, own_r, ghost_r), REACH, 8, lev.own)
        halos(lev, ylo, yhi, at, extra, (k, k), (r, r), 0, 8 + lev.own)
        at, extra = at + lev.n + 2, extra + lev.n
        clear(k, lev.rows, -8)
        clear(k, lev.rows, lev.span)
        fixup(k, lev, 0, lev.span)
        coef = [View(ref, 0) for ref in refs]
        setup(lev, k, coef, [(0, lev.span)], 1 if lev is MID else 3)
        others.append((lev, r, View(v_ref, 8), k, coef))
    strips = strip_views((wf, xf, uf, df, zf))
    (kl_v,), (kh_v,) = strip_bufs(ks)
    (rl_v,), (rh_v,) = strip_views((rs,))
    halos(FINE, ylo, yhi, 0, 0, (kl_v, kh_v), (rl_v, rh_v), 0, 136)
    for k, r, p_k, p_r, start, pad, kept in (
        (kl_v, rl_v, 8, 8, 0, -8, 16), (kh_v, rh_v, 120, 120, 128, 144, 120),
    ):
        side = 0 if start == 0 else 1
        own_rows(FINE, k, Parts(FINE, kz, gk), 4, p_k, 16)
        own_rows(FINE, r, Parts(FINE, rz, gr), REACH, p_r, 16)
        clear(k, FINE.rows, pad)
        fixup(k, FINE, start if side == 0 else 120, 24)
        setup(FINE, k, strips[side], [(start, 16)], 4)
        for number, (dst, src) in enumerate(zip(strips[side], early)):
            rows = FINE.work(REACH) + ([0, FINE.n + 2] if number == 1 else [])
            for i in rows:
                dst.set(i, kept, 8, src.get(i, kept, 8))
    bufs = strip_bufs(sa, sb)
    *late, vm, vl = late_smooth((rl_v, rh_v), early_v, bufs, strips, others, False)
    correction(vm, vl, tmp)
    whole = View(full, 8)
    for i in range(1, 17):
        m = (i - 1) // 4
        for p, size, v in ((0, 24, late[0]), (24, 48, early_v[3]), (72, 48, early_v[3]), (120, 24, late[1])):
            whole.set(i, p, size, STEP_WEIGHT * (v.get(i, p, size) + tmp[m, p : p + size]))
    fixup(whole, FINE, 8, 128, ghost=False)
    for most, p, size, coef in (
        (8, 8, 8, strips[0]), (1, 16, 56, early), (1, 72, 56, early), (8, 128, 8, strips[1]),
    ):
        for group in grouped(range(1, 17), most):
            i, before, after = near(group), near(group, -1), near(group, 1)
            _, x, u, d, z = [c.get(i, p, size) for c in coef]
            v = whole.get(i, p, size)
            image_z = z * (v - spin(v, LANES - 1)) + spin(z, 1) * (v - spin(v, 1))
            image = coef[1].get(before, p, size) * (v - whole.get(before, p, size))
            image = image + x * (v - whole.get(after, p, size))
            image = image + u * (v - whole.get(i, p + 1, size))
            image = image + d * (v - whole.get(i, p - 1, size))
            image = image + image_z
            defect[before, p - 8 : p - 8 + size] = rz[before, p - 8 : p - 8 + size] - image
            first[before, p - 8 : p - 8 + size] = v
    for p, size, coef in ((8, 8, strips[0]), (16, 112, early), (128, 8, strips[1])):
        cedge[p - 8 : p - 8 + size] = edges(coef[1].get(0, p, size), coef[1].get(16, p, size))
    sum_rows_mid(defect, tmp, dmid)
    dlow[...] = sum_rows_low(dmid, tmp)
    for out, is_low in ((low, True), (high, False)):
        edge = 0 if is_low else 3
        fine = join_slots([(defect[j if is_low else 15 - j], edge) for j in range(3)])
        for j in range(3):
            value, source = mid_piece(dmid, j, is_low)
            rows = slice(32 * j, 32 * j + 32)
            out[rows] = jnp.where(quarter((32, LANES)) == 3, move(value, source, 3), fine[rows])
            source = j if is_low else 3 - j
            rows = slice(96 + 8 * j, 104 + 8 * j)
            out[rows] = jnp.where(quarter((8, LANES)) == 3, move(dlow[...], source, 3), fine[rows])
        out[120:128] = fine[120:128]
        line = 0 if is_low else 15
        out[128:160] = join_slots([(first[line, 32 * g : 32 * g + 32], edge) for g in range(4)])
    ship("gx", low, high, send_a, send_b)


def fourth_kernel(
    got_a, got_b, first, defect, dmid, dlow, cedge,
    gf, gm, gl, d0, d15, m0, m3, lows, send_a, send_b, tmp, low, high,
):
    left, right = received("gx", got_a, got_b)
    face = cedge[...]
    group = quarter((128, LANES))
    other = [ghost_of(left[128:160], right[128:160], g) for g in range(4)]
    mine = face * jnp.concatenate(other, axis=0)
    theirs = face * edges(first[0], first[15])
    d0[...] = defect[0] + jnp.where(group == 0, mine, 0.0)
    d15[...] = defect[15] + jnp.where(group == 3, mine, 0.0)
    sums = []
    for n, value in enumerate((mine, theirs)):
        tmp[n, 0:128, :] = value
        mid = fourths(tmp.at[n], 32)
        tmp[n + 2, 0:32, :] = mid
        sums.append((mid, fourths(tmp.at[n + 2], 8)))
    group = quarter((32, LANES))
    m0[...] = dmid[0] + jnp.where(group == 0, sums[0][0], 0.0)
    m3[...] = dmid[3] + jnp.where(group == 3, sums[0][0], 0.0)
    lows[...] = dlow[...] + sums[0][1]
    for j in range(3):
        for out, rows, slot, add in (
            (gf, slice(0, 128), j, theirs),
            (gm, slice(32 * j, 32 * j + 32), 3, sums[1][0]),
            (gl, slice(96 + 8 * j, 104 + 8 * j), 3, sums[1][1]),
        ):
            value = ghost_of(left[rows], right[rows], slot)
            out[j] = value + add if j == 0 else value
    tiles = ([], [])
    for lev, r, ghost in (
        (FINE, Parts(FINE, defect, gf, {1: d0, 16: d15}), gf),
        (MID, Parts(MID, dmid, gm, {1: m0, 4: m3}), gm),
        (LOW, Parts(LOW, lows, gl), gl),
    ):
        for side, p in ((0, 8), (1, lev.own)):
            tiles[side].extend(r.get(i, p, 8) for i in range(1, lev.n + 1))
            a, b, c = [r.get(lev.ghost + j, p, 8) for j in range(3)]
            tiles[side].extend([two_in_one(a, b), c])
    pack_y(tiles[0], tiles[1], low, high)
    ship("gy", low, high, send_a, send_b)


def residual_halos(lev, ylo, yhi, at, r, p_low, p_high):
    for side, ref in ((0, ylo), (1, yhi)):
        start = p_low if side == 0 else p_high
        for i in range(lev.n):
            r[side].set(1 + i, start, 8, unpack_y(ref, at + i))
        both = unpack_y(ref, at + lev.n)
        r[side].set(lev.ghost, start, 8, one_of_two(both, 0))
        r[side].set(lev.ghost + 1, start, 8, one_of_two(both, 1))
        r[side].set(lev.ghost + 2, start, 8, unpack_y(ref, at + lev.n + 1))


def early_again_kernel(
    defect, gf, d0, d15, wa, xa, ua, da, za, w, cx, cu, cd, cz, b0, b1, b2, b3, v0, v1, v2, v3
):
    coef = split_views((wa, xa, ua, da, za), (w, cx, cu, cd, cz))
    views = stage_views((b0, b1, b2, b3), (v0, v1, v2, v3))
    early_smooth(Parts(FINE, defect, gf, {1: d0, 16: d15}), views, coef, False)


def fifth_kernel(
    wf, xf, uf, df, zf, wm, xm, um, dm, zm, wl, xl, ul, dl, zl,
    first, defect, dmid, gf, gm, gl, d0, d15, m0, m3, lows,
    b0, b1, b2, b3, v0, v1, v2, v3, got_a, got_b, out,
    rs, sa, sb, rm_s, va_m, vb_m, rl_s, va_l, vb_l, tmp, out_s, sems,
):
    ylo, yhi = received("gy", got_a, got_b)
    early_v = stage_views((b0, b1, b2, b3), (v0, v1, v2, v3))
    others = []
    at = 18
    for lev, parts, r_ref, va, vb, refs in (
        (MID, Parts(MID, dmid, gm, {1: m0, 4: m3}), rm_s, va_m, vb_m, (wm, xm, um, dm, zm)),
        (LOW, Parts(LOW, lows, gl), rl_s, va_l, vb_l, (wl, xl, ul, dl, zl)),
    ):
        r = View(r_ref, 0)
        own_rows(lev, r, parts, REACH, 8, lev.own)
        residual_halos(lev, ylo, yhi, at, (r, r), 0, 8 + lev.own)
        at += lev.n + 2
        coef = [View(ref, 0) for ref in refs]
        others.append((lev, r, View(va, 8), View(vb, 8), coef))
    strips = strip_views((wf, xf, uf, df, zf))
    (rl_v,), (rh_v,) = strip_views((rs,))
    parts = Parts(FINE, defect, gf, {1: d0, 16: d15})
    own_rows(FINE, rl_v, parts, REACH, 8, 16)
    own_rows(FINE, rh_v, parts, REACH, 120, 16)
    residual_halos(FINE, ylo, yhi, 0, (rl_v, rh_v), 0, 136)
    bufs = strip_bufs(sa, sb)
    *late, vm, vl = late_smooth((rl_v, rh_v), early_v, bufs, strips, others, True)
    correction(vm, vl, tmp)
    flat = out_s.reshape(2048, LANES)
    copies = []
    for x in range(16):
        pieces = []
        for p, size, v in ((8, 16, late[0]), (24, 96, early_v[3]), (120, 16, late[1])):
            part = v.get(1 + x, p, size) + tmp[x // 4, p : p + size]
            pieces.append(first[x, p - 8 : p - 8 + size] + STEP_WEIGHT * part)
        total = jnp.concatenate(pieces, axis=0).T
        for q in range(4):
            flat[pl.ds(16 * q + x, DEPTH, stride=64), :] = total[DEPTH * q : DEPTH * q + DEPTH]
        if x % 8 == 7:
            for q in range(4):
                rows = pl.ds(16 * q + x - 7, 8)
                copies.append(
                    pltpu.make_async_copy(out_s.at[:, rows], out.at[:, rows], sems.at[len(copies)])
                )
                copies[-1].start()
    for copy in copies:
        copy.wait()


def shape(*dims):
    return jax.ShapeDtypeStruct(dims, jnp.float32)


def scratch(*dims):
    return pltpu.VMEM(dims, jnp.float32)


def swap(a, b, axis):
    out = []
    for start, value in ((0, a), (1, b)):
        pairs = []
        for i in range(start, lax.axis_size(axis) - 1, 2):
            pairs += [(i, i + 1), (i + 1, i)]
        out.append(lax.ppermute(value, axis, pairs) if pairs else jnp.zeros_like(value))
    return out


def on_device(rhs, kappa):
    def call(body, outs, scratches=(), flops=10**6, ins=None, out=None, room=20):
        specs = {} if ins is None else {"in_specs": ins}
        if out is not None:
            specs["out_specs"] = out
        return pl.pallas_call(
            body,
            out_shape=outs,
            **specs,
            scratch_shapes=list(scratches),
            compiler_params=params(room),
            cost_estimate=cost(flops),
        )

    n = FINE.rows
    own = [shape(16, 128, LANES), shape(4, 32, LANES), shape(8, LANES)]
    tmp = scratch(5, 144, LANES)
    outs = [own[0], own[0], own[1], own[1], own[2], own[2]] + [shape(304, LANES)] * 2
    held = scratch(2048, LANES)
    far = pl.BlockSpec(memory_space=pltpu.HBM)
    bufs = [tmp, held, held] + [scratch(304, LANES)] * 2 + [pltpu.SemaphoreType.DMA((8,))]
    kz, rz, km, rm, kl, rl, *sends = call(first_kernel, outs, bufs, ins=[far, far], room=51)(
        rhs.reshape(2048, LANES), kappa.reshape(2048, LANES)
    )
    inside = [shape(16, 128, LANES)] * 4
    outs = [shape(16, 112, LANES)] * 5 + inside
    safe = call(safe_kernel, outs, (), 10**8)(kz, rz)
    kl, *safe = lax.optimization_barrier((kl, *safe))
    gots = swap(*sends, "gx")
    outs = [shape(g, width, LANES) for width in (128, 32, 8) for g in (4, 3)]
    bufs = [scratch(30, 8, LANES)] * 2
    *ghosts, send_a, send_b = call(second_kernel, outs + [shape(30, 8, LANES)] * 2, bufs)(
        *gots, kz, rz, km, rm, kl, rl
    )
    gk, gr = ghosts[:2]
    gots = swap(send_a, send_b, "gy")
    outs = [shape(n, 112, LANES)] * 5 + [shape(n, 128, LANES)] * 4
    early = call(early_kernel, outs, [scratch(n, 128, LANES)], 10**8)(
        kz, rz, gk, gr, *safe
    )
    strip = shape(n, 2, 24, LANES)
    outs = [strip] * 5
    for lev in (MID, LOW):
        outs += [shape(lev.rows, lev.span, LANES)] * 5
    outs += [own[0], own[0], own[1], own[2], shape(128, LANES)] + [shape(160, LANES)] * 2
    strip_scratch = [scratch(n, 2, 48, LANES), scratch(n, 2, 24, LANES)]
    bufs = strip_scratch + [scratch(n, 2, 48, LANES)] * 2
    for lev in (MID, LOW):
        wide = scratch(lev.rows, lev.span + 16, LANES)
        bufs += [wide, scratch(lev.rows, lev.span, LANES), wide]
    bufs += [scratch(n, 160, LANES), tmp] + [scratch(160, LANES)] * 2
    results = call(third_kernel, outs, bufs)(
        kz, rz, km, rm, kl, rl, *ghosts, *gots, *safe, *early
    )
    state = results[:15]
    first, defect, dmid, dlow, cedge, send_a, send_b = results[15:]
    gots = swap(send_a, send_b, "gx")
    again = call(safe_again_kernel, inside, (), 10**8)(defect, *safe[:5])
    dlow, *again = lax.optimization_barrier((dlow, *again))
    outs = [shape(3, width, LANES) for width in (128, 32, 8)]
    outs += [shape(128, LANES)] * 2 + [shape(32, LANES)] * 2 + [shape(8, LANES)]
    bufs = [tmp] + [scratch(14, 8, LANES)] * 2
    *halo, send_a, send_b = call(fourth_kernel, outs + [shape(14, 8, LANES)] * 2, bufs)(
        *gots, first, defect, dmid, dlow, cedge
    )
    gf, gm, gl, d0, d15, m0, m3, lows = halo
    gots = swap(send_a, send_b, "gy")
    inner = call(early_again_kernel, [shape(n, 128, LANES)] * 4, (), 10**8)(
        defect, gf, d0, d15, *safe[:5], *early[:5], *again
    )
    bufs = [strip_scratch[1]] + [scratch(n, 2, 48, LANES)] * 2
    for lev in (MID, LOW):
        wide = scratch(lev.rows, lev.span + 16, LANES)
        bufs += [scratch(lev.rows, lev.span, LANES), wide, wide]
    bufs += [tmp, scratch(*rhs.shape), pltpu.SemaphoreType.DMA((8,))]
    return call(fifth_kernel, shape(*rhs.shape), bufs, out=far)(
        *state, first, defect, dmid, *halo, *again, *inner, *gots
    )


def solution(mesh):
    return jax.shard_map(
        on_device,
        mesh=mesh,
        in_specs=(P("groups", "gx", "gy"), P("groups", "gx", "gy")),
        out_specs=P("groups", "gx", "gy"),
        check_vma=False,
    )
```
